32 devices in a mesh: dp: 8 (over y, x, core), mp: 4 (over z).
Axes of the slice: x: 2, y: 2, z: 4, core: 2. Of those that a mesh axis runs over, the one named last changes fastest.
Arguments:
- token_ids: int32 [8, 1024], P('dp'), may hold values from 0 to 50303
- prompt_len: int32 [8], replicated, may hold values from 1 to 512, as said below
- example_len: int32 [8], replicated, may hold values from 512 to 1024, as said below
- embedding: bfloat16 [50304, 1024], P('mp'), may hold values from -6 to 6
- w_qkv: bfloat16 [1024, 3072], P(None, 'mp'), may hold values from -0.1875 to 0.1875
- w_out: bfloat16 [1024, 1024], P('mp'), may hold values from -0.75 to 0.75
- w_in: bfloat16 [1024, 4096], P(None, 'mp'), may hold values from -0.1875 to 0.1875
- b_in: float32 [4096], P('mp'), may hold values from -3 to 3
- w_down: bfloat16 [4096, 1024], P('mp'), may hold values from -0.09375 to 0.09375
- unembed: bfloat16 [1024, 50304], P('dp', 'mp'), may hold values from -0.1875 to 0.1875
- ln_gain: float32 [3, 1024], replicated, may hold values from 0.5 to 1.5
- ln_bias: float32 [3, 1024], replicated, may hold values from -3 to 3
- master: float32 [8, 1024, 128], P(None, ('dp', 'mp')), may hold values from -0.1875 to 0.1875
- first_moment: float32 [8, 1024, 128], P(None, ('dp', 'mp')), may hold values from -1.5258789e-05 to 1.5258789e-05
- second_moment: float32 [8, 1024, 128], P(None, ('dp', 'mp')), may hold values from 4.7683716e-14 to 7.6293946e-13
- eigen_bases: float32 [8, 128, 128], replicated, as said below
Outputs:
- mean_loss: float32 [], replicated
- grad_norm: float32 [], replicated
- new_first: float32 [8, 1024, 128], P(None, ('dp', 'mp'))
- new_second: float32 [8, 1024, 128], P(None, ('dp', 'mp'))
- new_master: float32 [8, 1024, 128], P(None, ('dp', 'mp'))
The draws below stay inside these ranges and needn't reach their ends.
Inputs may be any that keep to these rules, and one draw needn't show every extreme that they name: `prompt_len`: each at most half of its example's length; the first example's is 512. `example_len`: the first example is 1024 tokens long. `eigen_bases`: each matrix is orthogonal.
All inputs are finite; a program needn't handle non-finite values.
Results may differ from the reference program's by a relative error of at most 0.0024.
Values may be sent and summed in bfloat16 or wider, within the bound.
A program may use at most 192 MiB of HBM per device.

```python
import math
import jax
import jax.numpy as jnp
import numpy as np
from jax import lax

D = 1024
HEADS = 16
FF = 4096
V = 50304
R = 128
L = 1024
ADAM_STEP = 10
HD = 64
ROT = 16
EX = 8
N_MP = 4


def lengths_pair(key):
    first_key, second_key = jax.random.split(jax.random.fold_in(key, 11))
    totals = jax.random.randint(first_key, (EX,), L // 2, L + 1).at[0].set(L)
    raw_draw = jax.random.randint(second_key, (EX,), 0, 1 << 20)
    prompts = (1 + raw_draw % (totals // 2)).at[0].set(L // 2)
    return (prompts, totals)


def draw_prompt_len(key, part):
    return lengths_pair(key)[0]


def draw_example_len(key, part):
    return lengths_pair(key)[1]


def draw_eigen_bases(key, part):
    sign_key, order_key = jax.random.split(jax.random.fold_in(key, 5))
    column = jnp.arange(R)
    parity = jnp.zeros((R, R), jnp.int32)
    for place in range(R.bit_length() - 1):
        parity = parity + (column[:, None] >> place & 1) * (column[None, :] >> place & 1)
    hadamard = (1 - 2 * (parity % 2)).astype(jnp.float32) / jnp.sqrt(jnp.float32(R))
    signs = (1 - 2 * jax.random.randint(sign_key, (8, R), 0, 2)).astype(jnp.float32)
    orders = jax.vmap(lambda sub_key: jax.random.permutation(sub_key, R))(jax.random.split(order_key, 8))
    return hadamard[orders] * signs[:, None, :]


def with_ends(result, key, low, high):
    longest = result.shape.index(max(result.shape))
    spots = []
    for shift in (0, 1):
        where = [jax.random.randint(jax.random.fold_in(key, axis), (), 0, length) for axis, length in enumerate(result.shape)]
        where[longest] = (where[longest] + shift) % result.shape[longest]
        spots.append(tuple(where))
    return result.at[spots[0]].set(low).at[spots[1]].set(high)


def block_scale(key, dims, cuts, low, high):
    factor_of, own = 1.0, jax.random.fold_in(key, 6)
    for dim, shards_of in cuts:
        steps = jnp.exp(jax.random.uniform(jax.random.fold_in(own, dim), (shards_of,), jnp.float32, low / len(cuts), high / len(cuts)))
        factor_of = factor_of * jnp.repeat(steps, dims[dim] // shards_of).reshape([-1 if axis == dim else 1 for axis in range(len(dims))])
    return factor_of


def rank_bounds(count, skew):
    weights = [(1 << 20) // math.isqrt(grade ** skew) + 1 for grade in range(1, count + 1)]
    scale = 1 + sum(weights) // (1 << 30)
    return np.cumsum(np.array([max(1, weight // scale) for weight in weights]))


def skewed_ids(own_key, shape, amount, skew):
    grid = rank_bounds(amount, skew)
    pick = jax.random.randint(jax.random.fold_in(own_key, 1), shape, 0, int(grid[amount - 1]))
    standing = jnp.searchsorted(jnp.asarray(grid, jnp.int32), pick, side="right")
    return jax.random.permutation(jax.random.fold_in(own_key, 2), amount)[standing].astype(jnp.int32)


def noise(key, extent, scale, bound, cuts=(), held_as=jnp.bfloat16):
    factor_of = block_scale(key, extent, cuts, -0.22, 0.18) if cuts else 1.0
    values = jax.random.normal(key, extent, jnp.float32) * scale * factor_of
    return jnp.minimum(jnp.maximum(values, -bound), bound).astype(held_as)


def setup_inputs(seed: int = 0) -> dict:
    key_list = jax.random.split(jax.random.key(seed), 17)
    return {
        "token_ids": with_ends(skewed_ids(key_list[0], (EX, L), V, 2), jax.random.fold_in(key_list[0], 3), 0, V - 1).astype(jnp.int32),
        "prompt_len": draw_prompt_len(jax.random.fold_in(key_list[16], 71), 0),
        "example_len": draw_example_len(jax.random.fold_in(key_list[16], 71), 0),
        "embedding": noise(key_list[3], (V, D), 1.0, 6.0, ((0, 4),)),
        "w_qkv": noise(key_list[4], (D, 3 * D), D ** -0.5, 0.1875, ((1, 4),)),
        "w_out": noise(key_list[5], (D, D), (D // 16) ** -0.5, 0.75, ((0, 4),)),
        "w_in": noise(key_list[6], (D, FF), D ** -0.5, 0.1875, ((1, 4),)),
        "b_in": noise(key_list[7], (FF,), 0.5, 3.0, ((0, 4),), jnp.float32),
        "w_down": noise(key_list[8], (FF, D), FF ** -0.5, 0.09375, ((0, 4),)),
        "unembed": noise(key_list[9], (D, V), D ** -0.5, 0.1875, ((0, 8), (1, 4))),
        "ln_gain": jnp.clip(1.0 + 0.1 * jax.random.normal(key_list[10], (3, D), jnp.float32), 0.5, 1.5),
        "ln_bias": noise(key_list[11], (3, D), 0.5, 3.0, (), jnp.float32),
        "master": noise(key_list[12], (8, D, R), D ** -0.5, 0.1875, ((1, 32),), jnp.float32),
        "first_moment": noise(key_list[13], (8, D, R), (0.0011 / (8 * D * R) ** 0.5), 1.52587890625e-05, ((1, 32),), jnp.float32),
        "second_moment": jnp.clip(jnp.exp(math.log(7.629394620407848e-13) - 2.7725887 * jax.random.uniform(key_list[14], (8, D, R), jnp.float32) ** block_scale(key_list[14], (8, D, R), ((1, 32),), -0.2, 0.2)), 4.768371637754905e-14, 7.629394620407848e-13),
        "eigen_bases": draw_eigen_bases(jax.random.fold_in(key_list[16], 71), 0),
    }


HIGH_PRECISION = lax.Precision.HIGHEST
NORM_EPS = 1e-05
ROPE_BASE = 10000.0
CLIP_LIMIT = 0.01
LEARN_RATE = 0.02
BETA_FIRST = 0.9
BETA_SECOND = 0.999
ADAM_EPS = 1e-08
DECAY_RATE = 0.01

@jax.custom_vjp
def low(v):
    return lax.optimization_barrier(v.astype(jnp.bfloat16)).astype(jnp.float32)

@jax.custom_vjp
def low_back(v):
    return v

def low_keep(v):
    return (low(v), None)

def low_pass(kept, grad):
    return (grad,)

def back_keep(v):
    return (v, None)

def backward_lowrank(kept, grad):
    return (low(grad),)
low.defvjp(low_keep, low_pass)
low_back.defvjp(back_keep, backward_lowrank)

def lowered(value):
    return low_back(low(value))

def layer_norm(values, gain, shift):
    centre = values - lax.optimization_barrier(jnp.mean(values, -1, keepdims=True))
    spread = lax.optimization_barrier(jnp.mean(centre * centre, -1, keepdims=True))
    return centre * lax.rsqrt(spread + NORM_EPS) * gain + shift

def rope_tables(length):
    half = ROT // 2
    freqs = ROPE_BASE ** (-2.0 * jnp.arange(half, dtype=jnp.float32) / ROT)
    angles = jnp.arange(length, dtype=jnp.float32)[:, None] * freqs[None, :]
    return (jnp.cos(angles)[:, None, :], jnp.sin(angles)[:, None, :])

def rotate(field, cosine, sine):
    half = ROT // 2
    first = field[..., :half]
    second = field[..., half:ROT]
    return jnp.concatenate([first * cosine - second * sine, second * cosine + first * sine, field[..., ROT:]], -1)

def matmul(left, right):
    return jnp.dot(left, right, precision=HIGH_PRECISION)

def example_loss(adapter_set, frozen, token_row, prompt, total_len, count):
    embedding, w_qkv, w_out, w_in, b_in, w_down, unembed, ln_gain, ln_bias = frozen
    start_rows = embedding[token_row]
    normed_attn = low(layer_norm(start_rows, ln_gain[0], ln_bias[0]))
    normed_ffn = low(layer_norm(start_rows, ln_gain[1], ln_bias[1]))
    inner = low(matmul(normed_attn, jnp.concatenate([adapter_set[0], adapter_set[1], adapter_set[2]], 1)))
    base = matmul(normed_attn, w_qkv).reshape(L, HEADS, 3, HD)

    def adapted(selector_index):
        extra = matmul(inner[:, selector_index * R:(selector_index + 1) * R], adapter_set[3 + selector_index].T)
        return base[:, :, selector_index] + extra.reshape(L, HEADS, HD)
    cosine, sine = rope_tables(L)
    queries = low(rotate(low_back(adapted(0)), cosine, sine))
    key_rows = low(rotate(low_back(adapted(1)), cosine, sine))
    value_rows = lowered(adapted(2))
    scores = low_back(jnp.einsum('qhd,khd->hqk', queries, key_rows, precision=HIGH_PRECISION) * HD ** (-0.5))
    causal = jnp.arange(L)[None, :] <= jnp.arange(L)[:, None]
    scores = jnp.where(causal[None], scores, -1e+30)
    probs = low(jax.nn.softmax(scores, -1))
    context = lowered(jnp.einsum('hqk,khd->qhd', probs, value_rows, precision=HIGH_PRECISION)).reshape(L, D)
    group_width = D // N_MP
    parts = jnp.einsum('ljd,jdr->jlr', context.reshape(L, N_MP, group_width), adapter_set[6].reshape(N_MP, group_width, R), precision=HIGH_PRECISION)
    inner_out = low_back(lax.optimization_barrier(jnp.sum(low(parts), 0)))
    attention = matmul(context, w_out) + matmul(inner_out, adapter_set[7].T)
    hidden = low(jax.nn.gelu(matmul(normed_ffn, w_in) + b_in, approximate=False))
    resid = start_rows + low_back(attention + matmul(hidden, w_down))
    final_rows = low(layer_norm(resid, ln_gain[2], ln_bias[2]))
    target = jnp.roll(token_row, -1)
    position = jnp.arange(L)
    keep = ((position >= prompt - 1) & (position < total_len - 1)).astype(jnp.float32)
    row_block = min(256, L)
    blocks = L // row_block

    def block_nll(pieces):
        rows_here, target_here, keep_here = pieces
        logits = low_back(matmul(rows_here, unembed))
        spread = jax.nn.logsumexp(logits, -1)
        picked = jnp.take_along_axis(logits, target_here[:, None], 1)[:, 0]
        return jnp.sum((spread - picked) * keep_here)
    losses = lax.map(jax.checkpoint(block_nll), (final_rows.reshape(blocks, row_block, D), target.reshape(blocks, row_block), keep.reshape(blocks, row_block)))
    return jnp.sum(losses) / count

def reference(token_ids, prompt_len, example_len, embedding, w_qkv, w_out, w_in, b_in, w_down, unembed, ln_gain, ln_bias, master, first_moment, second_moment, eigen_bases):
    frozen = (embedding.astype(jnp.float32), w_qkv.astype(jnp.float32), w_out.astype(jnp.float32), w_in.astype(jnp.float32), b_in, w_down.astype(jnp.float32), unembed.astype(jnp.float32), ln_gain, ln_bias)
    count = jnp.sum(example_len - prompt_len).astype(jnp.float32)

    def total_loss(weights):
        adapter_set = low(weights)

        def one_example(carry, pieces):
            token_row, prompt, total_len = pieces
            value = jax.checkpoint(example_loss)(adapter_set, frozen, token_row, prompt, total_len, count)
            return (carry + value, None)
        summed, _ = lax.scan(one_example, jnp.zeros((), jnp.float32), (token_ids, prompt_len, example_len))
        return summed
    mean_loss, pullback = jax.vjp(total_loss, master)
    gradient = pullback(jnp.ones((), jnp.float32))[0]
    grad_norm = jnp.sqrt(jnp.sum(gradient * gradient))
    clipped = gradient * jnp.minimum(1.0, CLIP_LIMIT / grad_norm)
    rotated = jnp.einsum('mdr,mrs->mds', clipped, eigen_bases, precision=HIGH_PRECISION)
    new_first = BETA_FIRST * first_moment + (1.0 - BETA_FIRST) * rotated
    new_second = BETA_SECOND * second_moment + (1.0 - BETA_SECOND) * rotated * rotated
    normed = new_first / (1.0 - BETA_FIRST ** ADAM_STEP) / (jnp.sqrt(new_second / (1.0 - BETA_SECOND ** ADAM_STEP)) + ADAM_EPS)
    turned = jnp.einsum('mds,mrs->mdr', normed, eigen_bases, precision=HIGH_PRECISION)
    new_master = master - LEARN_RATE * (turned + DECAY_RATE * master)
    return (mean_loss, grad_norm, new_first, new_second, new_master)
```

```python
import functools

import jax
import jax.numpy as jnp
from jax import lax
from jax.experimental import pallas as pl
from jax.experimental.pallas import tpu as pltpu
from jax.sharding import PartitionSpec as P

MESH = pl.DeviceIdType.MESH
VMEM_LIMIT = 60 * 1024 * 1024

D = 1024
HEADS = 16
R = 128
ADAM_STEP = 10
HD = 64
ROT = 16


HIGH_PRECISION = lax.Precision.HIGHEST
NORM_EPS = 1e-05
ROPE_BASE = 10000.0
CLIP_LIMIT = 0.01
LEARN_RATE = 0.02
BETA_FIRST = 0.9
BETA_SECOND = 0.999
ADAM_EPS = 1e-08
DECAY_RATE = 0.01


def merged(value, axis, join):
    pieces = jax.tree.map(lambda part: lax.all_gather(part, axis), value)
    head = jax.tree.map(lambda part: part[0], pieces)
    tail = jax.tree.map(lambda part: part[1:], pieces)
    running, _ = lax.scan(lambda running, section: (join(running, section), None), head, tail)
    return running


def layer_norm(values, gain, shift):
    centre = values - jnp.mean(values, -1, keepdims=True)
    spread = jnp.mean(centre * centre, -1, keepdims=True)
    return centre * lax.rsqrt(spread + NORM_EPS) * gain + shift


def rope_tables(length):
    half = ROT // 2
    freqs = ROPE_BASE ** (-2.0 * jnp.arange(half, dtype=jnp.float32) / ROT)
    angles = jnp.arange(length, dtype=jnp.float32)[:, None] * freqs[None, :]
    return (jnp.cos(angles)[:, None, :], jnp.sin(angles)[:, None, :])


def rotate(field, cosine, sine):
    half = ROT // 2
    first = field[..., :half]
    second = field[..., half:ROT]
    return jnp.concatenate(
        [first * cosine - second * sine, second * cosine + first * sine, field[..., ROT:]], -1
    )


def rotate_back(upstream, cosine, sine):
    half = ROT // 2
    first = upstream[..., :half]
    second = upstream[..., half:ROT]
    return jnp.concatenate(
        [first * cosine + second * sine, second * cosine - first * sine, upstream[..., ROT:]], -1
    )


def masked_scores(queries, key_rows, start_row, stop_row):
    scores = jnp.einsum(
        "qhd,khd->hqk",
        queries[start_row:stop_row],
        key_rows[:stop_row],
        preferred_element_type=jnp.float32,
    ) * HD ** (-0.5)
    query_pos = start_row + jnp.arange(stop_row - start_row)[:, None]
    causal = jnp.arange(stop_row)[None, :] <= query_pos
    return jnp.where(causal[None], scores, -1e30)


def attend(queries, key_rows, value_rows):
    length = queries.shape[0]
    row_block = min(512, length)
    outputs = []
    spreads = []
    for start_row in range(0, length, row_block):
        stop_row = start_row + row_block
        scores = masked_scores(queries, key_rows, start_row, stop_row)
        top_score = jnp.max(scores, -1, keepdims=True)
        weights = jnp.exp(scores - top_score)
        row_total = jnp.sum(weights, -1, keepdims=True)
        probs = (weights / row_total).astype(jnp.bfloat16)
        outputs.append(
            jnp.einsum(
                "hqk,khd->qhd", probs, value_rows[:stop_row], preferred_element_type=jnp.float32
            )
        )
        spreads.append((top_score + jnp.log(row_total))[..., 0])
    return (jnp.concatenate(outputs, 0).astype(jnp.bfloat16), jnp.concatenate(spreads, 1))


def attend_back(queries, key_rows, value_rows, spreads, upstream):
    length = queries.shape[0]
    row_block = min(512, length)
    scaling = HD ** (-0.5)
    query_grads = []
    key_grad = jnp.zeros(key_rows.shape, jnp.float32)
    value_grad = jnp.zeros(value_rows.shape, jnp.float32)
    for start_row in range(0, length, row_block):
        stop_row = start_row + row_block
        scores = masked_scores(queries, key_rows, start_row, stop_row)
        probs = jnp.exp(scores - spreads[:, start_row:stop_row, None])
        grad_here = upstream[start_row:stop_row]
        prob_grad = jnp.einsum(
            "qhd,khd->hqk", grad_here, value_rows[:stop_row], preferred_element_type=jnp.float32
        )
        inner_sum = jnp.sum(probs * prob_grad, -1, keepdims=True)
        score_grad = (probs * (prob_grad - inner_sum)).astype(jnp.bfloat16)
        query_grads.append(
            jnp.einsum(
                "hqk,khd->qhd", score_grad, key_rows[:stop_row], preferred_element_type=jnp.float32
            )
            * scaling
        )
        key_grad = key_grad.at[:stop_row].add(
            jnp.einsum(
                "hqk,qhd->khd",
                score_grad,
                queries[start_row:stop_row],
                preferred_element_type=jnp.float32,
            )
            * scaling
        )
        value_grad = value_grad.at[:stop_row].add(
            jnp.einsum(
                "hqk,qhd->khd",
                probs.astype(jnp.bfloat16),
                grad_here,
                preferred_element_type=jnp.float32,
            )
        )
    return (jnp.concatenate(query_grads, 0), key_grad, value_grad)


def merge_stats(first, second):
    top_score = jnp.maximum(first[0], second[0])
    row_total = first[1] * jnp.exp(first[0] - top_score) + second[1] * jnp.exp(
        second[0] - top_score
    )
    return (top_score, row_total, first[2] + second[2])


def line_chunk(index, size):
    return pl.ds(pl.multiple_of(index * size, size), size)


def greet_line(me, count):
    barrier = pltpu.get_barrier_semaphore()

    @pl.when(me > 0)
    def _():
        pl.semaphore_signal(
            barrier, inc=1, device_id={"mp": jnp.maximum(me - 1, 0)}, device_id_type=MESH
        )

    @pl.when(me < count - 1)
    def _():
        pl.semaphore_signal(
            barrier, inc=1, device_id={"mp": jnp.minimum(me + 1, count - 1)}, device_id_type=MESH
        )

    peers = jnp.where(me > 0, 1, 0) + jnp.where(me < count - 1, 1, 0)
    pl.semaphore_wait(barrier, peers)


def line_sum(count, chunk, own, wires, sems, prepare, emit):
    me = lax.axis_index("mp")
    from_low, from_high, to_high, to_low = wires
    up_send, up_recv, down_send, down_recv = sems
    length = own.shape[0]
    chunks = length // chunk
    above = jnp.minimum(me + 1, count - 1)
    below = jnp.maximum(me - 1, 0)

    def up_copy(index):
        rows = line_chunk(index, chunk)
        return pltpu.make_async_remote_copy(
            src_ref=to_high.at[rows],
            dst_ref=from_low.at[rows],
            send_sem=up_send.at[index],
            recv_sem=up_recv.at[index],
            device_id={"mp": above},
            device_id_type=MESH,
        )

    def down_copy(index):
        rows = line_chunk(index, chunk)
        return pltpu.make_async_remote_copy(
            src_ref=to_low.at[rows],
            dst_ref=from_high.at[rows],
            send_sem=down_send.at[index],
            recv_sem=down_recv.at[index],
            device_id={"mp": below},
            device_id_type=MESH,
        )

    greet_line(me, count)

    @pl.when(me == 0)
    def _():
        from_low[...] = jnp.zeros_like(from_low)

    @pl.when(me == count - 1)
    def _():
        from_high[...] = jnp.zeros_like(from_high)

    def step(at, carry):
        if prepare is not None:

            @pl.when(at < chunks)
            def _():
                prepare(at)

        up = at - LINE_LAG * me

        @pl.when((up >= 0) & (up < chunks))
        def _():
            rows = line_chunk(up, chunk)

            @pl.when(me > 0)
            def _():
                up_copy(up).wait_recv()

            @pl.when(me < count - 1)
            def _():
                to_high[rows, :] = (
                    from_low[rows, :].astype(jnp.float32) + own[rows, :].astype(jnp.float32)
                ).astype(jnp.bfloat16)
                up_copy(up).start()

        down = at - LINE_LAG * (count - 1 - me)

        @pl.when((down >= 0) & (down < chunks))
        def _():
            rows = line_chunk(down, chunk)

            @pl.when(me < count - 1)
            def _():
                down_copy(down).wait_recv()

            @pl.when(me > 0)
            def _():
                to_low[rows, :] = (
                    from_high[rows, :].astype(jnp.float32) + own[rows, :].astype(jnp.float32)
                ).astype(jnp.bfloat16)
                down_copy(down).start()

        ready = at - LINE_LAG * jnp.maximum(me, count - 1 - me)

        @pl.when((ready >= 0) & (ready < chunks))
        def _():
            rows = line_chunk(ready, chunk)
            total = (
                from_low[rows, :].astype(jnp.float32)
                + own[rows, :].astype(jnp.float32)
                + from_high[rows, :].astype(jnp.float32)
            )
            emit(rows, total)

        return carry

    lax.fori_loop(0, chunks + LINE_LAG * (count - 1), step, 0)

    def drain(index, carry):
        @pl.when(me < count - 1)
        def _():
            up_copy(index).wait_send()

        @pl.when(me > 0)
        def _():
            down_copy(index).wait_send()

        return carry

    lax.fori_loop(0, chunks, drain, 0)


LINE_CHUNK = 32
LINE_LAG = 3


def line_scratch(length, width):
    chunks = length // LINE_CHUNK
    return [pltpu.VMEM((length, width), jnp.bfloat16)] * 4 + [
        pltpu.SemaphoreType.DMA((chunks,))
    ] * 4


def line_call(kernel, name, collective_id, outs, scratch, operands, flops=0):
    size = sum(o.size * o.dtype.itemsize for o in operands) + sum(
        o.size * o.dtype.itemsize for o in outs
    )
    vmem = pl.BlockSpec(memory_space=pltpu.VMEM)
    return pl.pallas_call(
        kernel,
        name=name,
        out_shape=outs,
        in_specs=[vmem] * len(operands),
        out_specs=[vmem] * len(outs),
        scratch_shapes=scratch,
        compiler_params=pltpu.CompilerParams(
            collective_id=collective_id, has_side_effects=True, vmem_limit_bytes=VMEM_LIMIT
        ),
        cost_estimate=pl.CostEstimate(
            flops=flops, bytes_accessed=size + 100_000_000, transcendentals=0
        ),
    )(*operands)


def start_kernel(count, part, gain, shift, rows_out, attn_out, ffn_out, *scratch):
    def emit(rows, total):
        rows_out[rows, :] = total.astype(jnp.bfloat16)
        centre = total - jnp.mean(total, -1, keepdims=True)
        spread = jnp.mean(centre * centre, -1, keepdims=True)
        base = centre * lax.rsqrt(spread + NORM_EPS)
        attn_out[rows, :] = (base * gain[0:1, :] + shift[0:1, :]).astype(jnp.bfloat16)
        ffn_out[rows, :] = (base * gain[1:2, :] + shift[1:2, :]).astype(jnp.bfloat16)

    line_sum(count, LINE_CHUNK, part, scratch[:4], scratch[4:], None, emit)


def resid_kernel(count, part, start, gain, shift, resid_out, final_out, *scratch):
    def emit(rows, total):
        resid = start[rows, :].astype(jnp.float32) + total
        resid_out[rows, :] = resid
        normed = layer_norm(resid, gain[2:3, :], shift[2:3, :])
        final_out[rows, :] = normed.astype(jnp.bfloat16)

    line_sum(count, LINE_CHUNK, part, scratch[:4], scratch[4:], None, emit)


def branch_kernel(count, part, resid, gain, out, *scratch):
    def emit(rows, total):
        values = resid[rows, :]
        centre = values - jnp.mean(values, -1, keepdims=True)
        spread = jnp.mean(centre * centre, -1, keepdims=True)
        inverse = lax.rsqrt(spread + NORM_EPS)
        normed = centre * inverse
        up = total * gain[2:3, :]
        out[rows, :] = (
            inverse
            * (
                up
                - jnp.mean(up, -1, keepdims=True)
                - normed * jnp.mean(up * normed, -1, keepdims=True)
            )
        ).astype(jnp.bfloat16)

    line_sum(count, LINE_CHUNK, part, scratch[:4], scratch[4:], None, emit)


def per_device(
    token_ids,
    prompt_len,
    example_len,
    embedding,
    w_qkv,
    w_out,
    w_in,
    b_in,
    w_down,
    unembed,
    ln_gain,
    ln_bias,
    master,
    first_moment,
    second_moment,
    eigen_bases,
):
    group_count = lax.axis_size("mp")
    group_index = lax.axis_index("mp")
    adapters = lax.all_gather(master.astype(jnp.bfloat16), ("dp", "mp"), axis=1, tiled=True)
    head_local = lax.all_gather(unembed, "dp", axis=0, tiled=True)
    examples, length = token_ids.shape
    width = embedding.shape[0]
    vocab_local = head_local.shape[1]
    rows = examples * length
    local_heads = HEADS // group_count
    group_width = local_heads * HD
    flat_ids = token_ids.reshape(rows)
    relative = flat_ids - group_index * width
    inside = (relative >= 0) & (relative < width)
    picked = jnp.where(
        inside[:, None], embedding[jnp.clip(relative, 0, width - 1)].astype(jnp.float32), 0.0
    )
    shape_low = jax.ShapeDtypeStruct((rows, D), jnp.bfloat16)
    shape_wide = jax.ShapeDtypeStruct((rows, D), jnp.float32)
    start_rows, normed_attn, normed_ffn = line_call(
        functools.partial(start_kernel, group_count),
        "start_rows",
        0,
        [shape_low] * 3,
        line_scratch(rows, D),
        [picked.astype(jnp.bfloat16), ln_gain, ln_bias],
    )
    leading_example = lax.axis_index("dp") * examples
    prompts = lax.dynamic_slice_in_dim(prompt_len, leading_example, examples)
    totals = lax.dynamic_slice_in_dim(example_len, leading_example, examples)
    position = jnp.arange(length)
    keep = (position[None, :] >= prompts[:, None] - 1) & (position[None, :] < totals[:, None] - 1)
    count = jnp.sum(example_len - prompt_len).astype(jnp.float32)
    row_weight = keep.reshape(rows).astype(jnp.float32) / count
    target = jnp.roll(token_ids, -1, axis=1).reshape(rows)
    inner = jnp.dot(
        normed_attn,
        jnp.concatenate([adapters[0], adapters[1], adapters[2]], 1),
        preferred_element_type=jnp.float32,
    ).astype(jnp.bfloat16)
    base = jnp.dot(normed_attn, w_qkv, preferred_element_type=jnp.float32).reshape(
        rows, local_heads, 3, HD
    )
    adapter_rows = [
        lax.dynamic_slice_in_dim(
            adapters[3 + selector_index], group_index * group_width, group_width, 0
        )
        for selector_index in range(3)
    ]
    pre_parts = []
    for selector_index in range(3):
        extra = jnp.einsum(
            "lr,dr->ld",
            inner[:, selector_index * R : (selector_index + 1) * R],
            adapter_rows[selector_index],
            preferred_element_type=jnp.float32,
        )
        pre_parts.append(base[:, :, selector_index] + extra.reshape(rows, local_heads, HD))
    cosine, sine = rope_tables(length)
    queries = rotate(pre_parts[0].reshape(examples, length, local_heads, HD), cosine, sine).astype(
        jnp.bfloat16
    )
    key_rows = rotate(pre_parts[1].reshape(examples, length, local_heads, HD), cosine, sine).astype(
        jnp.bfloat16
    )
    value_rows = pre_parts[2].reshape(examples, length, local_heads, HD).astype(jnp.bfloat16)
    sample = 0
    context_here, spread_local = attend(queries[sample], key_rows[sample], value_rows[sample])
    spreads = [spread_local]
    context = context_here.reshape(rows, group_width)
    out_rows = lax.dynamic_slice_in_dim(adapters[6], group_index * group_width, group_width, 0)
    inner_out = jnp.dot(context, out_rows, preferred_element_type=jnp.float32).astype(jnp.bfloat16)
    hidden = jax.nn.gelu(
        jnp.dot(normed_ffn, w_in, preferred_element_type=jnp.float32) + b_in, approximate=False
    ).astype(jnp.bfloat16)
    partial_value = (
        jnp.dot(context, w_out, preferred_element_type=jnp.float32)
        + jnp.einsum("lr,dr->ld", inner_out, adapters[7], preferred_element_type=jnp.float32)
        + jnp.dot(hidden, w_down, preferred_element_type=jnp.float32)
    )
    resid, final_rows = line_call(
        functools.partial(resid_kernel, group_count),
        "resid_rows",
        1,
        [shape_wide, shape_low],
        line_scratch(rows, D),
        [partial_value.astype(jnp.bfloat16), start_rows, ln_gain, ln_bias],
    )
    row_block = min(256, rows)
    blocks = rows // row_block
    vocab_ids = jnp.arange(vocab_local)[None, :]

    def block_stats(pieces):
        rows_here, target_here = pieces
        logits = jnp.dot(rows_here, head_local, preferred_element_type=jnp.float32)
        top_score = jnp.max(logits, -1)
        row_total = jnp.sum(jnp.exp(logits - top_score[:, None]), -1)
        hit = vocab_ids == (target_here - group_index * vocab_local)[:, None]
        return (top_score, row_total, jnp.sum(jnp.where(hit, logits, 0.0), -1))

    stats = lax.map(
        block_stats, (final_rows.reshape(blocks, row_block, D), target.reshape(blocks, row_block))
    )
    top_score, row_total, target_logit = merged(
        (stats[0].reshape(rows), stats[1].reshape(rows), stats[2].reshape(rows)), "mp", merge_stats
    )
    spread_all = top_score + jnp.log(row_total)
    local_loss = jnp.sum((spread_all - target_logit) * row_weight)

    def block_back(pieces):
        rows_here, target_here, spread_local, weight_here = pieces
        logits = jnp.dot(rows_here, head_local, preferred_element_type=jnp.float32)
        hit = (vocab_ids == (target_here - group_index * vocab_local)[:, None]).astype(jnp.float32)
        logit_grad = (
            (jnp.exp(logits - spread_local[:, None]) - hit) * weight_here[:, None]
        ).astype(jnp.bfloat16)
        return jnp.einsum("lv,dv->ld", logit_grad, head_local, preferred_element_type=jnp.float32)

    head_grad = lax.map(
        block_back,
        (
            final_rows.reshape(blocks, row_block, D),
            target.reshape(blocks, row_block),
            spread_all.reshape(blocks, row_block),
            row_weight.reshape(blocks, row_block),
        ),
    ).reshape(rows, D)
    (branch_grad,) = line_call(
        functools.partial(branch_kernel, group_count),
        "branch_rows",
        2,
        [shape_low],
        line_scratch(rows, D),
        [head_grad.astype(jnp.bfloat16), resid, ln_gain],
    )
    inner_out_grad = jnp.dot(branch_grad, adapters[7], preferred_element_type=jnp.float32).astype(
        jnp.bfloat16
    )
    grad_out_b = jnp.einsum("ld,lr->dr", branch_grad, inner_out, preferred_element_type=jnp.float32)
    grad_out_a = jnp.einsum(
        "ld,lr->dr", context, inner_out_grad, preferred_element_type=jnp.float32
    )
    context_grad = jnp.einsum(
        "ld,ed->le", branch_grad, w_out, preferred_element_type=jnp.float32
    ) + jnp.einsum("lr,dr->ld", inner_out_grad, out_rows, preferred_element_type=jnp.float32)
    context_grad = context_grad.astype(jnp.bfloat16).reshape(examples, length, local_heads, HD)
    sample = 0
    query_grad, key_grad, value_grad = attend_back(
        queries[sample], key_rows[sample], value_rows[sample], spreads[sample], context_grad[sample]
    )
    query_parts = [rotate_back(query_grad, cosine, sine)]
    key_parts = [rotate_back(key_grad, cosine, sine)]
    value_parts = [value_grad]
    pre_grads = [
        parts[0].reshape(rows, group_width).astype(jnp.bfloat16)
        for parts in (query_parts, key_parts, value_parts)
    ]
    complete_gradients = []
    local_grads = []
    for selector_index in range(3):
        projected_values = jnp.einsum(
            "ld,le->de", normed_attn, pre_grads[selector_index], preferred_element_type=jnp.float32
        )
        complete_gradients.append(
            jnp.dot(
                projected_values,
                adapter_rows[selector_index].astype(jnp.float32),
                precision=HIGH_PRECISION,
            )
        )
        local_grads.append(
            jnp.einsum(
                "ld,lr->dr",
                pre_grads[selector_index],
                inner[:, selector_index * R : (selector_index + 1) * R],
                preferred_element_type=jnp.float32,
            )
        )
    local_grads.append(grad_out_a)
    placed = lax.dynamic_update_slice(
        jnp.zeros((4, D, R), jnp.float32), jnp.stack(local_grads), (0, group_index * group_width, 0)
    )
    gradient = jnp.concatenate([jnp.stack(complete_gradients), placed, grad_out_b[None]], 0)
    owned = lax.psum_scatter(gradient, ("dp", "mp"), scatter_dimension=1, tiled=True)
    squares = jnp.sum(owned * owned)
    norm_squared = lax.psum(squares, ("dp", "mp"))
    mean_loss = lax.psum(local_loss, "dp")
    grad_norm = jnp.sqrt(norm_squared)
    clipped = owned * jnp.minimum(1.0, CLIP_LIMIT / grad_norm)
    rotated = jnp.einsum("mdr,mrs->mds", clipped, eigen_bases, precision=HIGH_PRECISION)
    new_first = BETA_FIRST * first_moment + (1.0 - BETA_FIRST) * rotated
    new_second = BETA_SECOND * second_moment + (1.0 - BETA_SECOND) * rotated * rotated
    normed = (
        new_first
        / (1.0 - BETA_FIRST**ADAM_STEP)
        / (jnp.sqrt(new_second / (1.0 - BETA_SECOND**ADAM_STEP)) + ADAM_EPS)
    )
    turned = jnp.einsum("mds,mrs->mdr", normed, eigen_bases, precision=HIGH_PRECISION)
    new_master = master - LEARN_RATE * (turned + DECAY_RATE * master)
    return (mean_loss, grad_norm, new_first, new_second, new_master)


def solution(mesh):
    placed = (
        P("dp", None),
        P(),
        P(),
        P("mp", None),
        P(None, "mp"),
        P("mp", None),
        P(None, "mp"),
        P("mp"),
        P("mp", None),
        P("dp", "mp"),
        P(),
        P(),
        P(None, ("dp", "mp"), None),
        P(None, ("dp", "mp"), None),
        P(None, ("dp", "mp"), None),
        P(),
    )
    return jax.shard_map(
        per_device,
        mesh=mesh,
        in_specs=placed,
        out_specs=(
            P(),
            P(),
            P(None, ("dp", "mp"), None),
            P(None, ("dp", "mp"), None),
            P(None, ("dp", "mp"), None),
        ),
        check_vma=False,
    )
```

```python
import functools

import jax
import jax.numpy as jnp
from jax import lax
from jax.experimental import pallas as pl
from jax.experimental.pallas import tpu as pltpu
from jax.sharding import PartitionSpec as P

MESH = pl.DeviceIdType.MESH
VMEM_LIMIT = 60 * 1024 * 1024

D = 1024
HEADS = 16
R = 128
ADAM_STEP = 10
HD = 64
ROT = 16


HIGH_PRECISION = lax.Precision.HIGHEST
NORM_EPS = 1e-05
ROPE_BASE = 10000.0
CLIP_LIMIT = 0.01
LEARN_RATE = 0.02
BETA_FIRST = 0.9
BETA_SECOND = 0.999
ADAM_EPS = 1e-08
DECAY_RATE = 0.01


def merged(value, axis, join):
    pieces = jax.tree.map(lambda part: lax.all_gather(part, axis), value)
    head = jax.tree.map(lambda part: part[0], pieces)
    tail = jax.tree.map(lambda part: part[1:], pieces)
    running, _ = lax.scan(lambda running, section: (join(running, section), None), head, tail)
    return running


def layer_norm(values, gain, shift):
    centre = values - jnp.mean(values, -1, keepdims=True)
    spread = jnp.mean(centre * centre, -1, keepdims=True)
    return centre * lax.rsqrt(spread + NORM_EPS) * gain + shift


def rope_tables(length):
    half = ROT // 2
    freqs = ROPE_BASE ** (-2.0 * jnp.arange(half, dtype=jnp.float32) / ROT)
    angles = jnp.arange(length, dtype=jnp.float32)[:, None] * freqs[None, :]
    return (jnp.cos(angles)[:, None, :], jnp.sin(angles)[:, None, :])


def rotate(field, cosine, sine):
    half = ROT // 2
    first = field[..., :half]
    second = field[..., half:ROT]
    return jnp.concatenate(
        [first * cosine - second * sine, second * cosine + first * sine, field[..., ROT:]], -1
    )


def rotate_back(upstream, cosine, sine):
    half = ROT // 2
    first = upstream[..., :half]
    second = upstream[..., half:ROT]
    return jnp.concatenate(
        [first * cosine + second * sine, second * cosine - first * sine, upstream[..., ROT:]], -1
    )


def masked_scores(queries, key_rows, start_row, stop_row):
    scores = jnp.einsum(
        "qhd,khd->hqk",
        queries[start_row:stop_row],
        key_rows[:stop_row],
        preferred_element_type=jnp.float32,
    ) * HD ** (-0.5)
    query_pos = start_row + jnp.arange(stop_row - start_row)[:, None]
    causal = jnp.arange(stop_row)[None, :] <= query_pos
    return jnp.where(causal[None], scores, -1e30)


def attend(queries, key_rows, value_rows):
    length = queries.shape[0]
    row_block = min(512, length)
    outputs = []
    spreads = []
    for start_row in range(0, length, row_block):
        stop_row = start_row + row_block
        scores = masked_scores(queries, key_rows, start_row, stop_row)
        top_score = jnp.max(scores, -1, keepdims=True)
        weights = jnp.exp(scores - top_score)
        row_total = jnp.sum(weights, -1, keepdims=True)
        probs = (weights / row_total).astype(jnp.bfloat16)
        outputs.append(
            jnp.einsum(
                "hqk,khd->qhd", probs, value_rows[:stop_row], preferred_element_type=jnp.float32
            )
        )
        spreads.append((top_score + jnp.log(row_total))[..., 0])
    return (jnp.concatenate(outputs, 0).astype(jnp.bfloat16), jnp.concatenate(spreads, 1))


def attend_back(queries, key_rows, value_rows, spreads, upstream):
    length = queries.shape[0]
    row_block = min(512, length)
    scaling = HD ** (-0.5)
    query_grads = []
    key_grad = jnp.zeros(key_rows.shape, jnp.float32)
    value_grad = jnp.zeros(value_rows.shape, jnp.float32)
    for start_row in range(0, length, row_block):
        stop_row = start_row + row_block
        scores = masked_scores(queries, key_rows, start_row, stop_row)
        probs = jnp.exp(scores - spreads[:, start_row:stop_row, None])
        grad_here = upstream[start_row:stop_row]
        prob_grad = jnp.einsum(
            "qhd,khd->hqk", grad_here, value_rows[:stop_row], preferred_element_type=jnp.float32
        )
        inner_sum = jnp.sum(probs * prob_grad, -1, keepdims=True)
        score_grad = (probs * (prob_grad - inner_sum)).astype(jnp.bfloat16)
        query_grads.append(
            jnp.einsum(
                "hqk,khd->qhd", score_grad, key_rows[:stop_row], preferred_element_type=jnp.float32
            )
            * scaling
        )
        key_grad = key_grad.at[:stop_row].add(
            jnp.einsum(
                "hqk,qhd->khd",
                score_grad,
                queries[start_row:stop_row],
                preferred_element_type=jnp.float32,
            )
            * scaling
        )
        value_grad = value_grad.at[:stop_row].add(
            jnp.einsum(
                "hqk,qhd->khd",
                probs.astype(jnp.bfloat16),
                grad_here,
                preferred_element_type=jnp.float32,
            )
        )
    return (jnp.concatenate(query_grads, 0), key_grad, value_grad)


def merge_stats(first, second):
    top_score = jnp.maximum(first[0], second[0])
    row_total = first[1] * jnp.exp(first[0] - top_score) + second[1] * jnp.exp(
        second[0] - top_score
    )
    return (top_score, row_total, first[2] + second[2])


def line_chunk(index, size):
    return pl.ds(pl.multiple_of(index * size, size), size)


def greet_line(me, count):
    barrier = pltpu.get_barrier_semaphore()

    @pl.when(me > 0)
    def _():
        pl.semaphore_signal(
            barrier, inc=1, device_id={"mp": jnp.maximum(me - 1, 0)}, device_id_type=MESH
        )

    @pl.when(me < count - 1)
    def _():
        pl.semaphore_signal(
            barrier, inc=1, device_id={"mp": jnp.minimum(me + 1, count - 1)}, device_id_type=MESH
        )

    peers = jnp.where(me > 0, 1, 0) + jnp.where(me < count - 1, 1, 0)
    pl.semaphore_wait(barrier, peers)


def line_sum(count, chunk, own, wires, sems, prepare, emit):
    me = lax.axis_index("mp")
    from_low, from_high, to_high, to_low = wires
    up_send, up_recv, down_send, down_recv = sems
    length = own.shape[0]
    chunks = length // chunk
    above = jnp.minimum(me + 1, count - 1)
    below = jnp.maximum(me - 1, 0)

    def up_copy(index):
        rows = line_chunk(index, chunk)
        return pltpu.make_async_remote_copy(
            src_ref=to_high.at[rows],
            dst_ref=from_low.at[rows],
            send_sem=up_send.at[index],
            recv_sem=up_recv.at[index],
            device_id={"mp": above},
            device_id_type=MESH,
        )

    def down_copy(index):
        rows = line_chunk(index, chunk)
        return pltpu.make_async_remote_copy(
            src_ref=to_low.at[rows],
            dst_ref=from_high.at[rows],
            send_sem=down_send.at[index],
            recv_sem=down_recv.at[index],
            device_id={"mp": below},
            device_id_type=MESH,
        )

    greet_line(me, count)

    @pl.when(me == 0)
    def _():
        from_low[...] = jnp.zeros_like(from_low)

    @pl.when(me == count - 1)
    def _():
        from_high[...] = jnp.zeros_like(from_high)

    def step(at, carry):
        if prepare is not None:

            @pl.when(at < chunks)
            def _():
                prepare(at)

        up = at - LINE_LAG * me

        @pl.when((up >= 0) & (up < chunks))
        def _():
            rows = line_chunk(up, chunk)

            @pl.when(me > 0)
            def _():
                up_copy(up).wait_recv()

            @pl.when(me < count - 1)
            def _():
                to_high[rows, :] = (
                    from_low[rows, :].astype(jnp.float32) + own[rows, :].astype(jnp.float32)
                ).astype(jnp.bfloat16)
                up_copy(up).start()

        down = at - LINE_LAG * (count - 1 - me)

        @pl.when((down >= 0) & (down < chunks))
        def _():
            rows = line_chunk(down, chunk)

            @pl.when(me < count - 1)
            def _():
                down_copy(down).wait_recv()

            @pl.when(me > 0)
            def _():
                to_low[rows, :] = (
                    from_high[rows, :].astype(jnp.float32) + own[rows, :].astype(jnp.float32)
                ).astype(jnp.bfloat16)
                down_copy(down).start()

        ready = at - LINE_LAG * jnp.maximum(me, count - 1 - me)

        @pl.when((ready >= 0) & (ready < chunks))
        def _():
            rows = line_chunk(ready, chunk)
            total = (
                from_low[rows, :].astype(jnp.float32)
                + own[rows, :].astype(jnp.float32)
                + from_high[rows, :].astype(jnp.float32)
            )
            emit(rows, total)

        return carry

    lax.fori_loop(0, chunks + LINE_LAG * (count - 1), step, 0)

    def drain(index, carry):
        @pl.when(me < count - 1)
        def _():
            up_copy(index).wait_send()

        @pl.when(me > 0)
        def _():
            down_copy(index).wait_send()

        return carry

    lax.fori_loop(0, chunks, drain, 0)


LINE_CHUNK = 32
LINE_LAG = 3


def line_scratch(length, width):
    chunks = length // LINE_CHUNK
    return [pltpu.VMEM((length, width), jnp.bfloat16)] * 4 + [
        pltpu.SemaphoreType.DMA((chunks,))
    ] * 4


def line_call(kernel, name, collective_id, outs, scratch, operands, flops=0):
    size = sum(o.size * o.dtype.itemsize for o in operands) + sum(
        o.size * o.dtype.itemsize for o in outs
    )
    vmem = pl.BlockSpec(memory_space=pltpu.VMEM)
    return pl.pallas_call(
        kernel,
        name=name,
        out_shape=outs,
        in_specs=[vmem] * len(operands),
        out_specs=[vmem] * len(outs),
        scratch_shapes=scratch,
        compiler_params=pltpu.CompilerParams(
            collective_id=collective_id, has_side_effects=True, vmem_limit_bytes=VMEM_LIMIT
        ),
        cost_estimate=pl.CostEstimate(
            flops=flops, bytes_accessed=size + 100_000_000, transcendentals=0
        ),
    )(*operands)


def start_kernel(count, part, gain, shift, rows_out, attn_out, ffn_out, *scratch):
    def emit(rows, total):
        rows_out[rows, :] = total.astype(jnp.bfloat16)
        centre = total - jnp.mean(total, -1, keepdims=True)
        spread = jnp.mean(centre * centre, -1, keepdims=True)
        base = centre * lax.rsqrt(spread + NORM_EPS)
        attn_out[rows, :] = (base * gain[0:1, :] + shift[0:1, :]).astype(jnp.bfloat16)
        ffn_out[rows, :] = (base * gain[1:2, :] + shift[1:2, :]).astype(jnp.bfloat16)

    line_sum(count, LINE_CHUNK, part, scratch[:4], scratch[4:], None, emit)


def resid_kernel(count, part, start, gain, shift, resid_out, final_out, *scratch):
    def emit(rows, total):
        resid = start[rows, :].astype(jnp.float32) + total
        resid_out[rows, :] = resid
        normed = layer_norm(resid, gain[2:3, :], shift[2:3, :])
        final_out[rows, :] = normed.astype(jnp.bfloat16)

    line_sum(count, LINE_CHUNK, part, scratch[:4], scratch[4:], None, emit)


def branch_kernel(count, part, resid, gain, out, *scratch):
    def emit(rows, total):
        values = resid[rows, :]
        centre = values - jnp.mean(values, -1, keepdims=True)
        spread = jnp.mean(centre * centre, -1, keepdims=True)
        inverse = lax.rsqrt(spread + NORM_EPS)
        normed = centre * inverse
        up = total * gain[2:3, :]
        out[rows, :] = (
            inverse
            * (
                up
                - jnp.mean(up, -1, keepdims=True)
                - normed * jnp.mean(up * normed, -1, keepdims=True)
            )
        ).astype(jnp.bfloat16)

    line_sum(count, LINE_CHUNK, part, scratch[:4], scratch[4:], None, emit)


def fold_kernel(splits, count, *refs):
    fulls = refs[0:4]
    groups = refs[4:8]
    losses, master, first, second, bases = refs[8:13]
    loss_out, norm_out, first_out, second_out, master_out = refs[13:18]
    scratch = refs[18:]
    sends = scratch[0:splits]
    recvs = scratch[splits : 2 * splits]
    keeps = scratch[2 * splits : 3 * splits]
    (line_send, line_recv, turn_send, turn_recv, note_send, note_recv, tell_send, tell_recv) = scratch[
        3 * splits : 3 * splits + 8
    ]
    (half_out, half_in, line_out, line_in, turn_out, turn_in, note_out, note_in, tell_out, tell_in) = (
        scratch[3 * splits + 8 :]
    )
    shards = 2**splits
    me = lax.axis_index("dp")
    lane = lax.axis_index("mp")
    full_rows = fulls[0].shape[0] // shards
    group_rows = groups[0].shape[0] // shards
    own_rows = full_rows // count
    bits = [(me // 2**k) % 2 for k in range(splits)]
    mates = [me + 2**k * (1 - 2 * bits[k]) for k in range(splits)]
    peers = [lax.rem(lane + offset, count) for offset in range(count)]
    spot = lane * shards + me
    goal = (spot // count, lax.rem(spot, count))
    place = me * count + lane
    origin = (lax.rem(place, shards), place // shards)
    moved = spot != place

    barrier = pltpu.get_barrier_semaphore()
    for mate in mates:
        pl.semaphore_signal(barrier, inc=1, device_id={"dp": mate, "mp": lane}, device_id_type=MESH)
    for peer in peers[1:]:
        pl.semaphore_signal(barrier, inc=1, device_id={"dp": me, "mp": peer}, device_id_type=MESH)

    @pl.when(moved)
    def _():
        for device in (goal, origin):
            pl.semaphore_signal(
                barrier, inc=1, device_id={"dp": device[0], "mp": device[1]}, device_id_type=MESH
            )

    pl.semaphore_wait(barrier, splits + count - 1 + jnp.where(moved, 2, 0))

    def remote(src, dst, out_sem, in_sem, device):
        return pltpu.make_async_remote_copy(
            src_ref=src,
            dst_ref=dst,
            send_sem=out_sem,
            recv_sem=in_sem,
            device_id={"dp": device[0], "mp": device[1]},
            device_id_type=MESH,
        )

    def piece(index):
        whole = pl.ds(pl.multiple_of(index * full_rows, full_rows), full_rows)
        part = pl.ds(pl.multiple_of(index * group_rows, group_rows), group_rows)
        return jnp.concatenate(
            [ref[whole, :] for ref in fulls] + [ref[part, :] for ref in groups], 0
        )

    started = []
    current = piece
    for k in range(splits):
        half = shards >> (k + 1)
        for i in range(half):
            sends[k][i] = current(2 * i + 1 - bits[k]).astype(jnp.bfloat16)
        copy = remote(sends[k], recvs[k], half_out.at[k], half_in.at[k], (mates[k], lane))
        copy.start()
        started.append(copy)
        for i in range(half):
            keeps[k][i] = current(2 * i + bits[k])
        copy.wait_recv()
        current = functools.partial(
            lambda kept, came, i: kept[i] + came[i].astype(jnp.float32), keeps[k], recvs[k]
        )
    final = keeps[splits - 1]
    final[0] = current(0)

    def chosen(peer):
        return jnp.concatenate(
            [
                final[
                    0,
                    pl.ds(pl.multiple_of(a * full_rows + peer * own_rows, own_rows), own_rows),
                    :,
                ]
                for a in range(4)
            ],
            0,
        )

    turn_send[...] = final[0, 4 * full_rows :, :].astype(jnp.bfloat16)
    turn = remote(turn_send, turn_recv, turn_out, turn_in, goal)

    @pl.when(moved)
    def _():
        turn.start()

    for offset in range(1, count):
        line_send[offset] = chosen(peers[offset]).astype(jnp.bfloat16)
        copy = remote(
            line_send.at[offset],
            line_recv.at[offset],
            line_out.at[offset],
            line_in.at[offset],
            (me, peers[offset]),
        )
        copy.start()
        started.append(copy)
    total = chosen(lane)

    @pl.when(moved)
    def _():
        turn.wait()

    @pl.when(jnp.logical_not(moved))
    def _():
        turn_recv[...] = turn_send[...]

    for copy in started[splits:]:
        copy.wait_recv()
    for offset in range(1, count):
        total = total + line_recv[offset].astype(jnp.float32)
    part = turn_recv[...].astype(jnp.float32)

    column = lax.broadcasted_iota(jnp.int32, (8, 128), 1)
    row = lax.broadcasted_iota(jnp.int32, (8, 128), 0)
    squares = jnp.sum(total * total) + jnp.sum(part * part)
    spot_norm = (row == 0) & (column == 0)
    spot_loss = (row == 0) & (column == 1)
    note = jnp.where(spot_norm, squares, 0.0) + jnp.where(spot_loss, jnp.sum(losses[...]), 0.0)

    def rows_of(index):
        source, slot = (total, (0, 1, 2, 7).index(index)) if index in (0, 1, 2, 7) else (
            part,
            index - 3,
        )
        return source[slot * own_rows : (slot + 1) * own_rows, :]

    turned = [
        jnp.dot(
            rows_of(m), bases[m], precision=HIGH_PRECISION, preferred_element_type=jnp.float32
        )
        for m in range(8)
    ]
    for k in range(splits):
        note_send[k] = note
        copy = remote(
            note_send.at[k], note_recv.at[k], note_out.at[k], note_in.at[k], (mates[k], lane)
        )
        copy.start()
        started.append(copy)
        copy.wait_recv()
        note = note + note_recv[k]
    tell_send[...] = note
    tells = []
    for offset in range(1, count):
        copy = remote(
            tell_send,
            tell_recv.at[offset],
            tell_out.at[offset],
            tell_in.at[offset],
            (me, peers[offset]),
        )
        copy.start()
        tells.append(copy)
    for copy in tells:
        copy.wait_recv()
    everything = note
    for offset in range(1, count):
        everything = everything + tell_recv[offset]
    norm = jnp.sqrt(jnp.sum(jnp.where(spot_norm, everything, 0.0), keepdims=True))
    loss_out[...] = jnp.sum(jnp.where(spot_loss, note, 0.0), keepdims=True)
    norm_out[...] = norm
    factor = jnp.minimum(1.0, CLIP_LIMIT / norm)
    for m in range(8):
        rotated = turned[m] * factor
        new_first = BETA_FIRST * first[m] + (1.0 - BETA_FIRST) * rotated
        new_second = BETA_SECOND * second[m] + (1.0 - BETA_SECOND) * rotated * rotated
        first_out[m] = new_first
        second_out[m] = new_second
        normed = (
            new_first
            / (1.0 - BETA_FIRST**ADAM_STEP)
            / (jnp.sqrt(new_second / (1.0 - BETA_SECOND**ADAM_STEP)) + ADAM_EPS)
        )
        back = lax.dot_general(
            normed,
            bases[m],
            (((1,), (1,)), ((), ())),
            precision=HIGH_PRECISION,
            preferred_element_type=jnp.float32,
        )
        master_out[m] = master[m] - LEARN_RATE * (back + DECAY_RATE * master[m])
    for copy in started + tells:
        copy.wait_send()


def fold_call(fulls, groups, losses, master, first_moment, second_moment, bases):
    shards = lax.axis_size("dp")
    count = lax.axis_size("mp")
    splits = shards.bit_length() - 1
    width = fulls[0].shape[1]
    pile = 4 * (fulls[0].shape[0] + groups[0].shape[0]) // shards
    own = 4 * fulls[0].shape[0] // (shards * count)
    low = jnp.bfloat16
    halves = [shards >> (k + 1) for k in range(splits)]
    dma = pltpu.SemaphoreType.DMA
    scratch = (
        [pltpu.VMEM((half, pile, width), low) for half in halves] * 2
        + [pltpu.VMEM((half, pile, width), jnp.float32) for half in halves]
        + [pltpu.VMEM((count, own, width), low)] * 2
        + [pltpu.VMEM((4 * groups[0].shape[0] // shards, width), low)] * 2
        + [pltpu.VMEM((splits, 8, 128), jnp.float32)] * 2
        + [pltpu.VMEM((8, 128), jnp.float32), pltpu.VMEM((count, 8, 128), jnp.float32)]
        + [dma((splits,))] * 2
        + [dma((count,))] * 2
        + [dma(())] * 2
        + [dma((splits,))] * 2
        + [dma((count,))] * 2
    )
    scalar = jax.ShapeDtypeStruct((1, 1), jnp.float32)
    state = jax.ShapeDtypeStruct(master.shape, jnp.float32)
    return line_call(
        functools.partial(fold_kernel, splits, count),
        "fold",
        3,
        [scalar, scalar, state, state, state],
        scratch,
        [*fulls, *groups, losses, master, first_moment, second_moment, bases],
    )


def per_device(
    token_ids,
    prompt_len,
    example_len,
    embedding,
    w_qkv,
    w_out,
    w_in,
    b_in,
    w_down,
    unembed,
    ln_gain,
    ln_bias,
    master,
    first_moment,
    second_moment,
    eigen_bases,
):
    group_count = lax.axis_size("mp")
    group_index = lax.axis_index("mp")
    adapters = lax.all_gather(master.astype(jnp.bfloat16), ("dp", "mp"), axis=1, tiled=True)
    head_local = lax.all_gather(unembed, "dp", axis=0, tiled=True)
    examples, length = token_ids.shape
    width = embedding.shape[0]
    vocab_local = head_local.shape[1]
    rows = examples * length
    local_heads = HEADS // group_count
    group_width = local_heads * HD
    flat_ids = token_ids.reshape(rows)
    relative = flat_ids - group_index * width
    inside = (relative >= 0) & (relative < width)
    picked = jnp.where(
        inside[:, None], embedding[jnp.clip(relative, 0, width - 1)].astype(jnp.float32), 0.0
    )
    shape_low = jax.ShapeDtypeStruct((rows, D), jnp.bfloat16)
    shape_wide = jax.ShapeDtypeStruct((rows, D), jnp.float32)
    start_rows, normed_attn, normed_ffn = line_call(
        functools.partial(start_kernel, group_count),
        "start_rows",
        0,
        [shape_low] * 3,
        line_scratch(rows, D),
        [picked.astype(jnp.bfloat16), ln_gain, ln_bias],
    )
    leading_example = lax.axis_index("dp") * examples
    prompts = lax.dynamic_slice_in_dim(prompt_len, leading_example, examples)
    totals = lax.dynamic_slice_in_dim(example_len, leading_example, examples)
    position = jnp.arange(length)
    keep = (position[None, :] >= prompts[:, None] - 1) & (position[None, :] < totals[:, None] - 1)
    count = jnp.sum(example_len - prompt_len).astype(jnp.float32)
    row_weight = keep.reshape(rows).astype(jnp.float32) / count
    target = jnp.roll(token_ids, -1, axis=1).reshape(rows)
    inner = jnp.dot(
        normed_attn,
        jnp.concatenate([adapters[0], adapters[1], adapters[2]], 1),
        preferred_element_type=jnp.float32,
    ).astype(jnp.bfloat16)
    base = jnp.dot(normed_attn, w_qkv, preferred_element_type=jnp.float32).reshape(
        rows, local_heads, 3, HD
    )
    adapter_rows = [
        lax.dynamic_slice_in_dim(
            adapters[3 + selector_index], group_index * group_width, group_width, 0
        )
        for selector_index in range(3)
    ]
    pre_parts = []
    for selector_index in range(3):
        extra = jnp.einsum(
            "lr,dr->ld",
            inner[:, selector_index * R : (selector_index + 1) * R],
            adapter_rows[selector_index],
            preferred_element_type=jnp.float32,
        )
        pre_parts.append(base[:, :, selector_index] + extra.reshape(rows, local_heads, HD))
    cosine, sine = rope_tables(length)
    queries = rotate(pre_parts[0].reshape(examples, length, local_heads, HD), cosine, sine).astype(
        jnp.bfloat16
    )
    key_rows = rotate(pre_parts[1].reshape(examples, length, local_heads, HD), cosine, sine).astype(
        jnp.bfloat16
    )
    value_rows = pre_parts[2].reshape(examples, length, local_heads, HD).astype(jnp.bfloat16)
    sample = 0
    context_here, spread_local = attend(queries[sample], key_rows[sample], value_rows[sample])
    spreads = [spread_local]
    context = context_here.reshape(rows, group_width)
    out_rows = lax.dynamic_slice_in_dim(adapters[6], group_index * group_width, group_width, 0)
    inner_out = jnp.dot(context, out_rows, preferred_element_type=jnp.float32).astype(jnp.bfloat16)
    hidden = jax.nn.gelu(
        jnp.dot(normed_ffn, w_in, preferred_element_type=jnp.float32) + b_in, approximate=False
    ).astype(jnp.bfloat16)
    partial_value = (
        jnp.dot(context, w_out, preferred_element_type=jnp.float32)
        + jnp.einsum("lr,dr->ld", inner_out, adapters[7], preferred_element_type=jnp.float32)
        + jnp.dot(hidden, w_down, preferred_element_type=jnp.float32)
    )
    resid, final_rows = line_call(
        functools.partial(resid_kernel, group_count),
        "resid_rows",
        1,
        [shape_wide, shape_low],
        line_scratch(rows, D),
        [partial_value.astype(jnp.bfloat16), start_rows, ln_gain, ln_bias],
    )
    row_block = min(256, rows)
    blocks = rows // row_block
    vocab_ids = jnp.arange(vocab_local)[None, :]

    def block_stats(pieces):
        rows_here, target_here = pieces
        logits = jnp.dot(rows_here, head_local, preferred_element_type=jnp.float32)
        top_score = jnp.max(logits, -1)
        row_total = jnp.sum(jnp.exp(logits - top_score[:, None]), -1)
        hit = vocab_ids == (target_here - group_index * vocab_local)[:, None]
        return (top_score, row_total, jnp.sum(jnp.where(hit, logits, 0.0), -1))

    stats = lax.map(
        block_stats, (final_rows.reshape(blocks, row_block, D), target.reshape(blocks, row_block))
    )
    top_score, row_total, target_logit = merged(
        (stats[0].reshape(rows), stats[1].reshape(rows), stats[2].reshape(rows)), "mp", merge_stats
    )
    spread_all = top_score + jnp.log(row_total)
    losses = ((spread_all - target_logit) * row_weight).reshape(rows // 128, 128)

    def block_back(pieces):
        rows_here, target_here, spread_local, weight_here = pieces
        logits = jnp.dot(rows_here, head_local, preferred_element_type=jnp.float32)
        hit = (vocab_ids == (target_here - group_index * vocab_local)[:, None]).astype(jnp.float32)
        logit_grad = (
            (jnp.exp(logits - spread_local[:, None]) - hit) * weight_here[:, None]
        ).astype(jnp.bfloat16)
        return jnp.einsum("lv,dv->ld", logit_grad, head_local, preferred_element_type=jnp.float32)

    head_grad = lax.map(
        block_back,
        (
            final_rows.reshape(blocks, row_block, D),
            target.reshape(blocks, row_block),
            spread_all.reshape(blocks, row_block),
            row_weight.reshape(blocks, row_block),
        ),
    ).reshape(rows, D)
    (branch_grad,) = line_call(
        functools.partial(branch_kernel, group_count),
        "branch_rows",
        2,
        [shape_low],
        line_scratch(rows, D),
        [head_grad.astype(jnp.bfloat16), resid, ln_gain],
    )
    inner_out_grad = jnp.dot(branch_grad, adapters[7], preferred_element_type=jnp.float32).astype(
        jnp.bfloat16
    )
    grad_out_b = jnp.einsum("ld,lr->dr", branch_grad, inner_out, preferred_element_type=jnp.float32)
    grad_out_a = jnp.einsum(
        "ld,lr->dr", context, inner_out_grad, preferred_element_type=jnp.float32
    )
    context_grad = jnp.einsum(
        "ld,ed->le", branch_grad, w_out, preferred_element_type=jnp.float32
    ) + jnp.einsum("lr,dr->ld", inner_out_grad, out_rows, preferred_element_type=jnp.float32)
    context_grad = context_grad.astype(jnp.bfloat16).reshape(examples, length, local_heads, HD)
    sample = 0
    query_grad, key_grad, value_grad = attend_back(
        queries[sample], key_rows[sample], value_rows[sample], spreads[sample], context_grad[sample]
    )
    query_parts = [rotate_back(query_grad, cosine, sine)]
    key_parts = [rotate_back(key_grad, cosine, sine)]
    value_parts = [value_grad]
    pre_grads = [
        parts[0].reshape(rows, group_width).astype(jnp.bfloat16)
        for parts in (query_parts, key_parts, value_parts)
    ]
    complete_gradients = []
    local_grads = []
    for selector_index in range(3):
        projected_values = jnp.einsum(
            "ld,le->de", normed_attn, pre_grads[selector_index], preferred_element_type=jnp.float32
        )
        complete_gradients.append(
            jnp.dot(
                projected_values,
                adapter_rows[selector_index].astype(jnp.float32),
                precision=HIGH_PRECISION,
            )
        )
        local_grads.append(
            jnp.einsum(
                "ld,lr->dr",
                pre_grads[selector_index],
                inner[:, selector_index * R : (selector_index + 1) * R],
                preferred_element_type=jnp.float32,
            )
        )
    local_grads.append(grad_out_a)
    mean_loss, grad_norm, new_first, new_second, new_master = fold_call(
        [*complete_gradients, grad_out_b],
        local_grads,
        losses,
        master,
        first_moment,
        second_moment,
        eigen_bases,
    )
    return (mean_loss.reshape(()), grad_norm.reshape(()), new_first, new_second, new_master)


def solution(mesh):
    placed = (
        P("dp", None),
        P(),
        P(),
        P("mp", None),
        P(None, "mp"),
        P("mp", None),
        P(None, "mp"),
        P("mp"),
        P("mp", None),
        P("dp", "mp"),
        P(),
        P(),
        P(None, ("dp", "mp"), None),
        P(None, ("dp", "mp"), None),
        P(None, ("dp", "mp"), None),
        P(),
    )
    return jax.shard_map(
        per_device,
        mesh=mesh,
        in_specs=placed,
        out_specs=(
            P(),
            P(),
            P(None, ("dp", "mp"), None),
            P(None, ("dp", "mp"), None),
            P(None, ("dp", "mp"), None),
        ),
        check_vma=False,
    )
```

```python
import functools

import jax
import jax.numpy as jnp
from jax import lax
from jax.experimental import pallas as pl
from jax.experimental.pallas import tpu as pltpu
from jax.sharding import PartitionSpec as P

MESH = pl.DeviceIdType.MESH
VMEM_LIMIT = 60 * 1024 * 1024

D = 1024
HEADS = 16
R = 128
ADAM_STEP = 10
HD = 64
ROT = 16


HIGH_PRECISION = lax.Precision.HIGHEST
NORM_EPS = 1e-05
ROPE_BASE = 10000.0
CLIP_LIMIT = 0.01
LEARN_RATE = 0.02
BETA_FIRST = 0.9
BETA_SECOND = 0.999
ADAM_EPS = 1e-08
DECAY_RATE = 0.01


def layer_norm(values, gain, shift):
    centre = values - jnp.mean(values, -1, keepdims=True)
    spread = jnp.mean(centre * centre, -1, keepdims=True)
    return centre * lax.rsqrt(spread + NORM_EPS) * gain + shift


def rope_tables(length):
    half = ROT // 2
    freqs = ROPE_BASE ** (-2.0 * jnp.arange(half, dtype=jnp.float32) / ROT)
    angles = jnp.arange(length, dtype=jnp.float32)[:, None] * freqs[None, :]
    return (jnp.cos(angles)[:, None, :], jnp.sin(angles)[:, None, :])


def rotate(field, cosine, sine):
    half = ROT // 2
    first = field[..., :half]
    second = field[..., half:ROT]
    return jnp.concatenate(
        [first * cosine - second * sine, second * cosine + first * sine, field[..., ROT:]], -1
    )


def rotate_back(upstream, cosine, sine):
    half = ROT // 2
    first = upstream[..., :half]
    second = upstream[..., half:ROT]
    return jnp.concatenate(
        [first * cosine + second * sine, second * cosine - first * sine, upstream[..., ROT:]], -1
    )


def masked_scores(queries, key_rows, start_row, stop_row):
    scores = jnp.einsum(
        "qhd,khd->hqk",
        queries[start_row:stop_row],
        key_rows[:stop_row],
        preferred_element_type=jnp.float32,
    ) * HD ** (-0.5)
    query_pos = start_row + jnp.arange(stop_row - start_row)[:, None]
    causal = jnp.arange(stop_row)[None, :] <= query_pos
    return jnp.where(causal[None], scores, -1e30)


def attend(queries, key_rows, value_rows):
    length = queries.shape[0]
    row_block = min(512, length)
    outputs = []
    spreads = []
    for start_row in range(0, length, row_block):
        stop_row = start_row + row_block
        scores = masked_scores(queries, key_rows, start_row, stop_row)
        top_score = jnp.max(scores, -1, keepdims=True)
        weights = jnp.exp(scores - top_score)
        row_total = jnp.sum(weights, -1, keepdims=True)
        probs = (weights / row_total).astype(jnp.bfloat16)
        outputs.append(
            jnp.einsum(
                "hqk,khd->qhd", probs, value_rows[:stop_row], preferred_element_type=jnp.float32
            )
        )
        spreads.append((top_score + jnp.log(row_total))[..., 0])
    return (jnp.concatenate(outputs, 0).astype(jnp.bfloat16), jnp.concatenate(spreads, 1))


def attend_back(queries, key_rows, value_rows, spreads, upstream):
    length = queries.shape[0]
    row_block = min(512, length)
    scaling = HD ** (-0.5)
    query_grads = []
    key_grad = jnp.zeros(key_rows.shape, jnp.float32)
    value_grad = jnp.zeros(value_rows.shape, jnp.float32)
    for start_row in range(0, length, row_block):
        stop_row = start_row + row_block
        scores = masked_scores(queries, key_rows, start_row, stop_row)
        probs = jnp.exp(scores - spreads[:, start_row:stop_row, None])
        grad_here = upstream[start_row:stop_row]
        prob_grad = jnp.einsum(
            "qhd,khd->hqk", grad_here, value_rows[:stop_row], preferred_element_type=jnp.float32
        )
        inner_sum = jnp.sum(probs * prob_grad, -1, keepdims=True)
        score_grad = (probs * (prob_grad - inner_sum)).astype(jnp.bfloat16)
        query_grads.append(
            jnp.einsum(
                "hqk,khd->qhd", score_grad, key_rows[:stop_row], preferred_element_type=jnp.float32
            )
            * scaling
        )
        key_grad = key_grad.at[:stop_row].add(
            jnp.einsum(
                "hqk,qhd->khd",
                score_grad,
                queries[start_row:stop_row],
                preferred_element_type=jnp.float32,
            )
            * scaling
        )
        value_grad = value_grad.at[:stop_row].add(
            jnp.einsum(
                "hqk,qhd->khd",
                probs.astype(jnp.bfloat16),
                grad_here,
                preferred_element_type=jnp.float32,
            )
        )
    return (jnp.concatenate(query_grads, 0), key_grad, value_grad)


def line_chunk(index, size):
    return pl.ds(pl.multiple_of(index * size, size), size)


def greet_line(me, count):
    barrier = pltpu.get_barrier_semaphore()

    @pl.when(me > 0)
    def _():
        pl.semaphore_signal(
            barrier, inc=1, device_id={"mp": jnp.maximum(me - 1, 0)}, device_id_type=MESH
        )

    @pl.when(me < count - 1)
    def _():
        pl.semaphore_signal(
            barrier, inc=1, device_id={"mp": jnp.minimum(me + 1, count - 1)}, device_id_type=MESH
        )

    peers = jnp.where(me > 0, 1, 0) + jnp.where(me < count - 1, 1, 0)
    pl.semaphore_wait(barrier, peers)


def greet_peers(me, count):
    barrier = pltpu.get_barrier_semaphore()
    for offset in range(1, count):
        pl.semaphore_signal(
            barrier, inc=1, device_id={"mp": lax.rem(me + offset, count)}, device_id_type=MESH
        )
    pl.semaphore_wait(barrier, count - 1)


def line_sum(count, chunk, own, wires, sems, prepare, emit, greet=True):
    me = lax.axis_index("mp")
    from_low, from_high, to_high, to_low = wires
    up_send, up_recv, down_send, down_recv = sems
    length = own.shape[0]
    chunks = length // chunk
    above = jnp.minimum(me + 1, count - 1)
    below = jnp.maximum(me - 1, 0)

    def up_copy(index):
        rows = line_chunk(index, chunk)
        return pltpu.make_async_remote_copy(
            src_ref=to_high.at[rows],
            dst_ref=from_low.at[rows],
            send_sem=up_send.at[index],
            recv_sem=up_recv.at[index],
            device_id={"mp": above},
            device_id_type=MESH,
        )

    def down_copy(index):
        rows = line_chunk(index, chunk)
        return pltpu.make_async_remote_copy(
            src_ref=to_low.at[rows],
            dst_ref=from_high.at[rows],
            send_sem=down_send.at[index],
            recv_sem=down_recv.at[index],
            device_id={"mp": below},
            device_id_type=MESH,
        )

    if greet:
        greet_line(me, count)

    @pl.when(me == 0)
    def _():
        from_low[...] = jnp.zeros_like(from_low)

    @pl.when(me == count - 1)
    def _():
        from_high[...] = jnp.zeros_like(from_high)

    def step(at, carry):
        if prepare is not None:

            @pl.when(at < chunks)
            def _():
                prepare(at)

        up = at - LINE_LAG * me

        @pl.when((up >= 0) & (up < chunks))
        def _():
            rows = line_chunk(up, chunk)

            @pl.when(me > 0)
            def _():
                up_copy(up).wait_recv()

            @pl.when(me < count - 1)
            def _():
                to_high[rows, :] = (
                    from_low[rows, :].astype(jnp.float32) + own[rows, :].astype(jnp.float32)
                ).astype(jnp.bfloat16)
                up_copy(up).start()

        down = at - LINE_LAG * (count - 1 - me)

        @pl.when((down >= 0) & (down < chunks))
        def _():
            rows = line_chunk(down, chunk)

            @pl.when(me < count - 1)
            def _():
                down_copy(down).wait_recv()

            @pl.when(me > 0)
            def _():
                to_low[rows, :] = (
                    from_high[rows, :].astype(jnp.float32) + own[rows, :].astype(jnp.float32)
                ).astype(jnp.bfloat16)
                down_copy(down).start()

        ready = at - LINE_LAG * jnp.maximum(me, count - 1 - me)

        @pl.when((ready >= 0) & (ready < chunks))
        def _():
            rows = line_chunk(ready, chunk)
            total = (
                from_low[rows, :].astype(jnp.float32)
                + own[rows, :].astype(jnp.float32)
                + from_high[rows, :].astype(jnp.float32)
            )
            emit(rows, total)

        return carry

    lax.fori_loop(0, chunks + LINE_LAG * (count - 1), step, 0)

    def drain(index, carry):
        @pl.when(me < count - 1)
        def _():
            up_copy(index).wait_send()

        @pl.when(me > 0)
        def _():
            down_copy(index).wait_send()

        return carry

    lax.fori_loop(0, chunks, drain, 0)


LINE_CHUNK = 32
LINE_LAG = 3


def line_scratch(length, width):
    chunks = length // LINE_CHUNK
    return [pltpu.VMEM((length, width), jnp.bfloat16)] * 4 + [
        pltpu.SemaphoreType.DMA((chunks,))
    ] * 4


def line_call(kernel, name, collective_id, outs, scratch, operands, flops=0):
    size = sum(o.size * o.dtype.itemsize for o in operands) + sum(
        o.size * o.dtype.itemsize for o in outs
    )
    vmem = pl.BlockSpec(memory_space=pltpu.VMEM)
    return pl.pallas_call(
        kernel,
        name=name,
        out_shape=outs,
        in_specs=[vmem] * len(operands),
        out_specs=[vmem] * len(outs),
        scratch_shapes=scratch,
        compiler_params=pltpu.CompilerParams(
            collective_id=collective_id, has_side_effects=True, vmem_limit_bytes=VMEM_LIMIT
        ),
        cost_estimate=pl.CostEstimate(
            flops=flops, bytes_accessed=size + 100_000_000, transcendentals=0
        ),
    )(*operands)


def start_kernel(count, part, gain, shift, rows_out, attn_out, ffn_out, *scratch):
    def emit(rows, total):
        rows_out[rows, :] = total.astype(jnp.bfloat16)
        centre = total - jnp.mean(total, -1, keepdims=True)
        spread = jnp.mean(centre * centre, -1, keepdims=True)
        base = centre * lax.rsqrt(spread + NORM_EPS)
        attn_out[rows, :] = (base * gain[0:1, :] + shift[0:1, :]).astype(jnp.bfloat16)
        ffn_out[rows, :] = (base * gain[1:2, :] + shift[1:2, :]).astype(jnp.bfloat16)

    line_sum(count, LINE_CHUNK, part, scratch[:4], scratch[4:], None, emit)


def resid_kernel(count, part, start, gain, shift, resid_out, final_out, *scratch):
    def emit(rows, total):
        resid = start[rows, :].astype(jnp.float32) + total
        resid_out[rows, :] = resid
        normed = layer_norm(resid, gain[2:3, :], shift[2:3, :])
        final_out[rows, :] = normed.astype(jnp.bfloat16)

    line_sum(count, LINE_CHUNK, part, scratch[:4], scratch[4:], None, emit)


def branch_kernel(count, raw, hits, stats, weight, resid, gain, out, loss_out, *scratch):
    own, note_send, note_recv, scales, note_out, note_in = scratch[8:]
    me = lax.axis_index("mp")
    rows_all = raw.shape[0]
    greet_peers(me, count)
    note_send[...] = stats[...].T[0:8, :]
    copies = []
    for offset in range(1, count):
        copy = pltpu.make_async_remote_copy(
            src_ref=note_send,
            dst_ref=note_recv.at[offset],
            send_sem=note_out.at[offset],
            recv_sem=note_in.at[offset],
            device_id={"mp": lax.rem(me + offset, count)},
            device_id_type=MESH,
        )
        copy.start()
        copies.append(copy)
    mine = note_send[...]
    for copy in copies:
        copy.wait_recv()
    others = [mine] + [note_recv[offset] for offset in range(1, count)]
    top = functools.reduce(jnp.maximum, [part[0:1, :] for part in others])
    total = sum(part[1:2, :] * jnp.exp(part[0:1, :] - top) for part in others)
    found = sum(part[2:3, :] for part in others)
    spread_row = top + jnp.log(total)
    share = weight[...]
    loss_out[...] = (spread_row - found) * share
    factor = jnp.exp(mine[0:1, :] - spread_row) * share
    pair = jnp.concatenate([factor, share, jnp.zeros((126, rows_all), jnp.float32)], 0)
    scales[...] = pair.T

    def prepare(at):
        rows = line_chunk(at, LINE_CHUNK)
        scale = scales[rows, :]
        own[rows, :] = (
            raw[rows, :] * scale[:, 0:1] - hits[rows, :].astype(jnp.float32) * scale[:, 1:2]
        ).astype(jnp.bfloat16)

    def emit(rows, total):
        values = resid[rows, :]
        centre = values - jnp.mean(values, -1, keepdims=True)
        spread = jnp.mean(centre * centre, -1, keepdims=True)
        inverse = lax.rsqrt(spread + NORM_EPS)
        normed = centre * inverse
        up = total * gain[2:3, :]
        out[rows, :] = (
            inverse
            * (
                up
                - jnp.mean(up, -1, keepdims=True)
                - normed * jnp.mean(up * normed, -1, keepdims=True)
            )
        ).astype(jnp.bfloat16)

    line_sum(count, LINE_CHUNK, own, scratch[:4], scratch[4:8], prepare, emit, greet=False)
    for copy in copies:
        copy.wait_send()


def loss_kernel(vocab, tile, values, ahead, behind, hits, acc, stats, logits, probs, tops, sums):
    at = pl.program_id(0)
    tiles = pl.num_programs(0) - 1
    rows_all = values.shape[0]

    @pl.when(at == 0)
    def _():
        acc[...] = jnp.zeros_like(acc)
        tops[...] = jnp.full_like(tops, -1e29)
        sums[...] = jnp.zeros_like(sums)
        logits[...] = jnp.full_like(logits, -1e30)

    tail = vocab % tile
    if tail:

        @pl.when(at >= tiles - 1)
        def _():
            ahead[tail:, :] = jnp.zeros((tile - tail, ahead.shape[1]), ahead.dtype)

        @pl.when(at >= tiles)
        def _():
            behind[tail:, :] = jnp.zeros((tile - tail, behind.shape[1]), behind.dtype)

    ids = (at - 1) * tile + lax.broadcasted_iota(jnp.int32, (1, tile), 1)
    scores = logits[...] + jnp.where(ids < vocab, 0.0, -1e30)
    old = tops[:, 0:1]
    new = jnp.maximum(old, jnp.max(scores, -1, keepdims=True))
    weights = jnp.exp(scores - new)
    shrink = jnp.exp(old - new)
    sums[...] = sums[...] * shrink + jnp.sum(weights, -1, keepdims=True)
    tops[...] = jnp.broadcast_to(new, tops.shape)
    acc[...] = acc[...] * shrink
    probs[...] = weights.astype(jnp.bfloat16)
    logits[...] = lax.dot_general(
        values[...], ahead[...], (((1,), (1,)), ((), ())), preferred_element_type=jnp.float32
    )
    acc[...] += jnp.dot(probs[...], behind[...], preferred_element_type=jnp.float32)

    @pl.when(at == tiles)
    def _():
        found = jnp.sum(
            values[...].astype(jnp.float32) * hits[...].astype(jnp.float32), -1, keepdims=True
        )
        column = lax.broadcasted_iota(jnp.int32, (rows_all, 128), 1)
        stats[...] = jnp.where(
            column == 0, tops[...], jnp.where(column == 1, sums[...], found)
        )


LOSS_TILE = 512


def loss_call(values, head_rows, hits):
    rows, width = values.shape
    vocab = head_rows.shape[0]
    tile = LOSS_TILE
    tiles = pl.cdiv(vocab, tile)
    whole = pl.BlockSpec((rows, width), lambda j: (0, 0))
    return pl.pallas_call(
        functools.partial(loss_kernel, vocab, tile),
        name="loss",
        grid=(tiles + 1,),
        in_specs=[
            whole,
            pl.BlockSpec((tile, width), lambda j: (jnp.minimum(j, tiles - 1), 0)),
            pl.BlockSpec((tile, width), lambda j: (jnp.maximum(j - 1, 0), 0)),
            whole,
        ],
        out_specs=[whole, pl.BlockSpec((rows, 128), lambda j: (0, 0))],
        out_shape=[
            jax.ShapeDtypeStruct((rows, width), jnp.float32),
            jax.ShapeDtypeStruct((rows, 128), jnp.float32),
        ],
        scratch_shapes=[
            pltpu.VMEM((rows, tile), jnp.float32),
            pltpu.VMEM((rows, tile), jnp.bfloat16),
            pltpu.VMEM((rows, 128), jnp.float32),
            pltpu.VMEM((rows, 128), jnp.float32),
        ],
        compiler_params=pltpu.CompilerParams(vmem_limit_bytes=VMEM_LIMIT),
        cost_estimate=pl.CostEstimate(
            flops=4 * rows * width * vocab,
            bytes_accessed=4 * width * vocab,
            transcendentals=rows * vocab,
        ),
    )(values, head_rows, head_rows, hits)


def fold_kernel(splits, count, *refs):
    fulls = refs[0:4]
    groups = refs[4:8]
    losses, master, first, second, bases = refs[8:13]
    loss_out, norm_out, first_out, second_out, master_out = refs[13:18]
    scratch = refs[18:]
    sends = scratch[0:splits]
    recvs = scratch[splits : 2 * splits]
    keeps = scratch[2 * splits : 3 * splits]
    (line_send, line_recv, turn_send, turn_recv, note_send, note_recv, tell_send, tell_recv) = scratch[
        3 * splits : 3 * splits + 8
    ]
    (half_out, half_in, line_out, line_in, turn_out, turn_in, note_out, note_in, tell_out, tell_in) = (
        scratch[3 * splits + 8 :]
    )
    shards = 2**splits
    me = lax.axis_index("dp")
    lane = lax.axis_index("mp")
    full_rows = fulls[0].shape[0] // shards
    group_rows = groups[0].shape[0] // shards
    own_rows = full_rows // count
    bits = [(me // 2**k) % 2 for k in range(splits)]
    mates = [me + 2**k * (1 - 2 * bits[k]) for k in range(splits)]
    peers = [lax.rem(lane + offset, count) for offset in range(count)]
    spot = lane * shards + me
    goal = (spot // count, lax.rem(spot, count))
    place = me * count + lane
    origin = (lax.rem(place, shards), place // shards)
    moved = spot != place

    barrier = pltpu.get_barrier_semaphore()
    for mate in mates:
        pl.semaphore_signal(barrier, inc=1, device_id={"dp": mate, "mp": lane}, device_id_type=MESH)
    for peer in peers[1:]:
        pl.semaphore_signal(barrier, inc=1, device_id={"dp": me, "mp": peer}, device_id_type=MESH)

    @pl.when(moved)
    def _():
        for device in (goal, origin):
            pl.semaphore_signal(
                barrier, inc=1, device_id={"dp": device[0], "mp": device[1]}, device_id_type=MESH
            )

    pl.semaphore_wait(barrier, splits + count - 1 + jnp.where(moved, 2, 0))

    def remote(src, dst, out_sem, in_sem, device):
        return pltpu.make_async_remote_copy(
            src_ref=src,
            dst_ref=dst,
            send_sem=out_sem,
            recv_sem=in_sem,
            device_id={"dp": device[0], "mp": device[1]},
            device_id_type=MESH,
        )

    def piece(index):
        whole = pl.ds(pl.multiple_of(index * full_rows, full_rows), full_rows)
        part = pl.ds(pl.multiple_of(index * group_rows, group_rows), group_rows)
        return jnp.concatenate(
            [ref[whole, :] for ref in fulls] + [ref[part, :] for ref in groups], 0
        )

    started = []
    current = piece
    for k in range(splits):
        half = shards >> (k + 1)
        for i in range(half):
            sends[k][i] = current(2 * i + 1 - bits[k]).astype(jnp.bfloat16)
        copy = remote(sends[k], recvs[k], half_out.at[k], half_in.at[k], (mates[k], lane))
        copy.start()
        started.append(copy)
        for i in range(half):
            keeps[k][i] = current(2 * i + bits[k])
        copy.wait_recv()
        current = functools.partial(
            lambda kept, came, i: kept[i] + came[i].astype(jnp.float32), keeps[k], recvs[k]
        )
    final = keeps[splits - 1]
    final[0] = current(0)

    def chosen(peer):
        return jnp.concatenate(
            [
                final[
                    0,
                    pl.ds(pl.multiple_of(a * full_rows + peer * own_rows, own_rows), own_rows),
                    :,
                ]
                for a in range(4)
            ],
            0,
        )

    turn_send[...] = final[0, 4 * full_rows :, :].astype(jnp.bfloat16)
    turn = remote(turn_send, turn_recv, turn_out, turn_in, goal)

    @pl.when(moved)
    def _():
        turn.start()

    for offset in range(1, count):
        line_send[offset] = chosen(peers[offset]).astype(jnp.bfloat16)
        copy = remote(
            line_send.at[offset],
            line_recv.at[offset],
            line_out.at[offset],
            line_in.at[offset],
            (me, peers[offset]),
        )
        copy.start()
        started.append(copy)
    total = chosen(lane)

    @pl.when(moved)
    def _():
        turn.wait()

    @pl.when(jnp.logical_not(moved))
    def _():
        turn_recv[...] = turn_send[...]

    for copy in started[splits:]:
        copy.wait_recv()
    for offset in range(1, count):
        total = total + line_recv[offset].astype(jnp.float32)
    part = turn_recv[...].astype(jnp.float32)

    column = lax.broadcasted_iota(jnp.int32, (8, 128), 1)
    row = lax.broadcasted_iota(jnp.int32, (8, 128), 0)
    squares = jnp.sum(total * total) + jnp.sum(part * part)
    spot_norm = (row == 0) & (column == 0)
    spot_loss = (row == 0) & (column == 1)
    note = jnp.where(spot_norm, squares, 0.0) + jnp.where(spot_loss, jnp.sum(losses[...]), 0.0)

    def rows_of(index):
        source, slot = (total, (0, 1, 2, 7).index(index)) if index in (0, 1, 2, 7) else (
            part,
            index - 3,
        )
        return source[slot * own_rows : (slot + 1) * own_rows, :]

    turned = [
        jnp.dot(
            rows_of(m), bases[m], precision=HIGH_PRECISION, preferred_element_type=jnp.float32
        )
        for m in range(8)
    ]
    for k in range(splits):
        note_send[k] = note
        copy = remote(
            note_send.at[k], note_recv.at[k], note_out.at[k], note_in.at[k], (mates[k], lane)
        )
        copy.start()
        started.append(copy)
        copy.wait_recv()
        note = note + note_recv[k]
    tell_send[...] = note
    tells = []
    for offset in range(1, count):
        copy = remote(
            tell_send,
            tell_recv.at[offset],
            tell_out.at[offset],
            tell_in.at[offset],
            (me, peers[offset]),
        )
        copy.start()
        tells.append(copy)
    for copy in tells:
        copy.wait_recv()
    everything = note
    for offset in range(1, count):
        everything = everything + tell_recv[offset]
    norm = jnp.sqrt(jnp.sum(jnp.where(spot_norm, everything, 0.0), keepdims=True))
    loss_out[...] = jnp.sum(jnp.where(spot_loss, note, 0.0), keepdims=True)
    norm_out[...] = norm
    factor = jnp.minimum(1.0, CLIP_LIMIT / norm)
    for m in range(8):
        rotated = turned[m] * factor
        new_first = BETA_FIRST * first[m] + (1.0 - BETA_FIRST) * rotated
        new_second = BETA_SECOND * second[m] + (1.0 - BETA_SECOND) * rotated * rotated
        first_out[m] = new_first
        second_out[m] = new_second
        normed = (
            new_first
            / (1.0 - BETA_FIRST**ADAM_STEP)
            / (jnp.sqrt(new_second / (1.0 - BETA_SECOND**ADAM_STEP)) + ADAM_EPS)
        )
        back = lax.dot_general(
            normed,
            bases[m],
            (((1,), (1,)), ((), ())),
            precision=HIGH_PRECISION,
            preferred_element_type=jnp.float32,
        )
        master_out[m] = master[m] - LEARN_RATE * (back + DECAY_RATE * master[m])
    for copy in started + tells:
        copy.wait_send()


def fold_call(fulls, groups, losses, master, first_moment, second_moment, bases):
    shards = lax.axis_size("dp")
    count = lax.axis_size("mp")
    splits = shards.bit_length() - 1
    width = fulls[0].shape[1]
    pile = 4 * (fulls[0].shape[0] + groups[0].shape[0]) // shards
    own = 4 * fulls[0].shape[0] // (shards * count)
    low = jnp.bfloat16
    halves = [shards >> (k + 1) for k in range(splits)]
    dma = pltpu.SemaphoreType.DMA
    scratch = (
        [pltpu.VMEM((half, pile, width), low) for half in halves] * 2
        + [pltpu.VMEM((half, pile, width), jnp.float32) for half in halves]
        + [pltpu.VMEM((count, own, width), low)] * 2
        + [pltpu.VMEM((4 * groups[0].shape[0] // shards, width), low)] * 2
        + [pltpu.VMEM((splits, 8, 128), jnp.float32)] * 2
        + [pltpu.VMEM((8, 128), jnp.float32), pltpu.VMEM((count, 8, 128), jnp.float32)]
        + [dma((splits,))] * 2
        + [dma((count,))] * 2
        + [dma(())] * 2
        + [dma((splits,))] * 2
        + [dma((count,))] * 2
    )
    scalar = jax.ShapeDtypeStruct((1, 1), jnp.float32)
    state = jax.ShapeDtypeStruct(master.shape, jnp.float32)
    return line_call(
        functools.partial(fold_kernel, splits, count),
        "fold",
        3,
        [scalar, scalar, state, state, state],
        scratch,
        [*fulls, *groups, losses, master, first_moment, second_moment, bases],
    )


def per_device(
    token_ids,
    prompt_len,
    example_len,
    embedding,
    w_qkv,
    w_out,
    w_in,
    b_in,
    w_down,
    unembed,
    ln_gain,
    ln_bias,
    master,
    first_moment,
    second_moment,
    eigen_bases,
):
    group_count = lax.axis_size("mp")
    group_index = lax.axis_index("mp")
    adapters = lax.all_gather(master.astype(jnp.bfloat16), ("dp", "mp"), axis=1, tiled=True)
    head_rows = lax.all_gather(unembed.T, "dp", axis=1, tiled=True)
    examples, length = token_ids.shape
    width = embedding.shape[0]
    vocab_local = head_rows.shape[0]
    rows = examples * length
    local_heads = HEADS // group_count
    group_width = local_heads * HD
    flat_ids = token_ids.reshape(rows)
    relative = flat_ids - group_index * width
    inside = (relative >= 0) & (relative < width)
    picked = jnp.where(
        inside[:, None], embedding[jnp.clip(relative, 0, width - 1)].astype(jnp.float32), 0.0
    )
    shape_low = jax.ShapeDtypeStruct((rows, D), jnp.bfloat16)
    shape_wide = jax.ShapeDtypeStruct((rows, D), jnp.float32)
    start_rows, normed_attn, normed_ffn = line_call(
        functools.partial(start_kernel, group_count),
        "start_rows",
        0,
        [shape_low] * 3,
        line_scratch(rows, D),
        [picked.astype(jnp.bfloat16), ln_gain, ln_bias],
    )
    leading_example = lax.axis_index("dp") * examples
    prompts = lax.dynamic_slice_in_dim(prompt_len, leading_example, examples)
    totals = lax.dynamic_slice_in_dim(example_len, leading_example, examples)
    position = jnp.arange(length)
    keep = (position[None, :] >= prompts[:, None] - 1) & (position[None, :] < totals[:, None] - 1)
    count = jnp.sum(example_len - prompt_len).astype(jnp.float32)
    row_weight = keep.reshape(rows).astype(jnp.float32) / count
    target = jnp.roll(token_ids, -1, axis=1).reshape(rows)
    inner = jnp.dot(
        normed_attn,
        jnp.concatenate([adapters[0], adapters[1], adapters[2]], 1),
        preferred_element_type=jnp.float32,
    ).astype(jnp.bfloat16)
    base = jnp.dot(normed_attn, w_qkv, preferred_element_type=jnp.float32).reshape(
        rows, local_heads, 3, HD
    )
    adapter_rows = [
        lax.dynamic_slice_in_dim(
            adapters[3 + selector_index], group_index * group_width, group_width, 0
        )
        for selector_index in range(3)
    ]
    pre_parts = []
    for selector_index in range(3):
        extra = jnp.einsum(
            "lr,dr->ld",
            inner[:, selector_index * R : (selector_index + 1) * R],
            adapter_rows[selector_index],
            preferred_element_type=jnp.float32,
        )
        pre_parts.append(base[:, :, selector_index] + extra.reshape(rows, local_heads, HD))
    cosine, sine = rope_tables(length)
    queries = rotate(pre_parts[0].reshape(examples, length, local_heads, HD), cosine, sine).astype(
        jnp.bfloat16
    )
    key_rows = rotate(pre_parts[1].reshape(examples, length, local_heads, HD), cosine, sine).astype(
        jnp.bfloat16
    )
    value_rows = pre_parts[2].reshape(examples, length, local_heads, HD).astype(jnp.bfloat16)
    sample = 0
    context_here, spread_local = attend(queries[sample], key_rows[sample], value_rows[sample])
    spreads = [spread_local]
    context = context_here.reshape(rows, group_width)
    out_rows = lax.dynamic_slice_in_dim(adapters[6], group_index * group_width, group_width, 0)
    inner_out = jnp.dot(context, out_rows, preferred_element_type=jnp.float32).astype(jnp.bfloat16)
    hidden = jax.nn.gelu(
        jnp.dot(normed_ffn, w_in, preferred_element_type=jnp.float32) + b_in, approximate=False
    ).astype(jnp.bfloat16)
    partial_value = (
        jnp.dot(context, w_out, preferred_element_type=jnp.float32)
        + jnp.einsum("lr,dr->ld", inner_out, adapters[7], preferred_element_type=jnp.float32)
        + jnp.dot(hidden, w_down, preferred_element_type=jnp.float32)
    )
    resid, final_rows = line_call(
        functools.partial(resid_kernel, group_count),
        "resid_rows",
        1,
        [shape_wide, shape_low],
        line_scratch(rows, D),
        [partial_value.astype(jnp.bfloat16), start_rows, ln_gain, ln_bias],
    )
    goal = target - group_index * vocab_local
    near = (goal >= 0) & (goal < vocab_local)
    hits = jnp.where(near[:, None], head_rows[jnp.clip(goal, 0, vocab_local - 1)], 0.0).astype(
        jnp.bfloat16
    )
    raw_grad, stats = loss_call(final_rows, head_rows, hits)
    branch_grad, losses = line_call(
        functools.partial(branch_kernel, group_count),
        "branch_rows",
        2,
        [shape_low, jax.ShapeDtypeStruct((1, rows), jnp.float32)],
        line_scratch(rows, D)
        + [
            pltpu.VMEM((rows, D), jnp.bfloat16),
            pltpu.VMEM((8, rows), jnp.float32),
            pltpu.VMEM((group_count, 8, rows), jnp.float32),
            pltpu.VMEM((rows, 128), jnp.float32),
            pltpu.SemaphoreType.DMA((group_count,)),
            pltpu.SemaphoreType.DMA((group_count,)),
        ],
        [raw_grad, hits, stats, row_weight.reshape(1, rows), resid, ln_gain],
    )
    inner_out_grad = jnp.dot(branch_grad, adapters[7], preferred_element_type=jnp.float32).astype(
        jnp.bfloat16
    )
    grad_out_b = jnp.einsum("ld,lr->dr", branch_grad, inner_out, preferred_element_type=jnp.float32)
    grad_out_a = jnp.einsum(
        "ld,lr->dr", context, inner_out_grad, preferred_element_type=jnp.float32
    )
    context_grad = jnp.einsum(
        "ld,ed->le", branch_grad, w_out, preferred_element_type=jnp.float32
    ) + jnp.einsum("lr,dr->ld", inner_out_grad, out_rows, preferred_element_type=jnp.float32)
    context_grad = context_grad.astype(jnp.bfloat16).reshape(examples, length, local_heads, HD)
    sample = 0
    query_grad, key_grad, value_grad = attend_back(
        queries[sample], key_rows[sample], value_rows[sample], spreads[sample], context_grad[sample]
    )
    query_parts = [rotate_back(query_grad, cosine, sine)]
    key_parts = [rotate_back(key_grad, cosine, sine)]
    value_parts = [value_grad]
    pre_grads = [
        parts[0].reshape(rows, group_width).astype(jnp.bfloat16)
        for parts in (query_parts, key_parts, value_parts)
    ]
    complete_gradients = []
    local_grads = []
    for selector_index in range(3):
        projected_values = jnp.einsum(
            "ld,le->de", normed_attn, pre_grads[selector_index], preferred_element_type=jnp.float32
        )
        complete_gradients.append(
            jnp.dot(
                projected_values,
                adapter_rows[selector_index].astype(jnp.float32),
                precision=HIGH_PRECISION,
            )
        )
        local_grads.append(
            jnp.einsum(
                "ld,lr->dr",
                pre_grads[selector_index],
                inner[:, selector_index * R : (selector_index + 1) * R],
                preferred_element_type=jnp.float32,
            )
        )
    local_grads.append(grad_out_a)
    mean_loss, grad_norm, new_first, new_second, new_master = fold_call(
        [*complete_gradients, grad_out_b],
        local_grads,
        losses,
        master,
        first_moment,
        second_moment,
        eigen_bases,
    )
    return (mean_loss.reshape(()), grad_norm.reshape(()), new_first, new_second, new_master)


def solution(mesh):
    placed = (
        P("dp", None),
        P(),
        P(),
        P("mp", None),
        P(None, "mp"),
        P("mp", None),
        P(None, "mp"),
        P("mp"),
        P("mp", None),
        P("dp", "mp"),
        P(),
        P(),
        P(None, ("dp", "mp"), None),
        P(None, ("dp", "mp"), None),
        P(None, ("dp", "mp"), None),
        P(),
    )
    return jax.shard_map(
        per_device,
        mesh=mesh,
        in_specs=placed,
        out_specs=(
            P(),
            P(),
            P(None, ("dp", "mp"), None),
            P(None, ("dp", "mp"), None),
            P(None, ("dp", "mp"), None),
        ),
        check_vma=False,
    )
```

```python
import functools

import jax
import jax.numpy as jnp
from jax import lax
from jax.experimental import pallas as pl
from jax.experimental.pallas import tpu as pltpu
from jax.sharding import PartitionSpec as P

MESH = pl.DeviceIdType.MESH
VMEM_LIMIT = 60 * 1024 * 1024

D = 1024
HEADS = 16
R = 128
ADAM_STEP = 10
HD = 64
ROT = 16


HIGH_PRECISION = lax.Precision.HIGHEST
NORM_EPS = 1e-05
ROPE_BASE = 10000.0
CLIP_LIMIT = 0.01
LEARN_RATE = 0.02
BETA_FIRST = 0.9
BETA_SECOND = 0.999
ADAM_EPS = 1e-08
DECAY_RATE = 0.01


def layer_norm(values, gain, shift):
    centre = values - jnp.mean(values, -1, keepdims=True)
    spread = jnp.mean(centre * centre, -1, keepdims=True)
    return centre * lax.rsqrt(spread + NORM_EPS) * gain + shift


def rope_tables(length):
    half = ROT // 2
    freqs = ROPE_BASE ** (-2.0 * jnp.arange(half, dtype=jnp.float32) / ROT)
    angles = jnp.arange(length, dtype=jnp.float32)[:, None] * freqs[None, :]
    return (jnp.cos(angles)[:, None, :], jnp.sin(angles)[:, None, :])


def rotate(field, cosine, sine):
    half = ROT // 2
    first = field[..., :half]
    second = field[..., half:ROT]
    return jnp.concatenate(
        [first * cosine - second * sine, second * cosine + first * sine, field[..., ROT:]], -1
    )


def rotate_back(upstream, cosine, sine):
    half = ROT // 2
    first = upstream[..., :half]
    second = upstream[..., half:ROT]
    return jnp.concatenate(
        [first * cosine + second * sine, second * cosine - first * sine, upstream[..., ROT:]], -1
    )


def masked_scores(queries, key_rows, start_row, stop_row):
    scores = jnp.einsum(
        "qhd,khd->hqk",
        queries[start_row:stop_row],
        key_rows[:stop_row],
        preferred_element_type=jnp.float32,
    ) * HD ** (-0.5)
    query_pos = start_row + jnp.arange(stop_row - start_row)[:, None]
    causal = jnp.arange(stop_row)[None, :] <= query_pos
    return jnp.where(causal[None], scores, -1e30)


def attend(queries, key_rows, value_rows):
    length = queries.shape[0]
    row_block = min(512, length)
    outputs = []
    spreads = []
    for start_row in range(0, length, row_block):
        stop_row = start_row + row_block
        scores = masked_scores(queries, key_rows, start_row, stop_row)
        top_score = jnp.max(scores, -1, keepdims=True)
        weights = jnp.exp(scores - top_score)
        row_total = jnp.sum(weights, -1, keepdims=True)
        probs = (weights / row_total).astype(jnp.bfloat16)
        outputs.append(
            jnp.einsum(
                "hqk,khd->qhd", probs, value_rows[:stop_row], preferred_element_type=jnp.float32
            )
        )
        spreads.append((top_score + jnp.log(row_total))[..., 0])
    return (jnp.concatenate(outputs, 0).astype(jnp.bfloat16), jnp.concatenate(spreads, 1))


def attend_back(queries, key_rows, value_rows, spreads, upstream):
    length = queries.shape[0]
    row_block = min(512, length)
    scaling = HD ** (-0.5)
    query_grads = []
    key_grad = jnp.zeros(key_rows.shape, jnp.float32)
    value_grad = jnp.zeros(value_rows.shape, jnp.float32)
    for start_row in range(0, length, row_block):
        stop_row = start_row + row_block
        scores = masked_scores(queries, key_rows, start_row, stop_row)
        probs = jnp.exp(scores - spreads[:, start_row:stop_row, None])
        grad_here = upstream[start_row:stop_row]
        prob_grad = jnp.einsum(
            "qhd,khd->hqk", grad_here, value_rows[:stop_row], preferred_element_type=jnp.float32
        )
        inner_sum = jnp.sum(probs * prob_grad, -1, keepdims=True)
        score_grad = (probs * (prob_grad - inner_sum)).astype(jnp.bfloat16)
        query_grads.append(
            jnp.einsum(
                "hqk,khd->qhd", score_grad, key_rows[:stop_row], preferred_element_type=jnp.float32
            )
            * scaling
        )
        key_grad = key_grad.at[:stop_row].add(
            jnp.einsum(
                "hqk,qhd->khd",
                score_grad,
                queries[start_row:stop_row],
                preferred_element_type=jnp.float32,
            )
            * scaling
        )
        value_grad = value_grad.at[:stop_row].add(
            jnp.einsum(
                "hqk,qhd->khd",
                probs.astype(jnp.bfloat16),
                grad_here,
                preferred_element_type=jnp.float32,
            )
        )
    return (jnp.concatenate(query_grads, 0), key_grad, value_grad)


def line_chunk(index, size):
    return pl.ds(pl.multiple_of(index * size, size), size)


def greet_line(me, count):
    barrier = pltpu.get_barrier_semaphore()

    @pl.when(me > 0)
    def _():
        pl.semaphore_signal(
            barrier, inc=1, device_id={"mp": jnp.maximum(me - 1, 0)}, device_id_type=MESH
        )

    @pl.when(me < count - 1)
    def _():
        pl.semaphore_signal(
            barrier, inc=1, device_id={"mp": jnp.minimum(me + 1, count - 1)}, device_id_type=MESH
        )

    peers = jnp.where(me > 0, 1, 0) + jnp.where(me < count - 1, 1, 0)
    pl.semaphore_wait(barrier, peers)


def greet_peers(me, count):
    barrier = pltpu.get_barrier_semaphore()
    for offset in range(1, count):
        pl.semaphore_signal(
            barrier, inc=1, device_id={"mp": lax.rem(me + offset, count)}, device_id_type=MESH
        )
    pl.semaphore_wait(barrier, count - 1)


def line_sum(count, chunk, own, wires, sems, prepare, emit, greet=True, follow=None):
    me = lax.axis_index("mp")
    from_low, from_high, to_high, to_low = wires
    up_send, up_recv, down_send, down_recv = sems
    length = own.shape[0]
    chunks = length // chunk
    above = jnp.minimum(me + 1, count - 1)
    below = jnp.maximum(me - 1, 0)

    def up_copy(index):
        rows = line_chunk(index, chunk)
        return pltpu.make_async_remote_copy(
            src_ref=to_high.at[rows],
            dst_ref=from_low.at[rows],
            send_sem=up_send.at[index],
            recv_sem=up_recv.at[index],
            device_id={"mp": above},
            device_id_type=MESH,
        )

    def down_copy(index):
        rows = line_chunk(index, chunk)
        return pltpu.make_async_remote_copy(
            src_ref=to_low.at[rows],
            dst_ref=from_high.at[rows],
            send_sem=down_send.at[index],
            recv_sem=down_recv.at[index],
            device_id={"mp": below},
            device_id_type=MESH,
        )

    if greet:
        greet_line(me, count)

    @pl.when(me == 0)
    def _():
        from_low[...] = jnp.zeros_like(from_low)

    @pl.when(me == count - 1)
    def _():
        from_high[...] = jnp.zeros_like(from_high)

    def step(at, carry):
        if prepare is not None:

            @pl.when(at < chunks)
            def _():
                prepare(at)

        up = at - LINE_LAG * me

        @pl.when((up >= 0) & (up < chunks))
        def _():
            rows = line_chunk(up, chunk)

            @pl.when(me > 0)
            def _():
                up_copy(up).wait_recv()

            @pl.when(me < count - 1)
            def _():
                to_high[rows, :] = (
                    from_low[rows, :].astype(jnp.float32) + own[rows, :].astype(jnp.float32)
                ).astype(jnp.bfloat16)
                up_copy(up).start()

        down = at - LINE_LAG * (count - 1 - me)

        @pl.when((down >= 0) & (down < chunks))
        def _():
            rows = line_chunk(down, chunk)

            @pl.when(me < count - 1)
            def _():
                down_copy(down).wait_recv()

            @pl.when(me > 0)
            def _():
                to_low[rows, :] = (
                    from_high[rows, :].astype(jnp.float32) + own[rows, :].astype(jnp.float32)
                ).astype(jnp.bfloat16)
                down_copy(down).start()

        ready = at - LINE_LAG * jnp.maximum(me, count - 1 - me)

        @pl.when((ready >= 0) & (ready < chunks))
        def _():
            rows = line_chunk(ready, chunk)
            total = (
                from_low[rows, :].astype(jnp.float32)
                + own[rows, :].astype(jnp.float32)
                + from_high[rows, :].astype(jnp.float32)
            )
            emit(rows, total)
            if follow is not None:
                follow(ready)

        return carry

    lax.fori_loop(0, chunks + LINE_LAG * (count - 1), step, 0)

    def drain(index, carry):
        @pl.when(me < count - 1)
        def _():
            up_copy(index).wait_send()

        @pl.when(me > 0)
        def _():
            down_copy(index).wait_send()

        return carry

    lax.fori_loop(0, chunks, drain, 0)


PICK_GROUP = 32
PICK_ALIGN = 8


def pick_kernel(spots, places, table, out, held, sems):
    rows = out.shape[0]
    vocab = table.shape[0]
    span = PICK_GROUP * PICK_ALIGN

    def start(group, carry):
        def one(token, carry):
            at = group * PICK_GROUP + token
            row = jnp.clip(spots[at], 0, vocab - 1)
            base = pl.multiple_of(row - lax.rem(row, PICK_ALIGN), PICK_ALIGN)
            pltpu.make_async_copy(
                table.at[pl.ds(base, PICK_ALIGN)],
                held.at[pl.ds(pl.multiple_of(at * PICK_ALIGN, PICK_ALIGN), PICK_ALIGN)],
                sems.at[group],
            ).start()
            return carry

        return lax.fori_loop(0, PICK_GROUP, one, carry, unroll=8)

    lax.fori_loop(0, rows // PICK_GROUP, start, 0)

    def choose(group, carry):
        block = held.at[pl.ds(pl.multiple_of(group * span, span), span)]
        pltpu.make_async_copy(table.at[pl.ds(0, span)], block, sems.at[group]).wait()
        here = line_chunk(group, PICK_GROUP)
        place = places[here, :]
        inside = (place >= 0) & (place < vocab)
        token = lax.broadcasted_iota(jnp.int32, (PICK_GROUP, 1), 0)
        wanted = jnp.where(
            inside, token * PICK_ALIGN + lax.rem(jnp.clip(place, 0, vocab - 1), PICK_ALIGN), -1
        )
        column = lax.broadcasted_iota(jnp.int32, (PICK_GROUP, span), 1)
        chosen = jnp.where(column == wanted, 1.0, 0.0).astype(jnp.bfloat16)
        out[here, :] = jnp.dot(
            chosen, block[...], preferred_element_type=jnp.float32
        ).astype(jnp.bfloat16)
        return carry

    lax.fori_loop(0, rows // PICK_GROUP, choose, 0)


def pick_call(spots, table, name):
    rows = spots.shape[0]
    width = table.shape[1]
    return pl.pallas_call(
        pick_kernel,
        name=name,
        in_specs=[
            pl.BlockSpec(memory_space=pltpu.SMEM),
            pl.BlockSpec(memory_space=pltpu.VMEM),
            pl.BlockSpec(memory_space=pl.ANY),
        ],
        out_specs=pl.BlockSpec(memory_space=pltpu.VMEM),
        out_shape=jax.ShapeDtypeStruct((rows, width), jnp.bfloat16),
        scratch_shapes=[
            pltpu.VMEM((rows * PICK_ALIGN, width), jnp.bfloat16),
            pltpu.SemaphoreType.DMA((rows // PICK_GROUP,)),
        ],
        compiler_params=pltpu.CompilerParams(vmem_limit_bytes=VMEM_LIMIT),
        cost_estimate=pl.CostEstimate(
            flops=2 * rows * PICK_GROUP * PICK_ALIGN * width,
            bytes_accessed=2 * rows * PICK_ALIGN * width,
            transcendentals=0,
        ),
    )(spots, spots.reshape(rows, 1), table)


LINE_CHUNK = 32
LINE_LAG = 3
WORK_ROWS = 256


def line_scratch(length, width):
    chunks = length // LINE_CHUNK
    return [pltpu.VMEM((length, width), jnp.bfloat16)] * 4 + [
        pltpu.SemaphoreType.DMA((chunks,))
    ] * 4


def line_call(kernel, name, collective_id, outs, scratch, operands, flops=0, spaces=()):
    size = sum(o.size * o.dtype.itemsize for o in operands) + sum(
        o.size * o.dtype.itemsize for o in outs
    )
    vmem = pl.BlockSpec(memory_space=pltpu.VMEM)
    return pl.pallas_call(
        kernel,
        name=name,
        out_shape=outs,
        in_specs=[vmem] * (len(operands) - len(spaces))
        + [pl.BlockSpec(memory_space=space) for space in spaces],
        out_specs=[vmem] * len(outs),
        scratch_shapes=scratch,
        compiler_params=pltpu.CompilerParams(
            collective_id=collective_id, has_side_effects=True, vmem_limit_bytes=VMEM_LIMIT
        ),
        cost_estimate=pl.CostEstimate(
            flops=flops, bytes_accessed=size + 100_000_000, transcendentals=0
        ),
    )(*operands)


def start_kernel(
    count,
    part,
    gain,
    shift,
    bias,
    w_qkv,
    w_in,
    w_down,
    rows_out,
    attn_out,
    base_out,
    ffn_out,
    *scratch,
):
    normed, held_qkv, held_in, held_down, sems = scratch[8:]
    loads = [
        pltpu.make_async_copy(src, dst, sems.at[slot])
        for slot, (src, dst) in enumerate(
            ((w_qkv, held_qkv), (w_in, held_in), (w_down, held_down))
        )
    ]
    for load in loads:
        load.start()

    def emit(rows, total):
        rows_out[rows, :] = total.astype(jnp.bfloat16)
        centre = total - jnp.mean(total, -1, keepdims=True)
        spread = jnp.mean(centre * centre, -1, keepdims=True)
        base = centre * lax.rsqrt(spread + NORM_EPS)
        attn_out[rows, :] = (base * gain[0:1, :] + shift[0:1, :]).astype(jnp.bfloat16)
        normed[rows, :] = (base * gain[1:2, :] + shift[1:2, :]).astype(jnp.bfloat16)

    per = WORK_ROWS // LINE_CHUNK

    def follow(ready):
        @pl.when(ready == per - 1)
        def _():
            for load in loads:
                load.wait()

        @pl.when(lax.rem(ready, per) == per - 1)
        def _():
            rows = line_chunk(ready // per, WORK_ROWS)
            base_out[rows, :] = jnp.dot(
                attn_out[rows, :], held_qkv[...], preferred_element_type=jnp.float32
            )
            pre = (
                jnp.dot(normed[rows, :], held_in[...], preferred_element_type=jnp.float32)
                + bias[...]
            )
            hidden = (0.5 * pre * (1.0 + lax.erf(pre * 0.5**0.5))).astype(jnp.bfloat16)
            ffn_out[rows, :] = jnp.dot(
                hidden, held_down[...], preferred_element_type=jnp.float32
            ).astype(jnp.bfloat16)

    line_sum(count, LINE_CHUNK, part, scratch[:4], scratch[4:8], None, emit, follow=follow)


def resid_kernel(count, part, start, gain, shift, resid_out, final_out, *scratch):
    def emit(rows, total):
        resid = start[rows, :].astype(jnp.float32) + total
        resid_out[rows, :] = resid
        normed = layer_norm(resid, gain[2:3, :], shift[2:3, :])
        final_out[rows, :] = normed.astype(jnp.bfloat16)

    line_sum(count, LINE_CHUNK, part, scratch[:4], scratch[4:], None, emit)


def branch_kernel(
    count, raw, hits, stats, resid, gain, prompts, totals, out, loss_out, *scratch
):
    own, note_send, note_recv, scales, note_out, note_in = scratch[8:]
    me = lax.axis_index("mp")
    rows_all = raw.shape[0]
    greet_peers(me, count)
    note_send[...] = stats[...].T[0:8, :]
    copies = []
    for offset in range(1, count):
        copy = pltpu.make_async_remote_copy(
            src_ref=note_send,
            dst_ref=note_recv.at[offset],
            send_sem=note_out.at[offset],
            recv_sem=note_in.at[offset],
            device_id={"mp": lax.rem(me + offset, count)},
            device_id_type=MESH,
        )
        copy.start()
        copies.append(copy)
    mine = note_send[...]
    for copy in copies:
        copy.wait_recv()
    others = [mine] + [note_recv[offset] for offset in range(1, count)]
    top = functools.reduce(jnp.maximum, [part[0:1, :] for part in others])
    total = sum(part[1:2, :] * jnp.exp(part[0:1, :] - top) for part in others)
    found = sum(part[2:3, :] for part in others)
    spread_row = top + jnp.log(total)
    amount = sum(totals[e] - prompts[e] for e in range(prompts.shape[0]))
    example = lax.axis_index("dp")
    position = lax.broadcasted_iota(jnp.int32, (1, rows_all), 1)
    keep = (position >= prompts[example] - 1) & (position < totals[example] - 1)
    share = jnp.where(keep, 1.0 / jnp.broadcast_to(amount, (1, rows_all)).astype(jnp.float32), 0.0)
    loss_out[...] = (spread_row - found) * share
    factor = jnp.exp(mine[0:1, :] - spread_row) * share
    pair = jnp.concatenate([factor, share, jnp.zeros((126, rows_all), jnp.float32)], 0)
    scales[...] = pair.T

    def prepare(at):
        rows = line_chunk(at, LINE_CHUNK)
        scale = scales[rows, :]
        own[rows, :] = (
            raw[rows, :] * scale[:, 0:1] - hits[rows, :].astype(jnp.float32) * scale[:, 1:2]
        ).astype(jnp.bfloat16)

    def emit(rows, total):
        values = resid[rows, :]
        centre = values - jnp.mean(values, -1, keepdims=True)
        spread = jnp.mean(centre * centre, -1, keepdims=True)
        inverse = lax.rsqrt(spread + NORM_EPS)
        normed = centre * inverse
        up = total * gain[2:3, :]
        out[rows, :] = (
            inverse
            * (
                up
                - jnp.mean(up, -1, keepdims=True)
                - normed * jnp.mean(up * normed, -1, keepdims=True)
            )
        ).astype(jnp.bfloat16)

    line_sum(count, LINE_CHUNK, own, scratch[:4], scratch[4:8], prepare, emit, greet=False)
    for copy in copies:
        copy.wait_send()


def loss_kernel(vocab, tile, values, ahead, behind, hits, acc, stats, logits, probs, tops, sums):
    at = pl.program_id(0)
    tiles = pl.num_programs(0) - 1
    rows_all = values.shape[0]

    @pl.when(at == 0)
    def _():
        acc[...] = jnp.zeros_like(acc)
        tops[...] = jnp.full_like(tops, -1e29)
        sums[...] = jnp.zeros_like(sums)
        logits[...] = jnp.full_like(logits, -1e30)

    tail = vocab % tile
    if tail:

        @pl.when(at >= tiles - 1)
        def _():
            ahead[tail:, :] = jnp.zeros((tile - tail, ahead.shape[1]), ahead.dtype)

        @pl.when(at >= tiles)
        def _():
            behind[tail:, :] = jnp.zeros((tile - tail, behind.shape[1]), behind.dtype)

    ids = (at - 1) * tile + lax.broadcasted_iota(jnp.int32, (1, tile), 1)
    scores = logits[...] + jnp.where(ids < vocab, 0.0, -1e30)
    old = tops[:, 0:1]
    new = jnp.maximum(old, jnp.max(scores, -1, keepdims=True))
    weights = jnp.exp(scores - new)
    shrink = jnp.exp(old - new)
    sums[...] = sums[...] * shrink + jnp.sum(weights, -1, keepdims=True)
    tops[...] = jnp.broadcast_to(new, tops.shape)
    acc[...] = acc[...] * shrink
    probs[...] = weights.astype(jnp.bfloat16)
    logits[...] = lax.dot_general(
        values[...], ahead[...], (((1,), (1,)), ((), ())), preferred_element_type=jnp.float32
    )
    acc[...] += jnp.dot(probs[...], behind[...], preferred_element_type=jnp.float32)

    @pl.when(at == tiles)
    def _():
        found = jnp.sum(
            values[...].astype(jnp.float32) * hits[...].astype(jnp.float32), -1, keepdims=True
        )
        column = lax.broadcasted_iota(jnp.int32, (rows_all, 128), 1)
        stats[...] = jnp.where(
            column == 0, tops[...], jnp.where(column == 1, sums[...], found)
        )


LOSS_TILE = 512


def loss_call(values, head_rows, hits):
    rows, width = values.shape
    vocab = head_rows.shape[0]
    tile = LOSS_TILE
    tiles = pl.cdiv(vocab, tile)
    whole = pl.BlockSpec((rows, width), lambda j: (0, 0))
    return pl.pallas_call(
        functools.partial(loss_kernel, vocab, tile),
        name="loss",
        grid=(tiles + 1,),
        in_specs=[
            whole,
            pl.BlockSpec((tile, width), lambda j: (jnp.minimum(j, tiles - 1), 0)),
            pl.BlockSpec((tile, width), lambda j: (jnp.maximum(j - 1, 0), 0)),
            whole,
        ],
        out_specs=[whole, pl.BlockSpec((rows, 128), lambda j: (0, 0))],
        out_shape=[
            jax.ShapeDtypeStruct((rows, width), jnp.float32),
            jax.ShapeDtypeStruct((rows, 128), jnp.float32),
        ],
        scratch_shapes=[
            pltpu.VMEM((rows, tile), jnp.float32),
            pltpu.VMEM((rows, tile), jnp.bfloat16),
            pltpu.VMEM((rows, 128), jnp.float32),
            pltpu.VMEM((rows, 128), jnp.float32),
        ],
        compiler_params=pltpu.CompilerParams(vmem_limit_bytes=VMEM_LIMIT),
        cost_estimate=pl.CostEstimate(
            flops=4 * rows * width * vocab,
            bytes_accessed=4 * width * vocab,
            transcendentals=rows * vocab,
        ),
    )(values, head_rows, head_rows, hits)


def fold_kernel(splits, count, *refs):
    fulls = refs[0:4]
    groups = refs[4:8]
    losses, master, first, second, bases = refs[8:13]
    loss_out, norm_out, first_out, second_out, master_out = refs[13:18]
    scratch = refs[18:]
    sends = scratch[0:splits]
    recvs = scratch[splits : 2 * splits]
    keeps = scratch[2 * splits : 3 * splits]
    (line_send, line_recv, turn_send, turn_recv, note_send, note_recv, tell_send, tell_recv) = scratch[
        3 * splits : 3 * splits + 8
    ]
    (half_out, half_in, line_out, line_in, turn_out, turn_in, note_out, note_in, tell_out, tell_in) = (
        scratch[3 * splits + 8 :]
    )
    shards = 2**splits
    me = lax.axis_index("dp")
    lane = lax.axis_index("mp")
    full_rows = fulls[0].shape[0] // shards
    group_rows = groups[0].shape[0] // shards
    own_rows = full_rows // count
    bits = [(me // 2**k) % 2 for k in range(splits)]
    mates = [me + 2**k * (1 - 2 * bits[k]) for k in range(splits)]
    peers = [lax.rem(lane + offset, count) for offset in range(count)]
    spot = lane * shards + me
    goal = (spot // count, lax.rem(spot, count))
    place = me * count + lane
    origin = (lax.rem(place, shards), place // shards)
    moved = spot != place

    barrier = pltpu.get_barrier_semaphore()
    for mate in mates:
        pl.semaphore_signal(barrier, inc=1, device_id={"dp": mate, "mp": lane}, device_id_type=MESH)
    for peer in peers[1:]:
        pl.semaphore_signal(barrier, inc=1, device_id={"dp": me, "mp": peer}, device_id_type=MESH)

    @pl.when(moved)
    def _():
        for device in (goal, origin):
            pl.semaphore_signal(
                barrier, inc=1, device_id={"dp": device[0], "mp": device[1]}, device_id_type=MESH
            )

    pl.semaphore_wait(barrier, splits + count - 1 + jnp.where(moved, 2, 0))

    def remote(src, dst, out_sem, in_sem, device):
        return pltpu.make_async_remote_copy(
            src_ref=src,
            dst_ref=dst,
            send_sem=out_sem,
            recv_sem=in_sem,
            device_id={"dp": device[0], "mp": device[1]},
            device_id_type=MESH,
        )

    def piece(index):
        whole = pl.ds(pl.multiple_of(index * full_rows, full_rows), full_rows)
        part = pl.ds(pl.multiple_of(index * group_rows, group_rows), group_rows)
        return jnp.concatenate(
            [ref[whole, :] for ref in fulls] + [ref[part, :] for ref in groups], 0
        )

    started = []
    current = piece
    for k in range(splits):
        half = shards >> (k + 1)
        for i in range(half):
            sends[k][i] = current(2 * i + 1 - bits[k]).astype(jnp.bfloat16)
        copy = remote(sends[k], recvs[k], half_out.at[k], half_in.at[k], (mates[k], lane))
        copy.start()
        started.append(copy)
        for i in range(half):
            keeps[k][i] = current(2 * i + bits[k])
        copy.wait_recv()
        current = functools.partial(
            lambda kept, came, i: kept[i] + came[i].astype(jnp.float32), keeps[k], recvs[k]
        )
    final = keeps[splits - 1]
    final[0] = current(0)

    def chosen(peer):
        return jnp.concatenate(
            [
                final[
                    0,
                    pl.ds(pl.multiple_of(a * full_rows + peer * own_rows, own_rows), own_rows),
                    :,
                ]
                for a in range(4)
            ],
            0,
        )

    turn_send[...] = final[0, 4 * full_rows :, :].astype(jnp.bfloat16)
    turn = remote(turn_send, turn_recv, turn_out, turn_in, goal)

    @pl.when(moved)
    def _():
        turn.start()

    for offset in range(1, count):
        line_send[offset] = chosen(peers[offset]).astype(jnp.bfloat16)
        copy = remote(
            line_send.at[offset],
            line_recv.at[offset],
            line_out.at[offset],
            line_in.at[offset],
            (me, peers[offset]),
        )
        copy.start()
        started.append(copy)
    total = chosen(lane)

    @pl.when(moved)
    def _():
        turn.wait()

    @pl.when(jnp.logical_not(moved))
    def _():
        turn_recv[...] = turn_send[...]

    for copy in started[splits:]:
        copy.wait_recv()
    for offset in range(1, count):
        total = total + line_recv[offset].astype(jnp.float32)
    part = turn_recv[...].astype(jnp.float32)

    column = lax.broadcasted_iota(jnp.int32, (8, 128), 1)
    row = lax.broadcasted_iota(jnp.int32, (8, 128), 0)
    squares = jnp.sum(total * total) + jnp.sum(part * part)
    spot_norm = (row == 0) & (column == 0)
    spot_loss = (row == 0) & (column == 1)
    note = jnp.where(spot_norm, squares, 0.0) + jnp.where(spot_loss, jnp.sum(losses[...]), 0.0)

    def rows_of(index):
        source, slot = (total, (0, 1, 2, 7).index(index)) if index in (0, 1, 2, 7) else (
            part,
            index - 3,
        )
        return source[slot * own_rows : (slot + 1) * own_rows, :]

    turned = [
        jnp.dot(
            rows_of(m), bases[m], precision=HIGH_PRECISION, preferred_element_type=jnp.float32
        )
        for m in range(8)
    ]
    for k in range(splits):
        note_send[k] = note
        copy = remote(
            note_send.at[k], note_recv.at[k], note_out.at[k], note_in.at[k], (mates[k], lane)
        )
        copy.start()
        started.append(copy)
        copy.wait_recv()
        note = note + note_recv[k]
    tell_send[...] = note
    tells = []
    for offset in range(1, count):
        copy = remote(
            tell_send,
            tell_recv.at[offset],
            tell_out.at[offset],
            tell_in.at[offset],
            (me, peers[offset]),
        )
        copy.start()
        tells.append(copy)
    for copy in tells:
        copy.wait_recv()
    everything = note
    for offset in range(1, count):
        everything = everything + tell_recv[offset]
    norm = jnp.sqrt(jnp.sum(jnp.where(spot_norm, everything, 0.0), keepdims=True))
    loss_out[...] = jnp.sum(jnp.where(spot_loss, note, 0.0), keepdims=True)
    norm_out[...] = norm
    factor = jnp.minimum(1.0, CLIP_LIMIT / norm)
    for m in range(8):
        rotated = turned[m] * factor
        new_first = BETA_FIRST * first[m] + (1.0 - BETA_FIRST) * rotated
        new_second = BETA_SECOND * second[m] + (1.0 - BETA_SECOND) * rotated * rotated
        first_out[m] = new_first
        second_out[m] = new_second
        normed = (
            new_first
            / (1.0 - BETA_FIRST**ADAM_STEP)
            / (jnp.sqrt(new_second / (1.0 - BETA_SECOND**ADAM_STEP)) + ADAM_EPS)
        )
        back = lax.dot_general(
            normed,
            bases[m],
            (((1,), (1,)), ((), ())),
            precision=HIGH_PRECISION,
            preferred_element_type=jnp.float32,
        )
        master_out[m] = master[m] - LEARN_RATE * (back + DECAY_RATE * master[m])
    for copy in started + tells:
        copy.wait_send()


def fold_call(fulls, groups, losses, master, first_moment, second_moment, bases):
    shards = lax.axis_size("dp")
    count = lax.axis_size("mp")
    splits = shards.bit_length() - 1
    width = fulls[0].shape[1]
    pile = 4 * (fulls[0].shape[0] + groups[0].shape[0]) // shards
    own = 4 * fulls[0].shape[0] // (shards * count)
    low = jnp.bfloat16
    halves = [shards >> (k + 1) for k in range(splits)]
    dma = pltpu.SemaphoreType.DMA
    scratch = (
        [pltpu.VMEM((half, pile, width), low) for half in halves] * 2
        + [pltpu.VMEM((half, pile, width), jnp.float32) for half in halves]
        + [pltpu.VMEM((count, own, width), low)] * 2
        + [pltpu.VMEM((4 * groups[0].shape[0] // shards, width), low)] * 2
        + [pltpu.VMEM((splits, 8, 128), jnp.float32)] * 2
        + [pltpu.VMEM((8, 128), jnp.float32), pltpu.VMEM((count, 8, 128), jnp.float32)]
        + [dma((splits,))] * 2
        + [dma((count,))] * 2
        + [dma(())] * 2
        + [dma((splits,))] * 2
        + [dma((count,))] * 2
    )
    scalar = jax.ShapeDtypeStruct((1, 1), jnp.float32)
    state = jax.ShapeDtypeStruct(master.shape, jnp.float32)
    return line_call(
        functools.partial(fold_kernel, splits, count),
        "fold",
        3,
        [scalar, scalar, state, state, state],
        scratch,
        [*fulls, *groups, losses, master, first_moment, second_moment, bases],
    )


def per_device(
    token_ids,
    prompt_len,
    example_len,
    embedding,
    w_qkv,
    w_out,
    w_in,
    b_in,
    w_down,
    unembed,
    ln_gain,
    ln_bias,
    master,
    first_moment,
    second_moment,
    eigen_bases,
):
    group_count = lax.axis_size("mp")
    group_index = lax.axis_index("mp")
    adapters = lax.all_gather(master.astype(jnp.bfloat16), ("dp", "mp"), axis=1, tiled=True)
    head_rows = lax.all_gather(unembed.T, "dp", axis=1, tiled=True)
    examples, length = token_ids.shape
    width = embedding.shape[0]
    vocab_local = head_rows.shape[0]
    rows = examples * length
    local_heads = HEADS // group_count
    group_width = local_heads * HD
    flat_ids = token_ids.reshape(rows)
    picked = pick_call(flat_ids - group_index * width, embedding, "pick_start")
    shape_low = jax.ShapeDtypeStruct((rows, D), jnp.bfloat16)
    shape_wide = jax.ShapeDtypeStruct((rows, D), jnp.float32)
    start_rows, normed_attn, base, ffn_part = line_call(
        functools.partial(start_kernel, group_count),
        "start_rows",
        0,
        [
            shape_low,
            shape_low,
            jax.ShapeDtypeStruct((rows, w_qkv.shape[1]), jnp.float32),
            shape_low,
        ],
        line_scratch(rows, D)
        + [
            pltpu.VMEM((rows, D), jnp.bfloat16),
            pltpu.VMEM(w_qkv.shape, jnp.bfloat16),
            pltpu.VMEM(w_in.shape, jnp.bfloat16),
            pltpu.VMEM(w_down.shape, jnp.bfloat16),
            pltpu.SemaphoreType.DMA((3,)),
        ],
        [picked, ln_gain, ln_bias, b_in.reshape(1, -1), w_qkv, w_in, w_down],
        spaces=(pl.ANY,) * 3,
    )
    target = jnp.roll(token_ids, -1, axis=1).reshape(rows)
    inner = jnp.dot(
        normed_attn,
        jnp.concatenate([adapters[0], adapters[1], adapters[2]], 1),
        preferred_element_type=jnp.float32,
    ).astype(jnp.bfloat16)
    base = base.reshape(rows, local_heads, 3, HD)
    adapter_rows = [
        lax.dynamic_slice_in_dim(
            adapters[3 + selector_index], group_index * group_width, group_width, 0
        )
        for selector_index in range(3)
    ]
    pre_parts = []
    for selector_index in range(3):
        extra = jnp.einsum(
            "lr,dr->ld",
            inner[:, selector_index * R : (selector_index + 1) * R],
            adapter_rows[selector_index],
            preferred_element_type=jnp.float32,
        )
        pre_parts.append(base[:, :, selector_index] + extra.reshape(rows, local_heads, HD))
    cosine, sine = rope_tables(length)
    queries = rotate(pre_parts[0].reshape(examples, length, local_heads, HD), cosine, sine).astype(
        jnp.bfloat16
    )
    key_rows = rotate(pre_parts[1].reshape(examples, length, local_heads, HD), cosine, sine).astype(
        jnp.bfloat16
    )
    value_rows = pre_parts[2].reshape(examples, length, local_heads, HD).astype(jnp.bfloat16)
    sample = 0
    context_here, spread_local = attend(queries[sample], key_rows[sample], value_rows[sample])
    spreads = [spread_local]
    context = context_here.reshape(rows, group_width)
    out_rows = lax.dynamic_slice_in_dim(adapters[6], group_index * group_width, group_width, 0)
    inner_out = jnp.dot(context, out_rows, preferred_element_type=jnp.float32).astype(jnp.bfloat16)
    partial_value = (
        jnp.dot(context, w_out, preferred_element_type=jnp.float32)
        + jnp.einsum("lr,dr->ld", inner_out, adapters[7], preferred_element_type=jnp.float32)
        + ffn_part.astype(jnp.float32)
    )
    resid, final_rows = line_call(
        functools.partial(resid_kernel, group_count),
        "resid_rows",
        1,
        [shape_wide, shape_low],
        line_scratch(rows, D),
        [partial_value.astype(jnp.bfloat16), start_rows, ln_gain, ln_bias],
    )
    goal = target - group_index * vocab_local
    hits = pick_call(goal, head_rows, "pick_target")
    raw_grad, stats = loss_call(final_rows, head_rows, hits)
    branch_grad, losses = line_call(
        functools.partial(branch_kernel, group_count),
        "branch_rows",
        2,
        [shape_low, jax.ShapeDtypeStruct((1, rows), jnp.float32)],
        line_scratch(rows, D)
        + [
            pltpu.VMEM((rows, D), jnp.bfloat16),
            pltpu.VMEM((8, rows), jnp.float32),
            pltpu.VMEM((group_count, 8, rows), jnp.float32),
            pltpu.VMEM((rows, 128), jnp.float32),
            pltpu.SemaphoreType.DMA((group_count,)),
            pltpu.SemaphoreType.DMA((group_count,)),
        ],
        [raw_grad, hits, stats, resid, ln_gain, prompt_len, example_len],
        spaces=(pltpu.SMEM,) * 2,
    )
    inner_out_grad = jnp.dot(branch_grad, adapters[7], preferred_element_type=jnp.float32).astype(
        jnp.bfloat16
    )
    grad_out_b = jnp.einsum("ld,lr->dr", branch_grad, inner_out, preferred_element_type=jnp.float32)
    grad_out_a = jnp.einsum(
        "ld,lr->dr", context, inner_out_grad, preferred_element_type=jnp.float32
    )
    context_grad = jnp.einsum(
        "ld,ed->le", branch_grad, w_out, preferred_element_type=jnp.float32
    ) + jnp.einsum("lr,dr->ld", inner_out_grad, out_rows, preferred_element_type=jnp.float32)
    context_grad = context_grad.astype(jnp.bfloat16).reshape(examples, length, local_heads, HD)
    sample = 0
    query_grad, key_grad, value_grad = attend_back(
        queries[sample], key_rows[sample], value_rows[sample], spreads[sample], context_grad[sample]
    )
    query_parts = [rotate_back(query_grad, cosine, sine)]
    key_parts = [rotate_back(key_grad, cosine, sine)]
    value_parts = [value_grad]
    pre_grads = [
        parts[0].reshape(rows, group_width).astype(jnp.bfloat16)
        for parts in (query_parts, key_parts, value_parts)
    ]
    complete_gradients = []
    local_grads = []
    for selector_index in range(3):
        projected_values = jnp.einsum(
            "ld,le->de", normed_attn, pre_grads[selector_index], preferred_element_type=jnp.float32
        )
        complete_gradients.append(
            jnp.dot(
                projected_values,
                adapter_rows[selector_index].astype(jnp.float32),
                precision=HIGH_PRECISION,
            )
        )
        local_grads.append(
            jnp.einsum(
                "ld,lr->dr",
                pre_grads[selector_index],
                inner[:, selector_index * R : (selector_index + 1) * R],
                preferred_element_type=jnp.float32,
            )
        )
    local_grads.append(grad_out_a)
    mean_loss, grad_norm, new_first, new_second, new_master = fold_call(
        [*complete_gradients, grad_out_b],
        local_grads,
        losses,
        master,
        first_moment,
        second_moment,
        eigen_bases,
    )
    return (mean_loss.reshape(()), grad_norm.reshape(()), new_first, new_second, new_master)


def solution(mesh):
    placed = (
        P("dp", None),
        P(),
        P(),
        P("mp", None),
        P(None, "mp"),
        P("mp", None),
        P(None, "mp"),
        P("mp"),
        P("mp", None),
        P("dp", "mp"),
        P(),
        P(),
        P(None, ("dp", "mp"), None),
        P(None, ("dp", "mp"), None),
        P(None, ("dp", "mp"), None),
        P(),
    )
    return jax.shard_map(
        per_device,
        mesh=mesh,
        in_specs=placed,
        out_specs=(
            P(),
            P(),
            P(None, ("dp", "mp"), None),
            P(None, ("dp", "mp"), None),
            P(None, ("dp", "mp"), None),
        ),
        check_vma=False,
    )
```

```python
import functools

import jax
import jax.numpy as jnp
from jax import lax
from jax.experimental import pallas as pl
from jax.experimental.pallas import tpu as pltpu
from jax.sharding import PartitionSpec as P

MESH = pl.DeviceIdType.MESH
VMEM_LIMIT = 60 * 1024 * 1024

D = 1024
HEADS = 16
R = 128
ADAM_STEP = 10
HD = 64
ROT = 16


HIGH_PRECISION = lax.Precision.HIGHEST
NORM_EPS = 1e-05
ROPE_BASE = 10000.0
CLIP_LIMIT = 0.01
LEARN_RATE = 0.02
BETA_FIRST = 0.9
BETA_SECOND = 0.999
ADAM_EPS = 1e-08
DECAY_RATE = 0.01


def layer_norm(values, gain, shift):
    centre = values - jnp.mean(values, -1, keepdims=True)
    spread = jnp.mean(centre * centre, -1, keepdims=True)
    return centre * lax.rsqrt(spread + NORM_EPS) * gain + shift


def rope_tables(length):
    half = ROT // 2
    freqs = ROPE_BASE ** (-2.0 * jnp.arange(half, dtype=jnp.float32) / ROT)
    angles = jnp.arange(length, dtype=jnp.float32)[:, None] * freqs[None, :]
    return (jnp.cos(angles)[:, None, :], jnp.sin(angles)[:, None, :])


def rotate(field, cosine, sine):
    half = ROT // 2
    first = field[..., :half]
    second = field[..., half:ROT]
    return jnp.concatenate(
        [first * cosine - second * sine, second * cosine + first * sine, field[..., ROT:]], -1
    )


def rotate_back(upstream, cosine, sine):
    half = ROT // 2
    first = upstream[..., :half]
    second = upstream[..., half:ROT]
    return jnp.concatenate(
        [first * cosine + second * sine, second * cosine - first * sine, upstream[..., ROT:]], -1
    )


def masked_scores(queries, key_rows, start_row, stop_row):
    scores = jnp.einsum(
        "qhd,khd->hqk",
        queries[start_row:stop_row],
        key_rows[:stop_row],
        preferred_element_type=jnp.float32,
    ) * HD ** (-0.5)
    query_pos = start_row + jnp.arange(stop_row - start_row)[:, None]
    causal = jnp.arange(stop_row)[None, :] <= query_pos
    return jnp.where(causal[None], scores, -1e30)


def attend(queries, key_rows, value_rows):
    length = queries.shape[0]
    row_block = min(512, length)
    outputs = []
    spreads = []
    for start_row in range(0, length, row_block):
        stop_row = start_row + row_block
        scores = masked_scores(queries, key_rows, start_row, stop_row)
        top_score = jnp.max(scores, -1, keepdims=True)
        weights = jnp.exp(scores - top_score)
        row_total = jnp.sum(weights, -1, keepdims=True)
        probs = (weights / row_total).astype(jnp.bfloat16)
        outputs.append(
            jnp.einsum(
                "hqk,khd->qhd", probs, value_rows[:stop_row], preferred_element_type=jnp.float32
            )
        )
        spreads.append((top_score + jnp.log(row_total))[..., 0])
    return (jnp.concatenate(outputs, 0).astype(jnp.bfloat16), jnp.concatenate(spreads, 1))


def attend_back(queries, key_rows, value_rows, spreads, upstream):
    length = queries.shape[0]
    row_block = min(512, length)
    scaling = HD ** (-0.5)
    query_grads = []
    key_grad = jnp.zeros(key_rows.shape, jnp.float32)
    value_grad = jnp.zeros(value_rows.shape, jnp.float32)
    for start_row in range(0, length, row_block):
        stop_row = start_row + row_block
        scores = masked_scores(queries, key_rows, start_row, stop_row)
        probs = jnp.exp(scores - spreads[:, start_row:stop_row, None])
        grad_here = upstream[start_row:stop_row]
        prob_grad = jnp.einsum(
            "qhd,khd->hqk", grad_here, value_rows[:stop_row], preferred_element_type=jnp.float32
        )
        inner_sum = jnp.sum(probs * prob_grad, -1, keepdims=True)
        score_grad = (probs * (prob_grad - inner_sum)).astype(jnp.bfloat16)
        query_grads.append(
            jnp.einsum(
                "hqk,khd->qhd", score_grad, key_rows[:stop_row], preferred_element_type=jnp.float32
            )
            * scaling
        )
        key_grad = key_grad.at[:stop_row].add(
            jnp.einsum(
                "hqk,qhd->khd",
                score_grad,
                queries[start_row:stop_row],
                preferred_element_type=jnp.float32,
            )
            * scaling
        )
        value_grad = value_grad.at[:stop_row].add(
            jnp.einsum(
                "hqk,qhd->khd",
                probs.astype(jnp.bfloat16),
                grad_here,
                preferred_element_type=jnp.float32,
            )
        )
    return (jnp.concatenate(query_grads, 0), key_grad, value_grad)


def line_chunk(index, size):
    return pl.ds(pl.multiple_of(index * size, size), size)


def greet_line(me, count):
    barrier = pltpu.get_barrier_semaphore()

    @pl.when(me > 0)
    def _():
        pl.semaphore_signal(
            barrier, inc=1, device_id={"mp": jnp.maximum(me - 1, 0)}, device_id_type=MESH
        )

    @pl.when(me < count - 1)
    def _():
        pl.semaphore_signal(
            barrier, inc=1, device_id={"mp": jnp.minimum(me + 1, count - 1)}, device_id_type=MESH
        )

    peers = jnp.where(me > 0, 1, 0) + jnp.where(me < count - 1, 1, 0)
    pl.semaphore_wait(barrier, peers)


def greet_peers(me, count):
    barrier = pltpu.get_barrier_semaphore()
    for offset in range(1, count):
        pl.semaphore_signal(
            barrier, inc=1, device_id={"mp": lax.rem(me + offset, count)}, device_id_type=MESH
        )
    pl.semaphore_wait(barrier, count - 1)


def line_sum(count, chunk, own, wires, sems, prepare, emit, greet=True, follow=None, always=False):
    me = lax.axis_index("mp")
    from_low, from_high, to_high, to_low = wires
    up_send, up_recv, down_send, down_recv = sems
    length = own.shape[0]
    chunks = length // chunk
    above = jnp.minimum(me + 1, count - 1)
    below = jnp.maximum(me - 1, 0)

    def up_copy(index):
        rows = line_chunk(index, chunk)
        return pltpu.make_async_remote_copy(
            src_ref=to_high.at[rows],
            dst_ref=from_low.at[rows],
            send_sem=up_send.at[index],
            recv_sem=up_recv.at[index],
            device_id={"mp": above},
            device_id_type=MESH,
        )

    def down_copy(index):
        rows = line_chunk(index, chunk)
        return pltpu.make_async_remote_copy(
            src_ref=to_low.at[rows],
            dst_ref=from_high.at[rows],
            send_sem=down_send.at[index],
            recv_sem=down_recv.at[index],
            device_id={"mp": below},
            device_id_type=MESH,
        )

    if greet:
        greet_line(me, count)

    @pl.when(me == 0)
    def _():
        from_low[...] = jnp.zeros_like(from_low)

    @pl.when(me == count - 1)
    def _():
        from_high[...] = jnp.zeros_like(from_high)

    def step(at, carry):
        if prepare is not None and always:
            prepare(at)
        elif prepare is not None:

            @pl.when(at < chunks)
            def _():
                prepare(at)

        up = at - LINE_LAG * me

        @pl.when((up >= 0) & (up < chunks))
        def _():
            rows = line_chunk(up, chunk)

            @pl.when(me > 0)
            def _():
                up_copy(up).wait_recv()

            @pl.when(me < count - 1)
            def _():
                to_high[rows, :] = (
                    from_low[rows, :].astype(jnp.float32) + own[rows, :].astype(jnp.float32)
                ).astype(jnp.bfloat16)
                up_copy(up).start()

        down = at - LINE_LAG * (count - 1 - me)

        @pl.when((down >= 0) & (down < chunks))
        def _():
            rows = line_chunk(down, chunk)

            @pl.when(me < count - 1)
            def _():
                down_copy(down).wait_recv()

            @pl.when(me > 0)
            def _():
                to_low[rows, :] = (
                    from_high[rows, :].astype(jnp.float32) + own[rows, :].astype(jnp.float32)
                ).astype(jnp.bfloat16)
                down_copy(down).start()

        ready = at - LINE_LAG * jnp.maximum(me, count - 1 - me)

        @pl.when((ready >= 0) & (ready < chunks))
        def _():
            rows = line_chunk(ready, chunk)
            total = (
                from_low[rows, :].astype(jnp.float32)
                + own[rows, :].astype(jnp.float32)
                + from_high[rows, :].astype(jnp.float32)
            )
            emit(rows, total)
            if follow is not None:
                follow(ready)

        return carry

    lax.fori_loop(0, chunks + LINE_LAG * (count - 1), step, 0)

    def drain(index, carry):
        @pl.when(me < count - 1)
        def _():
            up_copy(index).wait_send()

        @pl.when(me > 0)
        def _():
            down_copy(index).wait_send()

        return carry

    lax.fori_loop(0, chunks, drain, 0)


PICK_GROUP = 32
PICK_ALIGN = 8


def pick_kernel(spots, places, table, out, held, sems):
    rows = out.shape[0]
    span = PICK_GROUP * PICK_ALIGN

    def start(group, carry):
        def one(token, carry):
            at = group * PICK_GROUP + token
            pltpu.make_async_copy(
                table.at[pl.ds(pl.multiple_of(spots[at], PICK_ALIGN), PICK_ALIGN)],
                held.at[pl.ds(pl.multiple_of(at * PICK_ALIGN, PICK_ALIGN), PICK_ALIGN)],
                sems.at[group],
            ).start()
            return carry

        return lax.fori_loop(0, PICK_GROUP, one, carry, unroll=8)

    lax.fori_loop(0, rows // PICK_GROUP, start, 0)

    def choose(group, carry):
        block = held.at[pl.ds(pl.multiple_of(group * span, span), span)]
        pltpu.make_async_copy(table.at[pl.ds(0, span)], block, sems.at[group]).wait()
        here = line_chunk(group, PICK_GROUP)
        wanted = places[here, :]
        column = lax.broadcasted_iota(jnp.int32, (PICK_GROUP, span), 1)
        chosen = jnp.where(column == wanted, 1.0, 0.0).astype(jnp.bfloat16)
        out[here, :] = jnp.dot(
            chosen, block[...], preferred_element_type=jnp.float32
        ).astype(jnp.bfloat16)
        return carry

    lax.fori_loop(0, rows // PICK_GROUP, choose, 0)


def pick_call(index, table, name):
    rows = index.shape[0]
    vocab, width = table.shape
    safe = jnp.clip(index, 0, vocab - 1)
    spots = safe - safe % PICK_ALIGN
    column = index.reshape(rows, 1)
    token = lax.broadcasted_iota(jnp.int32, (rows, 1), 0) % PICK_GROUP
    places = jnp.where(
        (column >= 0) & (column < vocab), token * PICK_ALIGN + column % PICK_ALIGN, -1
    )
    return pl.pallas_call(
        pick_kernel,
        name=name,
        in_specs=[
            pl.BlockSpec(memory_space=pltpu.SMEM),
            pl.BlockSpec(memory_space=pltpu.VMEM),
            pl.BlockSpec(memory_space=pl.ANY),
        ],
        out_specs=pl.BlockSpec(memory_space=pltpu.VMEM),
        out_shape=jax.ShapeDtypeStruct((rows, width), jnp.bfloat16),
        scratch_shapes=[
            pltpu.VMEM((rows * PICK_ALIGN, width), jnp.bfloat16),
            pltpu.SemaphoreType.DMA((rows // PICK_GROUP,)),
        ],
        compiler_params=pltpu.CompilerParams(vmem_limit_bytes=VMEM_LIMIT),
        cost_estimate=pl.CostEstimate(
            flops=2 * rows * PICK_GROUP * PICK_ALIGN * width,
            bytes_accessed=2 * rows * PICK_ALIGN * width,
            transcendentals=0,
        ),
    )(spots, places, table)


LINE_CHUNK = 32
LINE_LAG = 3
WORK_ROWS = 256


def line_scratch(length, width):
    chunks = length // LINE_CHUNK
    return [pltpu.VMEM((length, width), jnp.bfloat16)] * 4 + [
        pltpu.SemaphoreType.DMA((chunks,))
    ] * 4


def line_call(kernel, name, collective_id, outs, scratch, operands, flops=0, spaces=()):
    size = sum(o.size * o.dtype.itemsize for o in operands) + sum(
        o.size * o.dtype.itemsize for o in outs
    )
    vmem = pl.BlockSpec(memory_space=pltpu.VMEM)
    return pl.pallas_call(
        kernel,
        name=name,
        out_shape=outs,
        in_specs=[vmem] * (len(operands) - len(spaces))
        + [pl.BlockSpec(memory_space=space) for space in spaces],
        out_specs=[vmem] * len(outs),
        scratch_shapes=scratch,
        compiler_params=pltpu.CompilerParams(
            collective_id=collective_id, has_side_effects=True, vmem_limit_bytes=VMEM_LIMIT
        ),
        cost_estimate=pl.CostEstimate(
            flops=flops, bytes_accessed=size + 100_000_000, transcendentals=0
        ),
    )(*operands)


def start_kernel(
    count,
    part,
    gain,
    shift,
    bias,
    master,
    w_qkv,
    w_in,
    w_down,
    rows_out,
    attn_out,
    base_out,
    ffn_out,
    pool_out,
    *scratch,
):
    (normed, held_qkv, held_in, held_down, sems, pool, near_out, near_in, far_out, far_in) = (
        scratch[8:]
    )
    shards = pool.shape[0]
    splits = shards.bit_length() - 1
    me = lax.axis_index("dp")
    lane = lax.axis_index("mp")
    mates = [me + 2**k * (1 - 2 * ((me // 2**k) % 2)) for k in range(splits)]
    peers = [lax.rem(lane + offset, count) for offset in range(count)]
    barrier = pltpu.get_barrier_semaphore()
    for mate in mates:
        pl.semaphore_signal(barrier, inc=1, device_id={"dp": mate, "mp": lane}, device_id_type=MESH)
    for peer in peers[1:]:
        pl.semaphore_signal(barrier, inc=1, device_id={"dp": me, "mp": peer}, device_id_type=MESH)
    pl.semaphore_wait(barrier, splits + count - 1)
    pool[me, lane] = master[...].astype(jnp.bfloat16)

    def near(offset):
        return pltpu.make_async_remote_copy(
            src_ref=pool.at[me, lane],
            dst_ref=pool.at[me, lane],
            send_sem=near_out.at[offset],
            recv_sem=near_in.at[offset],
            device_id={"dp": me, "mp": peers[offset]},
            device_id_type=MESH,
        )

    def far(stage):
        bit = splits - 1 - stage
        copies = []
        for place in range(2**stage):
            slot = lax.rem(me, 2 ** (bit + 1)) + place * 2 ** (bit + 1)
            copies.append(
                pltpu.make_async_remote_copy(
                    src_ref=pool.at[slot],
                    dst_ref=pool.at[slot],
                    send_sem=far_out.at[2**stage - 1 + place],
                    recv_sem=far_in.at[2**stage - 1 + place],
                    device_id={"dp": mates[bit], "mp": lane},
                    device_id_type=MESH,
                )
            )
        return copies

    for offset in range(1, count):
        near(offset).start()

    pace = (part.shape[0] // LINE_CHUNK + 8) // (splits + 2)

    def prepare(at):
        for stage in range(splits + 1):

            @pl.when(at == pace * (stage + 1))
            def _(stage=stage):
                if stage == 0:
                    for offset in range(1, count):
                        near(offset).wait_recv()
                else:
                    for copy in far(stage - 1):
                        copy.wait_recv()
                if stage < splits:
                    for copy in far(stage):
                        copy.start()

    loads = [
        pltpu.make_async_copy(src, dst, sems.at[slot])
        for slot, (src, dst) in enumerate(
            ((w_qkv, held_qkv), (w_in, held_in), (w_down, held_down))
        )
    ]
    for load in loads:
        load.start()

    def emit(rows, total):
        rows_out[rows, :] = total.astype(jnp.bfloat16)
        centre = total - jnp.mean(total, -1, keepdims=True)
        spread = jnp.mean(centre * centre, -1, keepdims=True)
        base = centre * lax.rsqrt(spread + NORM_EPS)
        attn_out[rows, :] = (base * gain[0:1, :] + shift[0:1, :]).astype(jnp.bfloat16)
        normed[rows, :] = (base * gain[1:2, :] + shift[1:2, :]).astype(jnp.bfloat16)

    per = WORK_ROWS // LINE_CHUNK

    def follow(ready):
        @pl.when(ready == per - 1)
        def _():
            for load in loads:
                load.wait()

        @pl.when(lax.rem(ready, per) == per - 1)
        def _():
            rows = line_chunk(ready // per, WORK_ROWS)
            base_out[rows, :] = jnp.dot(
                attn_out[rows, :], held_qkv[...], preferred_element_type=jnp.float32
            )
            pre = (
                jnp.dot(normed[rows, :], held_in[...], preferred_element_type=jnp.float32)
                + bias[...]
            )
            hidden = (0.5 * pre * (1.0 + lax.erf(pre * 0.5**0.5))).astype(jnp.bfloat16)
            ffn_out[rows, :] = jnp.dot(
                hidden, held_down[...], preferred_element_type=jnp.float32
            ).astype(jnp.bfloat16)

    line_sum(
        count,
        LINE_CHUNK,
        part,
        scratch[:4],
        scratch[4:8],
        prepare,
        emit,
        greet=False,
        follow=follow,
        always=True,
    )
    pool_out[...] = pool[...]
    for offset in range(1, count):
        near(offset).wait_send()
    for stage in range(splits):
        for copy in far(stage):
            copy.wait_send()


def resid_kernel(count, part, start, gain, shift, resid_out, final_out, *scratch):
    def emit(rows, total):
        resid = start[rows, :].astype(jnp.float32) + total
        resid_out[rows, :] = resid
        normed = layer_norm(resid, gain[2:3, :], shift[2:3, :])
        final_out[rows, :] = normed.astype(jnp.bfloat16)

    line_sum(count, LINE_CHUNK, part, scratch[:4], scratch[4:], None, emit)


def branch_kernel(
    count, raw, hits, stats, resid, gain, prompts, totals, out, loss_out, *scratch
):
    own, note_send, note_recv, scales, note_out, note_in = scratch[8:]
    me = lax.axis_index("mp")
    rows_all = raw.shape[0]
    greet_peers(me, count)
    note_send[...] = stats[...].T[0:8, :]
    copies = []
    for offset in range(1, count):
        copy = pltpu.make_async_remote_copy(
            src_ref=note_send,
            dst_ref=note_recv.at[offset],
            send_sem=note_out.at[offset],
            recv_sem=note_in.at[offset],
            device_id={"mp": lax.rem(me + offset, count)},
            device_id_type=MESH,
        )
        copy.start()
        copies.append(copy)
    mine = note_send[...]
    for copy in copies:
        copy.wait_recv()
    others = [mine] + [note_recv[offset] for offset in range(1, count)]
    top = functools.reduce(jnp.maximum, [part[0:1, :] for part in others])
    total = sum(part[1:2, :] * jnp.exp(part[0:1, :] - top) for part in others)
    found = sum(part[2:3, :] for part in others)
    spread_row = top + jnp.log(total)
    amount = sum(totals[e] - prompts[e] for e in range(prompts.shape[0]))
    example = lax.axis_index("dp")
    position = lax.broadcasted_iota(jnp.int32, (1, rows_all), 1)
    keep = (position >= prompts[example] - 1) & (position < totals[example] - 1)
    share = jnp.where(keep, 1.0 / jnp.broadcast_to(amount, (1, rows_all)).astype(jnp.float32), 0.0)
    loss_out[...] = (spread_row - found) * share
    factor = jnp.exp(mine[0:1, :] - spread_row) * share
    pair = jnp.concatenate([factor, share, jnp.zeros((126, rows_all), jnp.float32)], 0)
    scales[...] = pair.T

    def prepare(at):
        rows = line_chunk(at, LINE_CHUNK)
        scale = scales[rows, :]
        own[rows, :] = (
            raw[rows, :] * scale[:, 0:1] - hits[rows, :].astype(jnp.float32) * scale[:, 1:2]
        ).astype(jnp.bfloat16)

    def emit(rows, total):
        values = resid[rows, :]
        centre = values - jnp.mean(values, -1, keepdims=True)
        spread = jnp.mean(centre * centre, -1, keepdims=True)
        inverse = lax.rsqrt(spread + NORM_EPS)
        normed = centre * inverse
        up = total * gain[2:3, :]
        out[rows, :] = (
            inverse
            * (
                up
                - jnp.mean(up, -1, keepdims=True)
                - normed * jnp.mean(up * normed, -1, keepdims=True)
            )
        ).astype(jnp.bfloat16)

    line_sum(count, LINE_CHUNK, own, scratch[:4], scratch[4:8], prepare, emit, greet=False)
    for copy in copies:
        copy.wait_send()


def loss_kernel(vocab, tile, values, ahead, behind, hits, acc, stats, logits, probs, tops, sums):
    at = pl.program_id(0)
    tiles = pl.num_programs(0) - 1
    rows_all = values.shape[0]

    @pl.when(at == 0)
    def _():
        acc[...] = jnp.zeros_like(acc)
        tops[...] = jnp.full_like(tops, -1e29)
        sums[...] = jnp.zeros_like(sums)
        logits[...] = jnp.full_like(logits, -1e30)

    tail = vocab % tile
    if tail:

        @pl.when(at >= tiles - 1)
        def _():
            ahead[tail:, :] = jnp.zeros((tile - tail, ahead.shape[1]), ahead.dtype)

        @pl.when(at >= tiles)
        def _():
            behind[tail:, :] = jnp.zeros((tile - tail, behind.shape[1]), behind.dtype)

    ids = (at - 1) * tile + lax.broadcasted_iota(jnp.int32, (1, tile), 1)
    scores = logits[...] + jnp.where(ids < vocab, 0.0, -1e30)
    old = tops[:, 0:1]
    new = jnp.maximum(old, jnp.max(scores, -1, keepdims=True))
    weights = jnp.exp(scores - new)
    shrink = jnp.exp(old - new)
    sums[...] = sums[...] * shrink + jnp.sum(weights, -1, keepdims=True)
    tops[...] = jnp.broadcast_to(new, tops.shape)
    acc[...] = acc[...] * shrink
    probs[...] = weights.astype(jnp.bfloat16)
    logits[...] = lax.dot_general(
        values[...], ahead[...], (((1,), (1,)), ((), ())), preferred_element_type=jnp.float32
    )
    acc[...] += jnp.dot(probs[...], behind[...], preferred_element_type=jnp.float32)

    @pl.when(at == tiles)
    def _():
        found = jnp.sum(
            values[...].astype(jnp.float32) * hits[...].astype(jnp.float32), -1, keepdims=True
        )
        column = lax.broadcasted_iota(jnp.int32, (rows_all, 128), 1)
        stats[...] = jnp.where(
            column == 0, tops[...], jnp.where(column == 1, sums[...], found)
        )


LOSS_TILE = 512


def loss_call(values, head_rows, hits):
    rows, width = values.shape
    vocab = head_rows.shape[0]
    tile = LOSS_TILE
    tiles = pl.cdiv(vocab, tile)
    whole = pl.BlockSpec((rows, width), lambda j: (0, 0))
    return pl.pallas_call(
        functools.partial(loss_kernel, vocab, tile),
        name="loss",
        grid=(tiles + 1,),
        in_specs=[
            whole,
            pl.BlockSpec((tile, width), lambda j: (jnp.minimum(j, tiles - 1), 0)),
            pl.BlockSpec((tile, width), lambda j: (jnp.maximum(j - 1, 0), 0)),
            whole,
        ],
        out_specs=[whole, pl.BlockSpec((rows, 128), lambda j: (0, 0))],
        out_shape=[
            jax.ShapeDtypeStruct((rows, width), jnp.float32),
            jax.ShapeDtypeStruct((rows, 128), jnp.float32),
        ],
        scratch_shapes=[
            pltpu.VMEM((rows, tile), jnp.float32),
            pltpu.VMEM((rows, tile), jnp.bfloat16),
            pltpu.VMEM((rows, 128), jnp.float32),
            pltpu.VMEM((rows, 128), jnp.float32),
        ],
        compiler_params=pltpu.CompilerParams(vmem_limit_bytes=VMEM_LIMIT),
        cost_estimate=pl.CostEstimate(
            flops=4 * rows * width * vocab,
            bytes_accessed=4 * width * vocab,
            transcendentals=rows * vocab,
        ),
    )(values, head_rows, head_rows, hits)


def fold_kernel(splits, count, *refs):
    fulls = refs[0:4]
    groups = refs[4:8]
    losses, master, first, second, bases = refs[8:13]
    loss_out, norm_out, first_out, second_out, master_out = refs[13:18]
    scratch = refs[18:]
    sends = scratch[0:splits]
    recvs = scratch[splits : 2 * splits]
    keeps = scratch[2 * splits : 3 * splits]
    (line_send, line_recv, turn_send, turn_recv, note_send, note_recv, tell_send, tell_recv) = scratch[
        3 * splits : 3 * splits + 8
    ]
    (half_out, half_in, line_out, line_in, turn_out, turn_in, note_out, note_in, tell_out, tell_in) = (
        scratch[3 * splits + 8 :]
    )
    shards = 2**splits
    me = lax.axis_index("dp")
    lane = lax.axis_index("mp")
    full_rows = fulls[0].shape[0] // shards
    group_rows = groups[0].shape[0] // shards
    own_rows = full_rows // count
    bits = [(me // 2**k) % 2 for k in range(splits)]
    mates = [me + 2**k * (1 - 2 * bits[k]) for k in range(splits)]
    peers = [lax.rem(lane + offset, count) for offset in range(count)]
    spot = lane * shards + me
    goal = (spot // count, lax.rem(spot, count))
    place = me * count + lane
    origin = (lax.rem(place, shards), place // shards)
    moved = spot != place

    barrier = pltpu.get_barrier_semaphore()
    for mate in mates:
        pl.semaphore_signal(barrier, inc=1, device_id={"dp": mate, "mp": lane}, device_id_type=MESH)
    for peer in peers[1:]:
        pl.semaphore_signal(barrier, inc=1, device_id={"dp": me, "mp": peer}, device_id_type=MESH)

    @pl.when(moved)
    def _():
        for device in (goal, origin):
            pl.semaphore_signal(
                barrier, inc=1, device_id={"dp": device[0], "mp": device[1]}, device_id_type=MESH
            )

    pl.semaphore_wait(barrier, splits + count - 1 + jnp.where(moved, 2, 0))

    def remote(src, dst, out_sem, in_sem, device):
        return pltpu.make_async_remote_copy(
            src_ref=src,
            dst_ref=dst,
            send_sem=out_sem,
            recv_sem=in_sem,
            device_id={"dp": device[0], "mp": device[1]},
            device_id_type=MESH,
        )

    def piece(index):
        whole = pl.ds(pl.multiple_of(index * full_rows, full_rows), full_rows)
        part = pl.ds(pl.multiple_of(index * group_rows, group_rows), group_rows)
        return jnp.concatenate(
            [ref[whole, :] for ref in fulls] + [ref[part, :] for ref in groups], 0
        )

    started = []
    current = piece
    for k in range(splits):
        half = shards >> (k + 1)
        for i in range(half):
            sends[k][i] = current(2 * i + 1 - bits[k]).astype(jnp.bfloat16)
        copy = remote(sends[k], recvs[k], half_out.at[k], half_in.at[k], (mates[k], lane))
        copy.start()
        started.append(copy)
        for i in range(half):
            keeps[k][i] = current(2 * i + bits[k])
        copy.wait_recv()
        current = functools.partial(
            lambda kept, came, i: kept[i] + came[i].astype(jnp.float32), keeps[k], recvs[k]
        )
    final = keeps[splits - 1]
    final[0] = current(0)

    def chosen(peer):
        return jnp.concatenate(
            [
                final[
                    0,
                    pl.ds(pl.multiple_of(a * full_rows + peer * own_rows, own_rows), own_rows),
                    :,
                ]
                for a in range(4)
            ],
            0,
        )

    turn_send[...] = final[0, 4 * full_rows :, :].astype(jnp.bfloat16)
    turn = remote(turn_send, turn_recv, turn_out, turn_in, goal)

    @pl.when(moved)
    def _():
        turn.start()

    for offset in range(1, count):
        line_send[offset] = chosen(peers[offset]).astype(jnp.bfloat16)
        copy = remote(
            line_send.at[offset],
            line_recv.at[offset],
            line_out.at[offset],
            line_in.at[offset],
            (me, peers[offset]),
        )
        copy.start()
        started.append(copy)
    total = chosen(lane)

    @pl.when(moved)
    def _():
        turn.wait()

    @pl.when(jnp.logical_not(moved))
    def _():
        turn_recv[...] = turn_send[...]

    for copy in started[splits:]:
        copy.wait_recv()
    for offset in range(1, count):
        total = total + line_recv[offset].astype(jnp.float32)
    part = turn_recv[...].astype(jnp.float32)

    column = lax.broadcasted_iota(jnp.int32, (8, 128), 1)
    row = lax.broadcasted_iota(jnp.int32, (8, 128), 0)
    squares = jnp.sum(total * total) + jnp.sum(part * part)
    spot_norm = (row == 0) & (column == 0)
    spot_loss = (row == 0) & (column == 1)
    note = jnp.where(spot_norm, squares, 0.0) + jnp.where(spot_loss, jnp.sum(losses[...]), 0.0)

    def rows_of(index):
        source, slot = (total, (0, 1, 2, 7).index(index)) if index in (0, 1, 2, 7) else (
            part,
            index - 3,
        )
        return source[slot * own_rows : (slot + 1) * own_rows, :]

    turned = [
        jnp.dot(
            rows_of(m), bases[m], precision=HIGH_PRECISION, preferred_element_type=jnp.float32
        )
        for m in range(8)
    ]
    for k in range(splits):
        note_send[k] = note
        copy = remote(
            note_send.at[k], note_recv.at[k], note_out.at[k], note_in.at[k], (mates[k], lane)
        )
        copy.start()
        started.append(copy)
        copy.wait_recv()
        note = note + note_recv[k]
    tell_send[...] = note
    tells = []
    for offset in range(1, count):
        copy = remote(
            tell_send,
            tell_recv.at[offset],
            tell_out.at[offset],
            tell_in.at[offset],
            (me, peers[offset]),
        )
        copy.start()
        tells.append(copy)
    for copy in tells:
        copy.wait_recv()
    everything = note
    for offset in range(1, count):
        everything = everything + tell_recv[offset]
    norm = jnp.sqrt(jnp.sum(jnp.where(spot_norm, everything, 0.0), keepdims=True))
    loss_out[...] = jnp.sum(jnp.where(spot_loss, note, 0.0), keepdims=True)
    norm_out[...] = norm
    factor = jnp.minimum(1.0, CLIP_LIMIT / norm)
    for m in range(8):
        rotated = turned[m] * factor
        new_first = BETA_FIRST * first[m] + (1.0 - BETA_FIRST) * rotated
        new_second = BETA_SECOND * second[m] + (1.0 - BETA_SECOND) * rotated * rotated
        first_out[m] = new_first
        second_out[m] = new_second
        normed = (
            new_first
            / (1.0 - BETA_FIRST**ADAM_STEP)
            / (jnp.sqrt(new_second / (1.0 - BETA_SECOND**ADAM_STEP)) + ADAM_EPS)
        )
        back = lax.dot_general(
            normed,
            bases[m],
            (((1,), (1,)), ((), ())),
            precision=HIGH_PRECISION,
            preferred_element_type=jnp.float32,
        )
        master_out[m] = master[m] - LEARN_RATE * (back + DECAY_RATE * master[m])
    for copy in started + tells:
        copy.wait_send()


def fold_call(fulls, groups, losses, master, first_moment, second_moment, bases):
    shards = lax.axis_size("dp")
    count = lax.axis_size("mp")
    splits = shards.bit_length() - 1
    width = fulls[0].shape[1]
    pile = 4 * (fulls[0].shape[0] + groups[0].shape[0]) // shards
    own = 4 * fulls[0].shape[0] // (shards * count)
    low = jnp.bfloat16
    halves = [shards >> (k + 1) for k in range(splits)]
    dma = pltpu.SemaphoreType.DMA
    scratch = (
        [pltpu.VMEM((half, pile, width), low) for half in halves] * 2
        + [pltpu.VMEM((half, pile, width), jnp.float32) for half in halves]
        + [pltpu.VMEM((count, own, width), low)] * 2
        + [pltpu.VMEM((4 * groups[0].shape[0] // shards, width), low)] * 2
        + [pltpu.VMEM((splits, 8, 128), jnp.float32)] * 2
        + [pltpu.VMEM((8, 128), jnp.float32), pltpu.VMEM((count, 8, 128), jnp.float32)]
        + [dma((splits,))] * 2
        + [dma((count,))] * 2
        + [dma(())] * 2
        + [dma((splits,))] * 2
        + [dma((count,))] * 2
    )
    scalar = jax.ShapeDtypeStruct((1, 1), jnp.float32)
    state = jax.ShapeDtypeStruct(master.shape, jnp.float32)
    return line_call(
        functools.partial(fold_kernel, splits, count),
        "fold",
        3,
        [scalar, scalar, state, state, state],
        scratch,
        [*fulls, *groups, losses, master, first_moment, second_moment, bases],
    )


def per_device(
    token_ids,
    prompt_len,
    example_len,
    embedding,
    w_qkv,
    w_out,
    w_in,
    b_in,
    w_down,
    unembed,
    ln_gain,
    ln_bias,
    master,
    first_moment,
    second_moment,
    eigen_bases,
):
    group_count = lax.axis_size("mp")
    group_index = lax.axis_index("mp")
    head_rows = lax.all_gather(unembed.T, "dp", axis=1, tiled=True)
    examples, length = token_ids.shape
    width = embedding.shape[0]
    vocab_local = head_rows.shape[0]
    rows = examples * length
    local_heads = HEADS // group_count
    group_width = local_heads * HD
    flat_ids = token_ids.reshape(rows)
    picked = pick_call(flat_ids - group_index * width, embedding, "pick_start")
    shape_low = jax.ShapeDtypeStruct((rows, D), jnp.bfloat16)
    shape_wide = jax.ShapeDtypeStruct((rows, D), jnp.float32)
    shards = lax.axis_size("dp")
    own_rows = master.shape[1]
    pool_shape = (shards, group_count, 8, own_rows, R)
    start_rows, normed_attn, base, ffn_part, pool = line_call(
        functools.partial(start_kernel, group_count),
        "start_rows",
        0,
        [
            shape_low,
            shape_low,
            jax.ShapeDtypeStruct((rows, w_qkv.shape[1]), jnp.float32),
            shape_low,
            jax.ShapeDtypeStruct(pool_shape, jnp.bfloat16),
        ],
        line_scratch(rows, D)
        + [
            pltpu.VMEM((rows, D), jnp.bfloat16),
            pltpu.VMEM(w_qkv.shape, jnp.bfloat16),
            pltpu.VMEM(w_in.shape, jnp.bfloat16),
            pltpu.VMEM(w_down.shape, jnp.bfloat16),
            pltpu.SemaphoreType.DMA((3,)),
            pltpu.VMEM(pool_shape, jnp.bfloat16),
        ]
        + [pltpu.SemaphoreType.DMA((group_count,))] * 2
        + [pltpu.SemaphoreType.DMA((shards - 1,))] * 2,
        [picked, ln_gain, ln_bias, b_in.reshape(1, -1), master, w_qkv, w_in, w_down],
        spaces=(pl.ANY,) * 3,
    )
    adapters = pool.transpose(2, 0, 1, 3, 4).reshape(8, -1, R)
    target = jnp.roll(token_ids, -1, axis=1).reshape(rows)
    inner = jnp.dot(
        normed_attn,
        jnp.concatenate([adapters[0], adapters[1], adapters[2]], 1),
        preferred_element_type=jnp.float32,
    ).astype(jnp.bfloat16)
    base = base.reshape(rows, local_heads, 3, HD)
    adapter_rows = [
        lax.dynamic_slice_in_dim(
            adapters[3 + selector_index], group_index * group_width, group_width, 0
        )
        for selector_index in range(3)
    ]
    pre_parts = []
    for selector_index in range(3):
        extra = jnp.einsum(
            "lr,dr->ld",
            inner[:, selector_index * R : (selector_index + 1) * R],
            adapter_rows[selector_index],
            preferred_element_type=jnp.float32,
        )
        pre_parts.append(base[:, :, selector_index] + extra.reshape(rows, local_heads, HD))
    cosine, sine = rope_tables(length)
    queries = rotate(pre_parts[0].reshape(examples, length, local_heads, HD), cosine, sine).astype(
        jnp.bfloat16
    )
    key_rows = rotate(pre_parts[1].reshape(examples, length, local_heads, HD), cosine, sine).astype(
        jnp.bfloat16
    )
    value_rows = pre_parts[2].reshape(examples, length, local_heads, HD).astype(jnp.bfloat16)
    sample = 0
    context_here, spread_local = attend(queries[sample], key_rows[sample], value_rows[sample])
    spreads = [spread_local]
    context = context_here.reshape(rows, group_width)
    out_rows = lax.dynamic_slice_in_dim(adapters[6], group_index * group_width, group_width, 0)
    inner_out = jnp.dot(context, out_rows, preferred_element_type=jnp.float32).astype(jnp.bfloat16)
    partial_value = (
        jnp.dot(context, w_out, preferred_element_type=jnp.float32)
        + jnp.einsum("lr,dr->ld", inner_out, adapters[7], preferred_element_type=jnp.float32)
        + ffn_part.astype(jnp.float32)
    )
    resid, final_rows = line_call(
        functools.partial(resid_kernel, group_count),
        "resid_rows",
        1,
        [shape_wide, shape_low],
        line_scratch(rows, D),
        [partial_value.astype(jnp.bfloat16), start_rows, ln_gain, ln_bias],
    )
    goal = target - group_index * vocab_local
    hits = pick_call(goal, head_rows, "pick_target")
    raw_grad, stats = loss_call(final_rows, head_rows, hits)
    branch_grad, losses = line_call(
        functools.partial(branch_kernel, group_count),
        "branch_rows",
        2,
        [shape_low, jax.ShapeDtypeStruct((1, rows), jnp.float32)],
        line_scratch(rows, D)
        + [
            pltpu.VMEM((rows, D), jnp.bfloat16),
            pltpu.VMEM((8, rows), jnp.float32),
            pltpu.VMEM((group_count, 8, rows), jnp.float32),
            pltpu.VMEM((rows, 128), jnp.float32),
            pltpu.SemaphoreType.DMA((group_count,)),
            pltpu.SemaphoreType.DMA((group_count,)),
        ],
        [raw_grad, hits, stats, resid, ln_gain, prompt_len, example_len],
        spaces=(pltpu.SMEM,) * 2,
    )
    inner_out_grad = jnp.dot(branch_grad, adapters[7], preferred_element_type=jnp.float32).astype(
        jnp.bfloat16
    )
    grad_out_b = jnp.einsum("ld,lr->dr", branch_grad, inner_out, preferred_element_type=jnp.float32)
    grad_out_a = jnp.einsum(
        "ld,lr->dr", context, inner_out_grad, preferred_element_type=jnp.float32
    )
    context_grad = jnp.einsum(
        "ld,ed->le", branch_grad, w_out, preferred_element_type=jnp.float32
    ) + jnp.einsum("lr,dr->ld", inner_out_grad, out_rows, preferred_element_type=jnp.float32)
    context_grad = context_grad.astype(jnp.bfloat16).reshape(examples, length, local_heads, HD)
    sample = 0
    query_grad, key_grad, value_grad = attend_back(
        queries[sample], key_rows[sample], value_rows[sample], spreads[sample], context_grad[sample]
    )
    query_parts = [rotate_back(query_grad, cosine, sine)]
    key_parts = [rotate_back(key_grad, cosine, sine)]
    value_parts = [value_grad]
    pre_grads = [
        parts[0].reshape(rows, group_width).astype(jnp.bfloat16)
        for parts in (query_parts, key_parts, value_parts)
    ]
    complete_gradients = []
    local_grads = []
    for selector_index in range(3):
        projected_values = jnp.einsum(
            "ld,le->de", normed_attn, pre_grads[selector_index], preferred_element_type=jnp.float32
        )
        complete_gradients.append(
            jnp.dot(
                projected_values,
                adapter_rows[selector_index].astype(jnp.float32),
                precision=HIGH_PRECISION,
            )
        )
        local_grads.append(
            jnp.einsum(
                "ld,lr->dr",
                pre_grads[selector_index],
                inner[:, selector_index * R : (selector_index + 1) * R],
                preferred_element_type=jnp.float32,
            )
        )
    local_grads.append(grad_out_a)
    mean_loss, grad_norm, new_first, new_second, new_master = fold_call(
        [*complete_gradients, grad_out_b],
        local_grads,
        losses,
        master,
        first_moment,
        second_moment,
        eigen_bases,
    )
    return (mean_loss.reshape(()), grad_norm.reshape(()), new_first, new_second, new_master)


def solution(mesh):
    placed = (
        P("dp", None),
        P(),
        P(),
        P("mp", None),
        P(None, "mp"),
        P("mp", None),
        P(None, "mp"),
        P("mp"),
        P("mp", None),
        P("dp", "mp"),
        P(),
        P(),
        P(None, ("dp", "mp"), None),
        P(None, ("dp", "mp"), None),
        P(None, ("dp", "mp"), None),
        P(),
    )
    return jax.shard_map(
        per_device,
        mesh=mesh,
        in_specs=placed,
        out_specs=(
            P(),
            P(),
            P(None, ("dp", "mp"), None),
            P(None, ("dp", "mp"), None),
            P(None, ("dp", "mp"), None),
        ),
        check_vma=False,
    )
```

```python
import functools

import jax
import jax.numpy as jnp
from jax import lax
from jax.experimental import pallas as pl
from jax.experimental.pallas import tpu as pltpu
from jax.sharding import PartitionSpec as P

MESH = pl.DeviceIdType.MESH
VMEM_LIMIT = 60 * 1024 * 1024

D = 1024
HEADS = 16
R = 128
ADAM_STEP = 10
HD = 64
ROT = 16


HIGH_PRECISION = lax.Precision.HIGHEST
NORM_EPS = 1e-05
ROPE_BASE = 10000.0
CLIP_LIMIT = 0.01
LEARN_RATE = 0.02
BETA_FIRST = 0.9
BETA_SECOND = 0.999
ADAM_EPS = 1e-08
DECAY_RATE = 0.01


def layer_norm(values, gain, shift):
    centre = values - jnp.mean(values, -1, keepdims=True)
    spread = jnp.mean(centre * centre, -1, keepdims=True)
    return centre * lax.rsqrt(spread + NORM_EPS) * gain + shift


def rope_tables(length):
    half = ROT // 2
    freqs = ROPE_BASE ** (-2.0 * jnp.arange(half, dtype=jnp.float32) / ROT)
    angles = jnp.arange(length, dtype=jnp.float32)[:, None] * freqs[None, :]
    return (jnp.cos(angles)[:, None, :], jnp.sin(angles)[:, None, :])


def rotate_back(upstream, cosine, sine):
    half = ROT // 2
    first = upstream[..., :half]
    second = upstream[..., half:ROT]
    return jnp.concatenate(
        [first * cosine + second * sine, second * cosine - first * sine, upstream[..., ROT:]], -1
    )


def masked_scores(queries, key_rows, start_row, stop_row):
    scores = jnp.einsum(
        "qhd,khd->hqk",
        queries[start_row:stop_row],
        key_rows[:stop_row],
        preferred_element_type=jnp.float32,
    ) * HD ** (-0.5)
    query_pos = start_row + jnp.arange(stop_row - start_row)[:, None]
    causal = jnp.arange(stop_row)[None, :] <= query_pos
    return jnp.where(causal[None], scores, -1e30)


def attend_back(queries, key_rows, value_rows, spreads, upstream):
    length = queries.shape[0]
    row_block = min(512, length)
    scaling = HD ** (-0.5)
    query_grads = []
    key_grad = jnp.zeros(key_rows.shape, jnp.float32)
    value_grad = jnp.zeros(value_rows.shape, jnp.float32)
    for start_row in range(0, length, row_block):
        stop_row = start_row + row_block
        scores = masked_scores(queries, key_rows, start_row, stop_row)
        probs = jnp.exp(scores - spreads[:, start_row:stop_row, None])
        grad_here = upstream[start_row:stop_row]
        prob_grad = jnp.einsum(
            "qhd,khd->hqk", grad_here, value_rows[:stop_row], preferred_element_type=jnp.float32
        )
        inner_sum = jnp.sum(probs * prob_grad, -1, keepdims=True)
        score_grad = (probs * (prob_grad - inner_sum)).astype(jnp.bfloat16)
        query_grads.append(
            jnp.einsum(
                "hqk,khd->qhd", score_grad, key_rows[:stop_row], preferred_element_type=jnp.float32
            )
            * scaling
        )
        key_grad = key_grad.at[:stop_row].add(
            jnp.einsum(
                "hqk,qhd->khd",
                score_grad,
                queries[start_row:stop_row],
                preferred_element_type=jnp.float32,
            )
            * scaling
        )
        value_grad = value_grad.at[:stop_row].add(
            jnp.einsum(
                "hqk,qhd->khd",
                probs.astype(jnp.bfloat16),
                grad_here,
                preferred_element_type=jnp.float32,
            )
        )
    return (jnp.concatenate(query_grads, 0), key_grad, value_grad)


def line_chunk(index, size):
    return pl.ds(pl.multiple_of(index * size, size), size)


def greet_line(me, count):
    barrier = pltpu.get_barrier_semaphore()

    @pl.when(me > 0)
    def _():
        pl.semaphore_signal(
            barrier, inc=1, device_id={"mp": jnp.maximum(me - 1, 0)}, device_id_type=MESH
        )

    @pl.when(me < count - 1)
    def _():
        pl.semaphore_signal(
            barrier, inc=1, device_id={"mp": jnp.minimum(me + 1, count - 1)}, device_id_type=MESH
        )

    peers = jnp.where(me > 0, 1, 0) + jnp.where(me < count - 1, 1, 0)
    pl.semaphore_wait(barrier, peers)


def greet_peers(me, count):
    barrier = pltpu.get_barrier_semaphore()
    for offset in range(1, count):
        pl.semaphore_signal(
            barrier, inc=1, device_id={"mp": lax.rem(me + offset, count)}, device_id_type=MESH
        )
    pl.semaphore_wait(barrier, count - 1)


def line_sum(count, chunk, own, wires, sems, prepare, emit, greet=True, follow=None, always=False):
    me = lax.axis_index("mp")
    from_low, from_high, to_high, to_low = wires
    up_send, up_recv, down_send, down_recv = sems
    length = own.shape[0]
    chunks = length // chunk
    above = jnp.minimum(me + 1, count - 1)
    below = jnp.maximum(me - 1, 0)

    def up_copy(index):
        rows = line_chunk(index, chunk)
        return pltpu.make_async_remote_copy(
            src_ref=to_high.at[rows],
            dst_ref=from_low.at[rows],
            send_sem=up_send.at[index],
            recv_sem=up_recv.at[index],
            device_id={"mp": above},
            device_id_type=MESH,
        )

    def down_copy(index):
        rows = line_chunk(index, chunk)
        return pltpu.make_async_remote_copy(
            src_ref=to_low.at[rows],
            dst_ref=from_high.at[rows],
            send_sem=down_send.at[index],
            recv_sem=down_recv.at[index],
            device_id={"mp": below},
            device_id_type=MESH,
        )

    if greet:
        greet_line(me, count)

    @pl.when(me == 0)
    def _():
        from_low[...] = jnp.zeros_like(from_low)

    @pl.when(me == count - 1)
    def _():
        from_high[...] = jnp.zeros_like(from_high)

    def step(at, carry):
        if prepare is not None and always:
            prepare(at)
        elif prepare is not None:

            @pl.when(at < chunks)
            def _():
                prepare(at)

        up = at - LINE_LAG * me

        @pl.when((up >= 0) & (up < chunks))
        def _():
            rows = line_chunk(up, chunk)

            @pl.when(me > 0)
            def _():
                up_copy(up).wait_recv()

            @pl.when(me < count - 1)
            def _():
                to_high[rows, :] = (
                    from_low[rows, :].astype(jnp.float32) + own[rows, :].astype(jnp.float32)
                ).astype(jnp.bfloat16)
                up_copy(up).start()

        down = at - LINE_LAG * (count - 1 - me)

        @pl.when((down >= 0) & (down < chunks))
        def _():
            rows = line_chunk(down, chunk)

            @pl.when(me < count - 1)
            def _():
                down_copy(down).wait_recv()

            @pl.when(me > 0)
            def _():
                to_low[rows, :] = (
                    from_high[rows, :].astype(jnp.float32) + own[rows, :].astype(jnp.float32)
                ).astype(jnp.bfloat16)
                down_copy(down).start()

        ready = at - LINE_LAG * jnp.maximum(me, count - 1 - me)

        @pl.when((ready >= 0) & (ready < chunks))
        def _():
            rows = line_chunk(ready, chunk)
            total = (
                from_low[rows, :].astype(jnp.float32)
                + own[rows, :].astype(jnp.float32)
                + from_high[rows, :].astype(jnp.float32)
            )
            emit(rows, total)
            if follow is not None:
                follow(ready)

        return carry

    lax.fori_loop(0, chunks + LINE_LAG * (count - 1), step, 0)

    def drain(index, carry):
        @pl.when(me < count - 1)
        def _():
            up_copy(index).wait_send()

        @pl.when(me > 0)
        def _():
            down_copy(index).wait_send()

        return carry

    lax.fori_loop(0, chunks, drain, 0)


PICK_GROUP = 32
PICK_ALIGN = 8


def pick_kernel(spots, places, table, out, held, sems):
    rows = out.shape[0]
    span = PICK_GROUP * PICK_ALIGN

    def start(group, carry):
        def one(token, carry):
            at = group * PICK_GROUP + token
            pltpu.make_async_copy(
                table.at[pl.ds(pl.multiple_of(spots[at], PICK_ALIGN), PICK_ALIGN)],
                held.at[pl.ds(pl.multiple_of(at * PICK_ALIGN, PICK_ALIGN), PICK_ALIGN)],
                sems.at[group],
            ).start()
            return carry

        return lax.fori_loop(0, PICK_GROUP, one, carry, unroll=8)

    lax.fori_loop(0, rows // PICK_GROUP, start, 0)

    def choose(group, carry):
        block = held.at[pl.ds(pl.multiple_of(group * span, span), span)]
        pltpu.make_async_copy(table.at[pl.ds(0, span)], block, sems.at[group]).wait()
        here = line_chunk(group, PICK_GROUP)
        wanted = places[here, :]
        column = lax.broadcasted_iota(jnp.int32, (PICK_GROUP, span), 1)
        chosen = jnp.where(column == wanted, 1.0, 0.0).astype(jnp.bfloat16)
        out[here, :] = jnp.dot(
            chosen, block[...], preferred_element_type=jnp.float32
        ).astype(jnp.bfloat16)
        return carry

    lax.fori_loop(0, rows // PICK_GROUP, choose, 0)


def pick_call(index, table, name):
    rows = index.shape[0]
    vocab, width = table.shape
    spread = (lax.iota(jnp.int32, rows) * PICK_ALIGN) % (vocab - PICK_ALIGN)
    safe = jnp.where((index >= 0) & (index < vocab), index, spread)
    spots = safe - safe % PICK_ALIGN
    column = index.reshape(rows, 1)
    token = lax.broadcasted_iota(jnp.int32, (rows, 1), 0) % PICK_GROUP
    places = jnp.where(
        (column >= 0) & (column < vocab), token * PICK_ALIGN + column % PICK_ALIGN, -1
    )
    return pl.pallas_call(
        pick_kernel,
        name=name,
        in_specs=[
            pl.BlockSpec(memory_space=pltpu.SMEM),
            pl.BlockSpec(memory_space=pltpu.VMEM),
            pl.BlockSpec(memory_space=pl.ANY),
        ],
        out_specs=pl.BlockSpec(memory_space=pltpu.VMEM),
        out_shape=jax.ShapeDtypeStruct((rows, width), jnp.bfloat16),
        scratch_shapes=[
            pltpu.VMEM((rows * PICK_ALIGN, width), jnp.bfloat16),
            pltpu.SemaphoreType.DMA((rows // PICK_GROUP,)),
        ],
        compiler_params=pltpu.CompilerParams(vmem_limit_bytes=VMEM_LIMIT),
        cost_estimate=pl.CostEstimate(
            flops=2 * rows * PICK_GROUP * PICK_ALIGN * width,
            bytes_accessed=2 * rows * PICK_ALIGN * width,
            transcendentals=0,
        ),
    )(spots, places, table)


LINE_CHUNK = 32
LINE_LAG = 3
WORK_ROWS = 256


def line_scratch(length, width):
    chunks = length // LINE_CHUNK
    return [pltpu.VMEM((length, width), jnp.bfloat16)] * 4 + [
        pltpu.SemaphoreType.DMA((chunks,))
    ] * 4


def line_call(kernel, name, collective_id, outs, scratch, operands, flops=0, spaces=()):
    size = sum(o.size * o.dtype.itemsize for o in operands) + sum(
        o.size * o.dtype.itemsize for o in outs
    )
    vmem = pl.BlockSpec(memory_space=pltpu.VMEM)
    return pl.pallas_call(
        kernel,
        name=name,
        out_shape=outs,
        in_specs=[vmem] * (len(operands) - len(spaces))
        + [pl.BlockSpec(memory_space=space) for space in spaces],
        out_specs=[vmem] * len(outs),
        scratch_shapes=scratch,
        compiler_params=pltpu.CompilerParams(
            collective_id=collective_id, has_side_effects=True, vmem_limit_bytes=VMEM_LIMIT
        ),
        cost_estimate=pl.CostEstimate(
            flops=flops, bytes_accessed=size + 100_000_000, transcendentals=0
        ),
    )(*operands)


def start_kernel(
    count,
    part,
    gain,
    shift,
    bias,
    master,
    w_qkv,
    w_in,
    w_down,
    rows_out,
    attn_out,
    base_out,
    ffn_out,
    pool_out,
    *scratch,
):
    (normed, held_qkv, turned, held_in, held_down, sems, pool, near_out, near_in, far_out, far_in) = (
        scratch[8:]
    )
    shards = pool.shape[0]
    splits = shards.bit_length() - 1
    me = lax.axis_index("dp")
    lane = lax.axis_index("mp")
    mates = [me + 2**k * (1 - 2 * ((me // 2**k) % 2)) for k in range(splits)]
    peers = [lax.rem(lane + offset, count) for offset in range(count)]
    barrier = pltpu.get_barrier_semaphore()
    for mate in mates:
        pl.semaphore_signal(barrier, inc=1, device_id={"dp": mate, "mp": lane}, device_id_type=MESH)
    for peer in peers[1:]:
        pl.semaphore_signal(barrier, inc=1, device_id={"dp": me, "mp": peer}, device_id_type=MESH)
    pl.semaphore_wait(barrier, splits + count - 1)
    pool[me, lane] = master[...].astype(jnp.bfloat16)

    def near(offset):
        return pltpu.make_async_remote_copy(
            src_ref=pool.at[me, lane],
            dst_ref=pool.at[me, lane],
            send_sem=near_out.at[offset],
            recv_sem=near_in.at[offset],
            device_id={"dp": me, "mp": peers[offset]},
            device_id_type=MESH,
        )

    def far(stage):
        bit = splits - 1 - stage
        copies = []
        for place in range(2**stage):
            slot = lax.rem(me, 2 ** (bit + 1)) + place * 2 ** (bit + 1)
            copies.append(
                pltpu.make_async_remote_copy(
                    src_ref=pool.at[slot],
                    dst_ref=pool.at[slot],
                    send_sem=far_out.at[2**stage - 1 + place],
                    recv_sem=far_in.at[2**stage - 1 + place],
                    device_id={"dp": mates[bit], "mp": lane},
                    device_id_type=MESH,
                )
            )
        return copies

    for offset in range(1, count):
        near(offset).start()

    first, last = 6, part.shape[0] // LINE_CHUNK + 2
    waits = (
        [first]
        + [
            first + (last - first) * (2 ** (stage + 1) - 1) // max(1, 2 ** (splits - 1) - 1)
            for stage in range(splits - 1)
        ]
        + [last + 6]
    )

    def prepare(at):
        for stage in range(splits + 1):

            @pl.when(at == waits[stage])
            def _(stage=stage):
                if stage == 0:
                    for offset in range(1, count):
                        near(offset).wait_recv()
                else:
                    for copy in far(stage - 1):
                        copy.wait_recv()
                if stage < splits:
                    for copy in far(stage):
                        copy.start()

    loads = [
        pltpu.make_async_copy(src, dst, sems.at[slot])
        for slot, (src, dst) in enumerate(
            ((w_qkv, held_qkv), (w_in, held_in), (w_down, held_down))
        )
    ]
    for load in loads:
        load.start()

    def emit(rows, total):
        rows_out[rows, :] = total.astype(jnp.bfloat16)
        centre = total - jnp.mean(total, -1, keepdims=True)
        spread = jnp.mean(centre * centre, -1, keepdims=True)
        base = centre * lax.rsqrt(spread + NORM_EPS)
        attn_out[rows, :] = (base * gain[0:1, :] + shift[0:1, :]).astype(jnp.bfloat16)
        normed[rows, :] = (base * gain[1:2, :] + shift[1:2, :]).astype(jnp.bfloat16)

    per = WORK_ROWS // LINE_CHUNK

    def follow(ready):
        @pl.when(ready == per - 1)
        def _():
            for load in loads:
                load.wait()
            heads = held_qkv.shape[1] // (3 * HD)
            for kind in range(3):
                for head in range(heads):
                    into = (kind * heads + head) * HD
                    source = (head * 3 + kind) * HD
                    turned[:, into : into + HD] = held_qkv[:, source : source + HD]

        @pl.when(lax.rem(ready, per) == per - 1)
        def _():
            rows = line_chunk(ready // per, WORK_ROWS)
            base_out[rows, :] = jnp.dot(
                attn_out[rows, :], turned[...], preferred_element_type=jnp.float32
            )
            pre = (
                jnp.dot(normed[rows, :], held_in[...], preferred_element_type=jnp.float32)
                + bias[...]
            )
            hidden = (0.5 * pre * (1.0 + lax.erf(pre * 0.5**0.5))).astype(jnp.bfloat16)
            ffn_out[rows, :] = jnp.dot(
                hidden, held_down[...], preferred_element_type=jnp.float32
            ).astype(jnp.bfloat16)

    line_sum(
        count,
        LINE_CHUNK,
        part,
        scratch[:4],
        scratch[4:8],
        prepare,
        emit,
        greet=False,
        follow=follow,
        always=True,
    )
    pool_out[...] = pool[...]
    for offset in range(1, count):
        near(offset).wait_send()
    for stage in range(splits):
        for copy in far(stage):
            copy.wait_send()


def turn_pairs(field, cosine, sine, sign):
    lane = lax.broadcasted_iota(jnp.int32, field.shape, 1) % HD
    half = ROT // 2
    other = jnp.where(
        lane < half, pltpu.roll(field, field.shape[1] - half, 1), pltpu.roll(field, half, 1)
    )
    return field * cosine + sign * other * sine


CROSS = (((1,), (1,)), ((), ()))


def resid_kernel(
    count,
    attn,
    base,
    ffn,
    start,
    gain,
    shift,
    cosine,
    sine,
    down_qkv,
    up_q,
    up_k,
    up_v,
    down_out,
    up_out,
    w_out,
    inner_out,
    query_out,
    key_out,
    value_out,
    context_out,
    spread_out,
    low_out,
    resid_out,
    final_out,
    *scratch,
):
    own = scratch[8]
    group = w_out.shape[0]
    total_rows = own.shape[0]
    key_out[...] = jnp.zeros_like(key_out)
    value_out[...] = jnp.zeros_like(value_out)

    def attend(block):
        rows = line_chunk(block, WORK_ROWS)
        low = jnp.dot(
            attn[rows, :], down_qkv[...], preferred_element_type=jnp.float32
        ).astype(jnp.bfloat16)
        inner_out[rows, :] = low
        for kind, (up, out) in enumerate(
            ((up_q, query_out), (up_k, key_out), (up_v, value_out))
        ):
            extra = lax.dot_general(
                low[:, kind * R : (kind + 1) * R],
                up[...],
                CROSS,
                preferred_element_type=jnp.float32,
            )
            for at in range(0, group, 128):
                field = base[rows, kind * group + at : kind * group + at + 128]
                field = field + extra[:, at : at + 128]
                if kind < 2:
                    field = turn_pairs(field, cosine[rows, :], sine[rows, :], 1.0)
                out[rows, at : at + 128] = field.astype(jnp.bfloat16)
        lane = lax.broadcasted_iota(jnp.int32, (WORK_ROWS, 128), 1)
        column = lax.broadcasted_iota(jnp.int32, (WORK_ROWS, total_rows), 1)
        place = lax.broadcasted_iota(jnp.int32, (WORK_ROWS, total_rows), 0)
        seen = column <= place + block * WORK_ROWS
        spreads = jnp.zeros((WORK_ROWS, 128), jnp.float32)
        for at in range(0, group, 128):
            pair = query_out[rows, at : at + 128]
            keys = key_out[:, at : at + 128]
            values = value_out[:, at : at + 128]
            results = []
            for side in range(128 // HD):
                mine = jnp.where(lane // HD == side, pair, jnp.zeros_like(pair))
                scores = (
                    lax.dot_general(mine, keys, CROSS, preferred_element_type=jnp.float32)
                    * HD**-0.5
                )
                scores = jnp.where(seen, scores, -1e30)
                top = jnp.max(scores, -1, keepdims=True)
                weights = jnp.exp(scores - top)
                total = jnp.sum(weights, -1, keepdims=True)
                probs = (weights * (1.0 / total)).astype(jnp.bfloat16)
                results.append(jnp.dot(probs, values, preferred_element_type=jnp.float32))
                head = at // HD + side
                spreads = jnp.where(lane == head, top + jnp.log(total), spreads)
            joined = results[0]
            for side in range(1, 128 // HD):
                joined = jnp.where(lane // HD == side, results[side], joined)
            context_out[rows, at : at + 128] = joined.astype(jnp.bfloat16)
        spread_out[rows, :] = spreads
        context = context_out[rows, :]
        low = jnp.dot(context, down_out[...], preferred_element_type=jnp.float32).astype(
            jnp.bfloat16
        )
        low_out[rows, :] = low
        own[rows, :] = (
            jnp.dot(context, w_out[...], preferred_element_type=jnp.float32)
            + lax.dot_general(low, up_out[...], CROSS, preferred_element_type=jnp.float32)
            + ffn[rows, :].astype(jnp.float32)
        ).astype(jnp.bfloat16)

    per = WORK_ROWS // LINE_CHUNK

    def prepare(at):
        @pl.when(lax.rem(at, per) == 0)
        def _():
            attend(at // per)

    def emit(rows, total):
        resid = start[rows, :].astype(jnp.float32) + total
        resid_out[rows, :] = resid
        normed = layer_norm(resid, gain[2:3, :], shift[2:3, :])
        final_out[rows, :] = normed.astype(jnp.bfloat16)

    line_sum(count, LINE_CHUNK, own, scratch[:4], scratch[4:8], prepare, emit)


def branch_kernel(
    count, raw, hits, stats, resid, gain, prompts, totals, out, loss_out, *scratch
):
    own, note_send, note_recv, scales, note_out, note_in = scratch[8:]
    me = lax.axis_index("mp")
    rows_all = raw.shape[0]
    greet_peers(me, count)
    note_send[...] = stats[...].T[0:8, :]
    copies = []
    for offset in range(1, count):
        copy = pltpu.make_async_remote_copy(
            src_ref=note_send,
            dst_ref=note_recv.at[offset],
            send_sem=note_out.at[offset],
            recv_sem=note_in.at[offset],
            device_id={"mp": lax.rem(me + offset, count)},
            device_id_type=MESH,
        )
        copy.start()
        copies.append(copy)
    mine = note_send[...]
    for copy in copies:
        copy.wait_recv()
    others = [mine] + [note_recv[offset] for offset in range(1, count)]
    top = functools.reduce(jnp.maximum, [part[0:1, :] for part in others])
    total = sum(part[1:2, :] * jnp.exp(part[0:1, :] - top) for part in others)
    found = sum(part[2:3, :] for part in others)
    spread_row = top + jnp.log(total)
    amount = sum(totals[e] - prompts[e] for e in range(prompts.shape[0]))
    example = lax.axis_index("dp")
    position = lax.broadcasted_iota(jnp.int32, (1, rows_all), 1)
    keep = (position >= prompts[example] - 1) & (position < totals[example] - 1)
    share = jnp.where(keep, 1.0 / jnp.broadcast_to(amount, (1, rows_all)).astype(jnp.float32), 0.0)
    loss_out[...] = (spread_row - found) * share
    factor = jnp.exp(mine[0:1, :] - spread_row) * share
    pair = jnp.concatenate([factor, share, jnp.zeros((126, rows_all), jnp.float32)], 0)
    scales[...] = pair.T

    def prepare(at):
        rows = line_chunk(at, LINE_CHUNK)
        scale = scales[rows, :]
        own[rows, :] = (
            raw[rows, :] * scale[:, 0:1] - hits[rows, :].astype(jnp.float32) * scale[:, 1:2]
        ).astype(jnp.bfloat16)

    def emit(rows, total):
        values = resid[rows, :]
        centre = values - jnp.mean(values, -1, keepdims=True)
        spread = jnp.mean(centre * centre, -1, keepdims=True)
        inverse = lax.rsqrt(spread + NORM_EPS)
        normed = centre * inverse
        up = total * gain[2:3, :]
        out[rows, :] = (
            inverse
            * (
                up
                - jnp.mean(up, -1, keepdims=True)
                - normed * jnp.mean(up * normed, -1, keepdims=True)
            )
        ).astype(jnp.bfloat16)

    line_sum(count, LINE_CHUNK, own, scratch[:4], scratch[4:8], prepare, emit, greet=False)
    for copy in copies:
        copy.wait_send()


def loss_kernel(vocab, tile, values, ahead, behind, hits, acc, stats, logits, probs, tops, sums):
    at = pl.program_id(0)
    tiles = pl.num_programs(0) - 1
    rows_all = values.shape[0]

    @pl.when(at == 0)
    def _():
        acc[...] = jnp.zeros_like(acc)
        tops[...] = jnp.full_like(tops, -1e29)
        sums[...] = jnp.zeros_like(sums)
        logits[...] = jnp.full_like(logits, -1e30)

    tail = vocab % tile
    if tail:

        @pl.when(at >= tiles - 1)
        def _():
            ahead[tail:, :] = jnp.zeros((tile - tail, ahead.shape[1]), ahead.dtype)

        @pl.when(at >= tiles)
        def _():
            behind[tail:, :] = jnp.zeros((tile - tail, behind.shape[1]), behind.dtype)

    ids = (at - 1) * tile + lax.broadcasted_iota(jnp.int32, (1, tile), 1)
    scores = logits[...] + jnp.where(ids < vocab, 0.0, -1e30)
    old = tops[:, 0:1]
    new = jnp.maximum(old, jnp.max(scores, -1, keepdims=True))
    weights = jnp.exp(scores - new)
    shrink = jnp.exp(old - new)
    sums[...] = sums[...] * shrink + jnp.sum(weights, -1, keepdims=True)
    tops[...] = jnp.broadcast_to(new, tops.shape)
    acc[...] = acc[...] * shrink
    probs[...] = weights.astype(jnp.bfloat16)
    logits[...] = lax.dot_general(
        values[...], ahead[...], (((1,), (1,)), ((), ())), preferred_element_type=jnp.float32
    )
    acc[...] += jnp.dot(probs[...], behind[...], preferred_element_type=jnp.float32)

    @pl.when(at == tiles)
    def _():
        found = jnp.sum(
            values[...].astype(jnp.float32) * hits[...].astype(jnp.float32), -1, keepdims=True
        )
        column = lax.broadcasted_iota(jnp.int32, (rows_all, 128), 1)
        stats[...] = jnp.where(
            column == 0, tops[...], jnp.where(column == 1, sums[...], found)
        )


LOSS_TILE = 512


def loss_call(values, head_rows, hits):
    rows, width = values.shape
    vocab = head_rows.shape[0]
    tile = LOSS_TILE
    tiles = pl.cdiv(vocab, tile)
    whole = pl.BlockSpec((rows, width), lambda j: (0, 0))
    return pl.pallas_call(
        functools.partial(loss_kernel, vocab, tile),
        name="loss",
        grid=(tiles + 1,),
        in_specs=[
            whole,
            pl.BlockSpec((tile, width), lambda j: (jnp.minimum(j, tiles - 1), 0)),
            pl.BlockSpec((tile, width), lambda j: (jnp.maximum(j - 1, 0), 0)),
            whole,
        ],
        out_specs=[whole, pl.BlockSpec((rows, 128), lambda j: (0, 0))],
        out_shape=[
            jax.ShapeDtypeStruct((rows, width), jnp.float32),
            jax.ShapeDtypeStruct((rows, 128), jnp.float32),
        ],
        scratch_shapes=[
            pltpu.VMEM((rows, tile), jnp.float32),
            pltpu.VMEM((rows, tile), jnp.bfloat16),
            pltpu.VMEM((rows, 128), jnp.float32),
            pltpu.VMEM((rows, 128), jnp.float32),
        ],
        compiler_params=pltpu.CompilerParams(vmem_limit_bytes=VMEM_LIMIT),
        cost_estimate=pl.CostEstimate(
            flops=4 * rows * width * vocab,
            bytes_accessed=4 * width * vocab,
            transcendentals=rows * vocab,
        ),
    )(values, head_rows, head_rows, hits)


def fold_kernel(splits, count, *refs):
    fulls = refs[0:4]
    groups = refs[4:8]
    losses, master, first, second, bases = refs[8:13]
    loss_out, norm_out, first_out, second_out, master_out = refs[13:18]
    scratch = refs[18:]
    sends = scratch[0:splits]
    recvs = scratch[splits : 2 * splits]
    keeps = scratch[2 * splits : 3 * splits]
    (line_send, line_recv, turn_send, turn_recv, note_send, note_recv, tell_send, tell_recv) = scratch[
        3 * splits : 3 * splits + 8
    ]
    (half_out, half_in, line_out, line_in, turn_out, turn_in, note_out, note_in, tell_out, tell_in) = (
        scratch[3 * splits + 8 :]
    )
    shards = 2**splits
    me = lax.axis_index("dp")
    lane = lax.axis_index("mp")
    full_rows = fulls[0].shape[0] // shards
    group_rows = groups[0].shape[0] // shards
    own_rows = full_rows // count
    bits = [(me // 2**k) % 2 for k in range(splits)]
    mates = [me + 2**k * (1 - 2 * bits[k]) for k in range(splits)]
    peers = [lax.rem(lane + offset, count) for offset in range(count)]
    spot = lane * shards + me
    goal = (spot // count, lax.rem(spot, count))
    place = me * count + lane
    origin = (lax.rem(place, shards), place // shards)
    moved = spot != place

    barrier = pltpu.get_barrier_semaphore()
    for mate in mates:
        pl.semaphore_signal(barrier, inc=1, device_id={"dp": mate, "mp": lane}, device_id_type=MESH)
    for peer in peers[1:]:
        pl.semaphore_signal(barrier, inc=1, device_id={"dp": me, "mp": peer}, device_id_type=MESH)

    @pl.when(moved)
    def _():
        for device in (goal, origin):
            pl.semaphore_signal(
                barrier, inc=1, device_id={"dp": device[0], "mp": device[1]}, device_id_type=MESH
            )

    pl.semaphore_wait(barrier, splits + count - 1 + jnp.where(moved, 2, 0))

    def remote(src, dst, out_sem, in_sem, device):
        return pltpu.make_async_remote_copy(
            src_ref=src,
            dst_ref=dst,
            send_sem=out_sem,
            recv_sem=in_sem,
            device_id={"dp": device[0], "mp": device[1]},
            device_id_type=MESH,
        )

    def piece(index):
        whole = pl.ds(pl.multiple_of(index * full_rows, full_rows), full_rows)
        part = pl.ds(pl.multiple_of(index * group_rows, group_rows), group_rows)
        return jnp.concatenate(
            [ref[whole, :] for ref in fulls] + [ref[part, :] for ref in groups], 0
        )

    started = []
    current = piece
    for k in range(splits):
        half = shards >> (k + 1)
        for i in range(half):
            sends[k][i] = current(2 * i + 1 - bits[k]).astype(jnp.bfloat16)
        copy = remote(sends[k], recvs[k], half_out.at[k], half_in.at[k], (mates[k], lane))
        copy.start()
        started.append(copy)
        for i in range(half):
            keeps[k][i] = current(2 * i + bits[k])
        copy.wait_recv()
        current = functools.partial(
            lambda kept, came, i: kept[i] + came[i].astype(jnp.float32), keeps[k], recvs[k]
        )
    final = keeps[splits - 1]
    final[0] = current(0)

    def chosen(peer):
        return jnp.concatenate(
            [
                final[
                    0,
                    pl.ds(pl.multiple_of(a * full_rows + peer * own_rows, own_rows), own_rows),
                    :,
                ]
                for a in range(4)
            ],
            0,
        )

    turn_send[...] = final[0, 4 * full_rows :, :].astype(jnp.bfloat16)
    turn = remote(turn_send, turn_recv, turn_out, turn_in, goal)

    @pl.when(moved)
    def _():
        turn.start()

    for offset in range(1, count):
        line_send[offset] = chosen(peers[offset]).astype(jnp.bfloat16)
        copy = remote(
            line_send.at[offset],
            line_recv.at[offset],
            line_out.at[offset],
            line_in.at[offset],
            (me, peers[offset]),
        )
        copy.start()
        started.append(copy)
    total = chosen(lane)

    @pl.when(moved)
    def _():
        turn.wait()

    @pl.when(jnp.logical_not(moved))
    def _():
        turn_recv[...] = turn_send[...]

    for copy in started[splits:]:
        copy.wait_recv()
    for offset in range(1, count):
        total = total + line_recv[offset].astype(jnp.float32)
    part = turn_recv[...].astype(jnp.float32)

    column = lax.broadcasted_iota(jnp.int32, (8, 128), 1)
    row = lax.broadcasted_iota(jnp.int32, (8, 128), 0)
    squares = jnp.sum(total * total) + jnp.sum(part * part)
    spot_norm = (row == 0) & (column == 0)
    spot_loss = (row == 0) & (column == 1)
    note = jnp.where(spot_norm, squares, 0.0) + jnp.where(spot_loss, jnp.sum(losses[...]), 0.0)

    def rows_of(index):
        source, slot = (total, (0, 1, 2, 7).index(index)) if index in (0, 1, 2, 7) else (
            part,
            index - 3,
        )
        return source[slot * own_rows : (slot + 1) * own_rows, :]

    turned = [
        jnp.dot(
            rows_of(m), bases[m], precision=HIGH_PRECISION, preferred_element_type=jnp.float32
        )
        for m in range(8)
    ]
    for k in range(splits):
        note_send[k] = note
        copy = remote(
            note_send.at[k], note_recv.at[k], note_out.at[k], note_in.at[k], (mates[k], lane)
        )
        copy.start()
        started.append(copy)
        copy.wait_recv()
        note = note + note_recv[k]
    tell_send[...] = note
    tells = []
    for offset in range(1, count):
        copy = remote(
            tell_send,
            tell_recv.at[offset],
            tell_out.at[offset],
            tell_in.at[offset],
            (me, peers[offset]),
        )
        copy.start()
        tells.append(copy)
    for copy in tells:
        copy.wait_recv()
    everything = note
    for offset in range(1, count):
        everything = everything + tell_recv[offset]
    norm = jnp.sqrt(jnp.sum(jnp.where(spot_norm, everything, 0.0), keepdims=True))
    loss_out[...] = jnp.sum(jnp.where(spot_loss, note, 0.0), keepdims=True)
    norm_out[...] = norm
    factor = jnp.minimum(1.0, CLIP_LIMIT / norm)
    for m in range(8):
        rotated = turned[m] * factor
        new_first = BETA_FIRST * first[m] + (1.0 - BETA_FIRST) * rotated
        new_second = BETA_SECOND * second[m] + (1.0 - BETA_SECOND) * rotated * rotated
        first_out[m] = new_first
        second_out[m] = new_second
        normed = (
            new_first
            / (1.0 - BETA_FIRST**ADAM_STEP)
            / (jnp.sqrt(new_second / (1.0 - BETA_SECOND**ADAM_STEP)) + ADAM_EPS)
        )
        back = lax.dot_general(
            normed,
            bases[m],
            (((1,), (1,)), ((), ())),
            precision=HIGH_PRECISION,
            preferred_element_type=jnp.float32,
        )
        master_out[m] = master[m] - LEARN_RATE * (back + DECAY_RATE * master[m])
    for copy in started + tells:
        copy.wait_send()


def fold_call(fulls, groups, losses, master, first_moment, second_moment, bases):
    shards = lax.axis_size("dp")
    count = lax.axis_size("mp")
    splits = shards.bit_length() - 1
    width = fulls[0].shape[1]
    pile = 4 * (fulls[0].shape[0] + groups[0].shape[0]) // shards
    own = 4 * fulls[0].shape[0] // (shards * count)
    low = jnp.bfloat16
    halves = [shards >> (k + 1) for k in range(splits)]
    dma = pltpu.SemaphoreType.DMA
    scratch = (
        [pltpu.VMEM((half, pile, width), low) for half in halves] * 2
        + [pltpu.VMEM((half, pile, width), jnp.float32) for half in halves]
        + [pltpu.VMEM((count, own, width), low)] * 2
        + [pltpu.VMEM((4 * groups[0].shape[0] // shards, width), low)] * 2
        + [pltpu.VMEM((splits, 8, 128), jnp.float32)] * 2
        + [pltpu.VMEM((8, 128), jnp.float32), pltpu.VMEM((count, 8, 128), jnp.float32)]
        + [dma((splits,))] * 2
        + [dma((count,))] * 2
        + [dma(())] * 2
        + [dma((splits,))] * 2
        + [dma((count,))] * 2
    )
    scalar = jax.ShapeDtypeStruct((1, 1), jnp.float32)
    state = jax.ShapeDtypeStruct(master.shape, jnp.float32)
    return line_call(
        functools.partial(fold_kernel, splits, count),
        "fold",
        3,
        [scalar, scalar, state, state, state],
        scratch,
        [*fulls, *groups, losses, master, first_moment, second_moment, bases],
    )


def per_device(
    token_ids,
    prompt_len,
    example_len,
    embedding,
    w_qkv,
    w_out,
    w_in,
    b_in,
    w_down,
    unembed,
    ln_gain,
    ln_bias,
    master,
    first_moment,
    second_moment,
    eigen_bases,
):
    group_count = lax.axis_size("mp")
    group_index = lax.axis_index("mp")
    head_rows = lax.all_gather(unembed.T, "dp", axis=1, tiled=True)
    examples, length = token_ids.shape
    width = embedding.shape[0]
    vocab_local = head_rows.shape[0]
    rows = examples * length
    local_heads = HEADS // group_count
    group_width = local_heads * HD
    flat_ids = token_ids.reshape(rows)
    picked = pick_call(flat_ids - group_index * width, embedding, "pick_start")
    shape_low = jax.ShapeDtypeStruct((rows, D), jnp.bfloat16)
    shape_wide = jax.ShapeDtypeStruct((rows, D), jnp.float32)
    shards = lax.axis_size("dp")
    own_rows = master.shape[1]
    pool_shape = (shards, group_count, 8, own_rows, R)
    start_rows, normed_attn, base, ffn_part, pool = line_call(
        functools.partial(start_kernel, group_count),
        "start_rows",
        0,
        [
            shape_low,
            shape_low,
            jax.ShapeDtypeStruct((rows, w_qkv.shape[1]), jnp.float32),
            shape_low,
            jax.ShapeDtypeStruct(pool_shape, jnp.bfloat16),
        ],
        line_scratch(rows, D)
        + [
            pltpu.VMEM((rows, D), jnp.bfloat16),
            pltpu.VMEM(w_qkv.shape, jnp.bfloat16),
            pltpu.VMEM(w_qkv.shape, jnp.bfloat16),
            pltpu.VMEM(w_in.shape, jnp.bfloat16),
            pltpu.VMEM(w_down.shape, jnp.bfloat16),
            pltpu.SemaphoreType.DMA((3,)),
            pltpu.VMEM(pool_shape, jnp.bfloat16),
        ]
        + [pltpu.SemaphoreType.DMA((group_count,))] * 2
        + [pltpu.SemaphoreType.DMA((shards - 1,))] * 2,
        [picked, ln_gain, ln_bias, b_in.reshape(1, -1), master, w_qkv, w_in, w_down],
        spaces=(pl.ANY,) * 3,
    )
    adapters = pool.transpose(2, 0, 1, 3, 4).reshape(8, -1, R)
    target = jnp.roll(token_ids, -1, axis=1).reshape(rows)
    adapter_rows = [
        lax.dynamic_slice_in_dim(
            adapters[3 + selector_index], group_index * group_width, group_width, 0
        )
        for selector_index in range(3)
    ]
    out_rows = lax.dynamic_slice_in_dim(adapters[6], group_index * group_width, group_width, 0)
    cosine, sine = rope_tables(length)
    rest = jnp.zeros((length, HD - ROT), jnp.float32)
    wide_cosine = jnp.concatenate([cosine[:, 0], cosine[:, 0], rest + 1.0] * (128 // HD), 1)
    wide_sine = jnp.concatenate([-sine[:, 0], sine[:, 0], rest] * (128 // HD), 1)
    shape_group = jax.ShapeDtypeStruct((rows, group_width), jnp.bfloat16)
    (
        inner,
        queries,
        key_rows,
        value_rows,
        context,
        spread_lanes,
        inner_out,
        resid,
        final_rows,
    ) = line_call(
        functools.partial(resid_kernel, group_count),
        "resid_rows",
        1,
        [
            jax.ShapeDtypeStruct((rows, 3 * R), jnp.bfloat16),
            shape_group,
            shape_group,
            shape_group,
            shape_group,
            jax.ShapeDtypeStruct((rows, 128), jnp.float32),
            jax.ShapeDtypeStruct((rows, R), jnp.bfloat16),
            shape_wide,
            shape_low,
        ],
        line_scratch(rows, D) + [pltpu.VMEM((rows, D), jnp.bfloat16)],
        [
            normed_attn,
            base,
            ffn_part,
            start_rows,
            ln_gain,
            ln_bias,
            wide_cosine,
            wide_sine,
            jnp.concatenate([adapters[0], adapters[1], adapters[2]], 1),
            *adapter_rows,
            out_rows,
            adapters[7],
            w_out,
        ],
    )
    queries = queries.reshape(1, length, local_heads, HD)
    key_rows = key_rows.reshape(1, length, local_heads, HD)
    value_rows = value_rows.reshape(1, length, local_heads, HD)
    spreads = [spread_lanes[:, :local_heads].T]
    goal = target - group_index * vocab_local
    hits = pick_call(goal, head_rows, "pick_target")
    raw_grad, stats = loss_call(final_rows, head_rows, hits)
    branch_grad, losses = line_call(
        functools.partial(branch_kernel, group_count),
        "branch_rows",
        2,
        [shape_low, jax.ShapeDtypeStruct((1, rows), jnp.float32)],
        line_scratch(rows, D)
        + [
            pltpu.VMEM((rows, D), jnp.bfloat16),
            pltpu.VMEM((8, rows), jnp.float32),
            pltpu.VMEM((group_count, 8, rows), jnp.float32),
            pltpu.VMEM((rows, 128), jnp.float32),
            pltpu.SemaphoreType.DMA((group_count,)),
            pltpu.SemaphoreType.DMA((group_count,)),
        ],
        [raw_grad, hits, stats, resid, ln_gain, prompt_len, example_len],
        spaces=(pltpu.SMEM,) * 2,
    )
    inner_out_grad = jnp.dot(branch_grad, adapters[7], preferred_element_type=jnp.float32).astype(
        jnp.bfloat16
    )
    grad_out_b = jnp.einsum("ld,lr->dr", branch_grad, inner_out, preferred_element_type=jnp.float32)
    grad_out_a = jnp.einsum(
        "ld,lr->dr", context, inner_out_grad, preferred_element_type=jnp.float32
    )
    context_grad = jnp.einsum(
        "ld,ed->le", branch_grad, w_out, preferred_element_type=jnp.float32
    ) + jnp.einsum("lr,dr->ld", inner_out_grad, out_rows, preferred_element_type=jnp.float32)
    context_grad = context_grad.astype(jnp.bfloat16).reshape(examples, length, local_heads, HD)
    sample = 0
    query_grad, key_grad, value_grad = attend_back(
        queries[sample], key_rows[sample], value_rows[sample], spreads[sample], context_grad[sample]
    )
    query_parts = [rotate_back(query_grad, cosine, sine)]
    key_parts = [rotate_back(key_grad, cosine, sine)]
    value_parts = [value_grad]
    pre_grads = [
        parts[0].reshape(rows, group_width).astype(jnp.bfloat16)
        for parts in (query_parts, key_parts, value_parts)
    ]
    complete_gradients = []
    local_grads = []
    for selector_index in range(3):
        projected_values = jnp.einsum(
            "ld,le->de", normed_attn, pre_grads[selector_index], preferred_element_type=jnp.float32
        )
        complete_gradients.append(
            jnp.dot(
                projected_values,
                adapter_rows[selector_index].astype(jnp.float32),
                precision=HIGH_PRECISION,
            )
        )
        local_grads.append(
            jnp.einsum(
                "ld,lr->dr",
                pre_grads[selector_index],
                inner[:, selector_index * R : (selector_index + 1) * R],
                preferred_element_type=jnp.float32,
            )
        )
    local_grads.append(grad_out_a)
    mean_loss, grad_norm, new_first, new_second, new_master = fold_call(
        [*complete_gradients, grad_out_b],
        local_grads,
        losses,
        master,
        first_moment,
        second_moment,
        eigen_bases,
    )
    return (mean_loss.reshape(()), grad_norm.reshape(()), new_first, new_second, new_master)


def solution(mesh):
    placed = (
        P("dp", None),
        P(),
        P(),
        P("mp", None),
        P(None, "mp"),
        P("mp", None),
        P(None, "mp"),
        P("mp"),
        P("mp", None),
        P("dp", "mp"),
        P(),
        P(),
        P(None, ("dp", "mp"), None),
        P(None, ("dp", "mp"), None),
        P(None, ("dp", "mp"), None),
        P(),
    )
    return jax.shard_map(
        per_device,
        mesh=mesh,
        in_specs=placed,
        out_specs=(
            P(),
            P(),
            P(None, ("dp", "mp"), None),
            P(None, ("dp", "mp"), None),
            P(None, ("dp", "mp"), None),
        ),
        check_vma=False,
    )
```

```python
import functools

import jax
import jax.numpy as jnp
from jax import lax
from jax.experimental import pallas as pl
from jax.experimental.pallas import tpu as pltpu
from jax.sharding import PartitionSpec as P

MESH = pl.DeviceIdType.MESH
VMEM_LIMIT = 60 * 1024 * 1024

D = 1024
HEADS = 16
R = 128
ADAM_STEP = 10
HD = 64
ROT = 16


HIGH_PRECISION = lax.Precision.HIGHEST
NORM_EPS = 1e-05
ROPE_BASE = 10000.0
CLIP_LIMIT = 0.01
LEARN_RATE = 0.02
BETA_FIRST = 0.9
BETA_SECOND = 0.999
ADAM_EPS = 1e-08
DECAY_RATE = 0.01


def layer_norm(values, gain, shift):
    centre = values - jnp.mean(values, -1, keepdims=True)
    spread = jnp.mean(centre * centre, -1, keepdims=True)
    return centre * lax.rsqrt(spread + NORM_EPS) * gain + shift


def rope_tables(length):
    half = ROT // 2
    freqs = ROPE_BASE ** (-2.0 * jnp.arange(half, dtype=jnp.float32) / ROT)
    angles = jnp.arange(length, dtype=jnp.float32)[:, None] * freqs[None, :]
    return (jnp.cos(angles)[:, None, :], jnp.sin(angles)[:, None, :])


def line_chunk(index, size):
    return pl.ds(pl.multiple_of(index * size, size), size)


def greet_line(me, count):
    barrier = pltpu.get_barrier_semaphore()

    @pl.when(me > 0)
    def _():
        pl.semaphore_signal(
            barrier, inc=1, device_id={"mp": jnp.maximum(me - 1, 0)}, device_id_type=MESH
        )

    @pl.when(me < count - 1)
    def _():
        pl.semaphore_signal(
            barrier, inc=1, device_id={"mp": jnp.minimum(me + 1, count - 1)}, device_id_type=MESH
        )

    peers = jnp.where(me > 0, 1, 0) + jnp.where(me < count - 1, 1, 0)
    pl.semaphore_wait(barrier, peers)


def greet_peers(me, count):
    barrier = pltpu.get_barrier_semaphore()
    for offset in range(1, count):
        pl.semaphore_signal(
            barrier, inc=1, device_id={"mp": lax.rem(me + offset, count)}, device_id_type=MESH
        )
    pl.semaphore_wait(barrier, count - 1)


def line_sum(count, chunk, own, wires, sems, prepare, emit, greet=True, follow=None, always=False):
    me = lax.axis_index("mp")
    from_low, from_high, to_high, to_low = wires
    up_send, up_recv, down_send, down_recv = sems
    length = own.shape[0]
    chunks = length // chunk
    above = jnp.minimum(me + 1, count - 1)
    below = jnp.maximum(me - 1, 0)

    def up_copy(index):
        rows = line_chunk(index, chunk)
        return pltpu.make_async_remote_copy(
            src_ref=to_high.at[rows],
            dst_ref=from_low.at[rows],
            send_sem=up_send.at[index],
            recv_sem=up_recv.at[index],
            device_id={"mp": above},
            device_id_type=MESH,
        )

    def down_copy(index):
        rows = line_chunk(index, chunk)
        return pltpu.make_async_remote_copy(
            src_ref=to_low.at[rows],
            dst_ref=from_high.at[rows],
            send_sem=down_send.at[index],
            recv_sem=down_recv.at[index],
            device_id={"mp": below},
            device_id_type=MESH,
        )

    if greet:
        greet_line(me, count)

    @pl.when(me == 0)
    def _():
        from_low[...] = jnp.zeros_like(from_low)

    @pl.when(me == count - 1)
    def _():
        from_high[...] = jnp.zeros_like(from_high)

    def step(at, carry):
        if prepare is not None and always:
            prepare(at)
        elif prepare is not None:

            @pl.when(at < chunks)
            def _():
                prepare(at)

        up = at - LINE_LAG * me

        @pl.when((up >= 0) & (up < chunks))
        def _():
            rows = line_chunk(up, chunk)

            @pl.when(me > 0)
            def _():
                up_copy(up).wait_recv()

            @pl.when(me < count - 1)
            def _():
                to_high[rows, :] = (
                    from_low[rows, :].astype(jnp.float32) + own[rows, :].astype(jnp.float32)
                ).astype(jnp.bfloat16)
                up_copy(up).start()

        down = at - LINE_LAG * (count - 1 - me)

        @pl.when((down >= 0) & (down < chunks))
        def _():
            rows = line_chunk(down, chunk)

            @pl.when(me < count - 1)
            def _():
                down_copy(down).wait_recv()

            @pl.when(me > 0)
            def _():
                to_low[rows, :] = (
                    from_high[rows, :].astype(jnp.float32) + own[rows, :].astype(jnp.float32)
                ).astype(jnp.bfloat16)
                down_copy(down).start()

        ready = at - LINE_LAG * jnp.maximum(me, count - 1 - me)

        @pl.when((ready >= 0) & (ready < chunks))
        def _():
            rows = line_chunk(ready, chunk)
            total = (
                from_low[rows, :].astype(jnp.float32)
                + own[rows, :].astype(jnp.float32)
                + from_high[rows, :].astype(jnp.float32)
            )
            emit(rows, total)
            if follow is not None:
                follow(ready)

        return carry

    lax.fori_loop(0, chunks + LINE_LAG * (count - 1), step, 0)

    def drain(index, carry):
        @pl.when(me < count - 1)
        def _():
            up_copy(index).wait_send()

        @pl.when(me > 0)
        def _():
            down_copy(index).wait_send()

        return carry

    lax.fori_loop(0, chunks, drain, 0)


PICK_GROUP = 32
PICK_ALIGN = 8


def pick_kernel(spots, places, table, out, held, sems):
    rows = out.shape[0]
    span = PICK_GROUP * PICK_ALIGN

    def start(group, carry):
        def one(token, carry):
            at = group * PICK_GROUP + token
            pltpu.make_async_copy(
                table.at[pl.ds(pl.multiple_of(spots[at], PICK_ALIGN), PICK_ALIGN)],
                held.at[pl.ds(pl.multiple_of(at * PICK_ALIGN, PICK_ALIGN), PICK_ALIGN)],
                sems.at[group],
            ).start()
            return carry

        return lax.fori_loop(0, PICK_GROUP, one, carry, unroll=8)

    lax.fori_loop(0, rows // PICK_GROUP, start, 0)

    def choose(group, carry):
        block = held.at[pl.ds(pl.multiple_of(group * span, span), span)]
        pltpu.make_async_copy(table.at[pl.ds(0, span)], block, sems.at[group]).wait()
        here = line_chunk(group, PICK_GROUP)
        wanted = places[here, :]
        column = lax.broadcasted_iota(jnp.int32, (PICK_GROUP, span), 1)
        chosen = jnp.where(column == wanted, 1.0, 0.0).astype(jnp.bfloat16)
        out[here, :] = jnp.dot(
            chosen, block[...], preferred_element_type=jnp.float32
        ).astype(jnp.bfloat16)
        return carry

    lax.fori_loop(0, rows // PICK_GROUP, choose, 0)


def pick_call(index, table, name):
    rows = index.shape[0]
    vocab, width = table.shape
    spread = (lax.iota(jnp.int32, rows) * PICK_ALIGN) % (vocab - PICK_ALIGN)
    safe = jnp.where((index >= 0) & (index < vocab), index, spread)
    spots = safe - safe % PICK_ALIGN
    column = index.reshape(rows, 1)
    token = lax.broadcasted_iota(jnp.int32, (rows, 1), 0) % PICK_GROUP
    places = jnp.where(
        (column >= 0) & (column < vocab), token * PICK_ALIGN + column % PICK_ALIGN, -1
    )
    return pl.pallas_call(
        pick_kernel,
        name=name,
        in_specs=[
            pl.BlockSpec(memory_space=pltpu.SMEM),
            pl.BlockSpec(memory_space=pltpu.VMEM),
            pl.BlockSpec(memory_space=pl.ANY),
        ],
        out_specs=pl.BlockSpec(memory_space=pltpu.VMEM),
        out_shape=jax.ShapeDtypeStruct((rows, width), jnp.bfloat16),
        scratch_shapes=[
            pltpu.VMEM((rows * PICK_ALIGN, width), jnp.bfloat16),
            pltpu.SemaphoreType.DMA((rows // PICK_GROUP,)),
        ],
        compiler_params=pltpu.CompilerParams(vmem_limit_bytes=VMEM_LIMIT),
        cost_estimate=pl.CostEstimate(
            flops=2 * rows * PICK_GROUP * PICK_ALIGN * width,
            bytes_accessed=2 * rows * PICK_ALIGN * width,
            transcendentals=0,
        ),
    )(spots, places, table)


LINE_CHUNK = 32
LINE_LAG = 3
WORK_ROWS = 256


def line_scratch(length, width):
    chunks = length // LINE_CHUNK
    return [pltpu.VMEM((length, width), jnp.bfloat16)] * 4 + [
        pltpu.SemaphoreType.DMA((chunks,))
    ] * 4


def line_call(kernel, name, collective_id, outs, scratch, operands, flops=0, spaces=()):
    size = sum(o.size * o.dtype.itemsize for o in operands) + sum(
        o.size * o.dtype.itemsize for o in outs
    )
    vmem = pl.BlockSpec(memory_space=pltpu.VMEM)
    return pl.pallas_call(
        kernel,
        name=name,
        out_shape=outs,
        in_specs=[vmem] * (len(operands) - len(spaces))
        + [pl.BlockSpec(memory_space=space) for space in spaces],
        out_specs=[vmem] * len(outs),
        scratch_shapes=scratch,
        compiler_params=pltpu.CompilerParams(
            collective_id=collective_id, has_side_effects=True, vmem_limit_bytes=VMEM_LIMIT
        ),
        cost_estimate=pl.CostEstimate(
            flops=flops, bytes_accessed=size + 100_000_000, transcendentals=0
        ),
    )(*operands)


def start_kernel(
    count,
    part,
    gain,
    shift,
    bias,
    master,
    w_qkv,
    w_in,
    w_down,
    rows_out,
    attn_out,
    base_out,
    ffn_out,
    pool_out,
    *scratch,
):
    (normed, held_qkv, turned, held_in, held_down, sems, pool, near_out, near_in, far_out, far_in) = (
        scratch[8:]
    )
    shards = pool.shape[0]
    splits = shards.bit_length() - 1
    me = lax.axis_index("dp")
    lane = lax.axis_index("mp")
    mates = [me + 2**k * (1 - 2 * ((me // 2**k) % 2)) for k in range(splits)]
    peers = [lax.rem(lane + offset, count) for offset in range(count)]
    barrier = pltpu.get_barrier_semaphore()
    for mate in mates:
        pl.semaphore_signal(barrier, inc=1, device_id={"dp": mate, "mp": lane}, device_id_type=MESH)
    for peer in peers[1:]:
        pl.semaphore_signal(barrier, inc=1, device_id={"dp": me, "mp": peer}, device_id_type=MESH)
    pl.semaphore_wait(barrier, splits + count - 1)
    pool[me, lane] = master[...].astype(jnp.bfloat16)

    def near(offset):
        return pltpu.make_async_remote_copy(
            src_ref=pool.at[me, lane],
            dst_ref=pool.at[me, lane],
            send_sem=near_out.at[offset],
            recv_sem=near_in.at[offset],
            device_id={"dp": me, "mp": peers[offset]},
            device_id_type=MESH,
        )

    def far(stage):
        bit = splits - 1 - stage
        copies = []
        for place in range(2**stage):
            slot = lax.rem(me, 2 ** (bit + 1)) + place * 2 ** (bit + 1)
            copies.append(
                pltpu.make_async_remote_copy(
                    src_ref=pool.at[slot],
                    dst_ref=pool.at[slot],
                    send_sem=far_out.at[2**stage - 1 + place],
                    recv_sem=far_in.at[2**stage - 1 + place],
                    device_id={"dp": mates[bit], "mp": lane},
                    device_id_type=MESH,
                )
            )
        return copies

    for offset in range(1, count):
        near(offset).start()

    first, last = 6, part.shape[0] // LINE_CHUNK + 2
    waits = (
        [first]
        + [
            first + (last - first) * (2 ** (stage + 1) - 1) // max(1, 2 ** (splits - 1) - 1)
            for stage in range(splits - 1)
        ]
        + [last + 6]
    )

    def prepare(at):
        for stage in range(splits + 1):

            @pl.when(at == waits[stage])
            def _(stage=stage):
                if stage == 0:
                    for offset in range(1, count):
                        near(offset).wait_recv()
                else:
                    for copy in far(stage - 1):
                        copy.wait_recv()
                if stage < splits:
                    for copy in far(stage):
                        copy.start()

    loads = [
        pltpu.make_async_copy(src, dst, sems.at[slot])
        for slot, (src, dst) in enumerate(
            ((w_qkv, held_qkv), (w_in, held_in), (w_down, held_down))
        )
    ]
    for load in loads:
        load.start()

    def emit(rows, total):
        rows_out[rows, :] = total.astype(jnp.bfloat16)
        centre = total - jnp.mean(total, -1, keepdims=True)
        spread = jnp.mean(centre * centre, -1, keepdims=True)
        base = centre * lax.rsqrt(spread + NORM_EPS)
        attn_out[rows, :] = (base * gain[0:1, :] + shift[0:1, :]).astype(jnp.bfloat16)
        normed[rows, :] = (base * gain[1:2, :] + shift[1:2, :]).astype(jnp.bfloat16)

    per = WORK_ROWS // LINE_CHUNK

    def follow(ready):
        @pl.when(ready == per - 1)
        def _():
            for load in loads:
                load.wait()
            heads = held_qkv.shape[1] // (3 * HD)
            for kind in range(3):
                for head in range(heads):
                    into = (kind * heads + head) * HD
                    source = (head * 3 + kind) * HD
                    turned[:, into : into + HD] = held_qkv[:, source : source + HD]

        @pl.when(lax.rem(ready, per) == per - 1)
        def _():
            rows = line_chunk(ready // per, WORK_ROWS)
            base_out[rows, :] = jnp.dot(
                attn_out[rows, :], turned[...], preferred_element_type=jnp.float32
            )
            pre = (
                jnp.dot(normed[rows, :], held_in[...], preferred_element_type=jnp.float32)
                + bias[...]
            )
            hidden = (0.5 * pre * (1.0 + lax.erf(pre * 0.5**0.5))).astype(jnp.bfloat16)
            ffn_out[rows, :] = jnp.dot(
                hidden, held_down[...], preferred_element_type=jnp.float32
            ).astype(jnp.bfloat16)

    line_sum(
        count,
        LINE_CHUNK,
        part,
        scratch[:4],
        scratch[4:8],
        prepare,
        emit,
        greet=False,
        follow=follow,
        always=True,
    )
    pool_out[...] = pool[...]
    for offset in range(1, count):
        near(offset).wait_send()
    for stage in range(splits):
        for copy in far(stage):
            copy.wait_send()


def turn_pairs(field, cosine, sine, sign):
    lane = lax.broadcasted_iota(jnp.int32, field.shape, 1) % HD
    half = ROT // 2
    other = jnp.where(
        lane < half, pltpu.roll(field, field.shape[1] - half, 1), pltpu.roll(field, half, 1)
    )
    return field * cosine + sign * other * sine


CROSS = (((1,), (1,)), ((), ()))


def resid_kernel(
    count,
    attn,
    base,
    ffn,
    start,
    gain,
    shift,
    cosine,
    sine,
    down_qkv,
    up_q,
    up_k,
    up_v,
    down_out,
    up_out,
    w_out,
    inner_out,
    query_out,
    key_out,
    value_out,
    context_out,
    spread_out,
    low_out,
    resid_out,
    final_out,
    *scratch,
):
    own = scratch[8]
    group = w_out.shape[0]
    total_rows = own.shape[0]
    key_out[...] = jnp.zeros_like(key_out)
    value_out[...] = jnp.zeros_like(value_out)

    def attend(block):
        rows = line_chunk(block, WORK_ROWS)
        low = jnp.dot(
            attn[rows, :], down_qkv[...], preferred_element_type=jnp.float32
        ).astype(jnp.bfloat16)
        inner_out[rows, :] = low
        for kind, (up, out) in enumerate(
            ((up_q, query_out), (up_k, key_out), (up_v, value_out))
        ):
            extra = lax.dot_general(
                low[:, kind * R : (kind + 1) * R],
                up[...],
                CROSS,
                preferred_element_type=jnp.float32,
            )
            for at in range(0, group, 128):
                field = base[rows, kind * group + at : kind * group + at + 128]
                field = field + extra[:, at : at + 128]
                if kind < 2:
                    field = turn_pairs(field, cosine[rows, :], sine[rows, :], 1.0)
                out[rows, at : at + 128] = field.astype(jnp.bfloat16)
        lane = lax.broadcasted_iota(jnp.int32, (WORK_ROWS, 128), 1)
        column = lax.broadcasted_iota(jnp.int32, (WORK_ROWS, total_rows), 1)
        place = lax.broadcasted_iota(jnp.int32, (WORK_ROWS, total_rows), 0)
        seen = column <= place + block * WORK_ROWS
        spreads = jnp.zeros((WORK_ROWS, 128), jnp.float32)
        for at in range(0, group, 128):
            pair = query_out[rows, at : at + 128]
            keys = key_out[:, at : at + 128]
            values = value_out[:, at : at + 128]
            results = []
            for side in range(128 // HD):
                mine = jnp.where(lane // HD == side, pair, jnp.zeros_like(pair))
                scores = (
                    lax.dot_general(mine, keys, CROSS, preferred_element_type=jnp.float32)
                    * HD**-0.5
                )
                scores = jnp.where(seen, scores, -1e30)
                top = jnp.max(scores, -1, keepdims=True)
                weights = jnp.exp(scores - top)
                total = jnp.sum(weights, -1, keepdims=True)
                probs = (weights * (1.0 / total)).astype(jnp.bfloat16)
                results.append(jnp.dot(probs, values, preferred_element_type=jnp.float32))
                head = at // HD + side
                spreads = jnp.where(lane == head, top + jnp.log(total), spreads)
            joined = results[0]
            for side in range(1, 128 // HD):
                joined = jnp.where(lane // HD == side, results[side], joined)
            context_out[rows, at : at + 128] = joined.astype(jnp.bfloat16)
        spread_out[rows, :] = spreads
        context = context_out[rows, :]
        low = jnp.dot(context, down_out[...], preferred_element_type=jnp.float32).astype(
            jnp.bfloat16
        )
        low_out[rows, :] = low
        own[rows, :] = (
            jnp.dot(context, w_out[...], preferred_element_type=jnp.float32)
            + lax.dot_general(low, up_out[...], CROSS, preferred_element_type=jnp.float32)
            + ffn[rows, :].astype(jnp.float32)
        ).astype(jnp.bfloat16)

    per = WORK_ROWS // LINE_CHUNK

    def prepare(at):
        @pl.when(lax.rem(at, per) == 0)
        def _():
            attend(at // per)

    def emit(rows, total):
        resid = start[rows, :].astype(jnp.float32) + total
        resid_out[rows, :] = resid
        normed = layer_norm(resid, gain[2:3, :], shift[2:3, :])
        final_out[rows, :] = normed.astype(jnp.bfloat16)

    line_sum(count, LINE_CHUNK, own, scratch[:4], scratch[4:8], prepare, emit)


DOWN = (((0,), (0,)), ((), ()))


def branch_kernel(count, raw, hits, stats, gain, up_q, up_k, up_v, down_out, *refs):
    prompts, totals = refs[0:2]
    sources = refs[2:15]
    loss_out = refs[15]
    grad_down = refs[16:19]
    grad_out_b = refs[19]
    grad_up = refs[20:23]
    grad_out_a = refs[23]
    scratch = refs[24:]
    own, note_send, note_recv, scales, note_out, note_in = scratch[8:14]
    held = scratch[14:27]
    sems, out, query_grad, key_turned, value_turned, out_b_turned, out_a_turned = scratch[27:]
    (
        resid,
        queries,
        keys,
        values,
        context,
        spreads,
        inner,
        low,
        attn,
        w_out,
        up_out,
        cosine,
        sine,
    ) = held
    me = lax.axis_index("mp")
    rows_all = raw.shape[0]
    group = w_out.shape[0]
    loads = [
        pltpu.make_async_copy(src, dst, sems.at[slot])
        for slot, (src, dst) in enumerate(zip(sources, held))
    ]
    for load in loads:
        load.start()
    greet_peers(me, count)
    note_send[...] = stats[...].T[0:8, :]
    copies = []
    for offset in range(1, count):
        copy = pltpu.make_async_remote_copy(
            src_ref=note_send,
            dst_ref=note_recv.at[offset],
            send_sem=note_out.at[offset],
            recv_sem=note_in.at[offset],
            device_id={"mp": lax.rem(me + offset, count)},
            device_id_type=MESH,
        )
        copy.start()
        copies.append(copy)
    for ref in (key_turned, value_turned, out_b_turned, out_a_turned):
        ref[...] = jnp.zeros_like(ref)
    mine = note_send[...]
    for copy in copies:
        copy.wait_recv()
    others = [mine] + [note_recv[offset] for offset in range(1, count)]
    top = functools.reduce(jnp.maximum, [part[0:1, :] for part in others])
    total = sum(part[1:2, :] * jnp.exp(part[0:1, :] - top) for part in others)
    found = sum(part[2:3, :] for part in others)
    spread_row = top + jnp.log(total)
    amount = sum(totals[e] - prompts[e] for e in range(prompts.shape[0]))
    example = lax.axis_index("dp")
    position = lax.broadcasted_iota(jnp.int32, (1, rows_all), 1)
    keep = (position >= prompts[example] - 1) & (position < totals[example] - 1)
    share = jnp.where(keep, 1.0 / jnp.broadcast_to(amount, (1, rows_all)).astype(jnp.float32), 0.0)
    loss_out[...] = (spread_row - found) * share
    factor = jnp.exp(mine[0:1, :] - spread_row) * share
    pair = jnp.concatenate([factor, share, jnp.zeros((126, rows_all), jnp.float32)], 0)
    scales[...] = pair.T
    for load in loads:
        load.wait()

    def prepare(at):
        rows = line_chunk(at, LINE_CHUNK)
        scale = scales[rows, :]
        own[rows, :] = (
            raw[rows, :] * scale[:, 0:1] - hits[rows, :].astype(jnp.float32) * scale[:, 1:2]
        ).astype(jnp.bfloat16)

    def emit(rows, total):
        values_here = resid[rows, :]
        centre = values_here - jnp.mean(values_here, -1, keepdims=True)
        spread = jnp.mean(centre * centre, -1, keepdims=True)
        inverse = lax.rsqrt(spread + NORM_EPS)
        normed = centre * inverse
        up = total * gain[2:3, :]
        out[rows, :] = (
            inverse
            * (
                up
                - jnp.mean(up, -1, keepdims=True)
                - normed * jnp.mean(up * normed, -1, keepdims=True)
            )
        ).astype(jnp.bfloat16)

    def attend_back(block):
        rows = line_chunk(block, WORK_ROWS)
        upstream = out[rows, :]
        low_grad = jnp.dot(upstream, up_out[...], preferred_element_type=jnp.float32).astype(
            jnp.bfloat16
        )
        grads = (
            lax.dot_general(upstream, w_out[...], CROSS, preferred_element_type=jnp.float32)
            + lax.dot_general(low_grad, down_out[...], CROSS, preferred_element_type=jnp.float32)
        ).astype(jnp.bfloat16)
        out_b_turned[...] += lax.dot_general(
            low[rows, :], upstream, DOWN, preferred_element_type=jnp.float32
        )
        out_a_turned[...] += lax.dot_general(
            low_grad, context[rows, :], DOWN, preferred_element_type=jnp.float32
        )
        lane = lax.broadcasted_iota(jnp.int32, (WORK_ROWS, 128), 1)
        column = lax.broadcasted_iota(jnp.int32, (WORK_ROWS, rows_all), 1)
        place = lax.broadcasted_iota(jnp.int32, (WORK_ROWS, rows_all), 0)
        seen = column <= place + block * WORK_ROWS
        for at in range(0, group, 128):
            pick = slice(at, at + 128)
            joined = jnp.zeros((WORK_ROWS, 128), jnp.float32)
            key_part = jnp.zeros((128, rows_all), jnp.float32)
            value_part = jnp.zeros((128, rows_all), jnp.float32)
            for side in range(128 // HD):
                head = at // HD + side
                here = lane // HD == side
                query = jnp.where(here, queries[rows, pick], jnp.zeros((), jnp.bfloat16))
                grad = jnp.where(here, grads[:, pick], jnp.zeros((), jnp.bfloat16))
                scores = (
                    lax.dot_general(
                        query, keys[:, pick], CROSS, preferred_element_type=jnp.float32
                    )
                    * HD**-0.5
                )
                scores = jnp.where(seen, scores, -1e30)
                probs = jnp.exp(scores - spreads[rows, head : head + 1])
                prob_grad = lax.dot_general(
                    grad, values[:, pick], CROSS, preferred_element_type=jnp.float32
                )
                mean = jnp.sum(probs * prob_grad, -1, keepdims=True)
                score_grad = (probs * (prob_grad - mean)).astype(jnp.bfloat16)
                result = jnp.dot(score_grad, keys[:, pick], preferred_element_type=jnp.float32)
                joined = jnp.where(here, result, joined)
                key_part += lax.dot_general(
                    query, score_grad, DOWN, preferred_element_type=jnp.float32
                )
                value_part += lax.dot_general(
                    grad, probs.astype(jnp.bfloat16), DOWN, preferred_element_type=jnp.float32
                )
            key_turned[pick, :] += key_part
            value_turned[pick, :] += value_part
            query_grad[rows, pick] = turn_pairs(
                joined * HD**-0.5, cosine[rows, :], sine[rows, :], -1.0
            ).astype(jnp.bfloat16)

    per = WORK_ROWS // LINE_CHUNK

    def follow(ready):
        @pl.when(lax.rem(ready, per) == per - 1)
        def _():
            attend_back(ready // per)

    line_sum(
        count,
        LINE_CHUNK,
        own,
        scratch[:4],
        scratch[4:8],
        prepare,
        emit,
        greet=False,
        follow=follow,
    )
    key_grad = jnp.concatenate(
        [
            turn_pairs(
                key_turned[at : at + 128, :].T * HD**-0.5, cosine[...], sine[...], -1.0
            ).astype(jnp.bfloat16)
            for at in range(0, group, 128)
        ],
        1,
    )
    value_grad = value_turned[...].T.astype(jnp.bfloat16)
    for kind, (grad, up) in enumerate(
        ((query_grad[...], up_q), (key_grad, up_k), (value_grad, up_v))
    ):
        wide = jnp.dot(grad, up[...], preferred_element_type=jnp.float32)
        high = wide.astype(jnp.bfloat16)
        rest = (wide - high.astype(jnp.float32)).astype(jnp.bfloat16)
        turned = lax.dot_general(high, attn[...], DOWN, preferred_element_type=jnp.float32)
        turned += lax.dot_general(rest, attn[...], DOWN, preferred_element_type=jnp.float32)
        grad_down[kind][...] = turned.T
        grad_up[kind][...] = lax.dot_general(
            inner[:, kind * R : (kind + 1) * R], grad, DOWN, preferred_element_type=jnp.float32
        ).T
    grad_out_b[...] = out_b_turned[...].T
    grad_out_a[...] = out_a_turned[...].T
    for copy in copies:
        copy.wait_send()


def loss_kernel(vocab, tile, values, ahead, behind, hits, acc, stats, logits, probs, tops, sums):
    at = pl.program_id(0)
    tiles = pl.num_programs(0) - 1
    rows_all = values.shape[0]

    @pl.when(at == 0)
    def _():
        acc[...] = jnp.zeros_like(acc)
        tops[...] = jnp.full_like(tops, -1e29)
        sums[...] = jnp.zeros_like(sums)
        logits[...] = jnp.full_like(logits, -1e30)

    tail = vocab % tile
    if tail:

        @pl.when(at >= tiles - 1)
        def _():
            ahead[tail:, :] = jnp.zeros((tile - tail, ahead.shape[1]), ahead.dtype)

        @pl.when(at >= tiles)
        def _():
            behind[tail:, :] = jnp.zeros((tile - tail, behind.shape[1]), behind.dtype)

    ids = (at - 1) * tile + lax.broadcasted_iota(jnp.int32, (1, tile), 1)
    scores = logits[...] + jnp.where(ids < vocab, 0.0, -1e30)
    old = tops[:, 0:1]
    new = jnp.maximum(old, jnp.max(scores, -1, keepdims=True))
    weights = jnp.exp(scores - new)
    shrink = jnp.exp(old - new)
    sums[...] = sums[...] * shrink + jnp.sum(weights, -1, keepdims=True)
    tops[...] = jnp.broadcast_to(new, tops.shape)
    acc[...] = acc[...] * shrink
    probs[...] = weights.astype(jnp.bfloat16)
    logits[...] = lax.dot_general(
        values[...], ahead[...], (((1,), (1,)), ((), ())), preferred_element_type=jnp.float32
    )
    acc[...] += jnp.dot(probs[...], behind[...], preferred_element_type=jnp.float32)

    @pl.when(at == tiles)
    def _():
        found = jnp.sum(
            values[...].astype(jnp.float32) * hits[...].astype(jnp.float32), -1, keepdims=True
        )
        column = lax.broadcasted_iota(jnp.int32, (rows_all, 128), 1)
        stats[...] = jnp.where(
            column == 0, tops[...], jnp.where(column == 1, sums[...], found)
        )


LOSS_TILE = 512


def loss_call(values, head_rows, hits):
    rows, width = values.shape
    vocab = head_rows.shape[0]
    tile = LOSS_TILE
    tiles = pl.cdiv(vocab, tile)
    whole = pl.BlockSpec((rows, width), lambda j: (0, 0))
    return pl.pallas_call(
        functools.partial(loss_kernel, vocab, tile),
        name="loss",
        grid=(tiles + 1,),
        in_specs=[
            whole,
            pl.BlockSpec((tile, width), lambda j: (jnp.minimum(j, tiles - 1), 0)),
            pl.BlockSpec((tile, width), lambda j: (jnp.maximum(j - 1, 0), 0)),
            whole,
        ],
        out_specs=[whole, pl.BlockSpec((rows, 128), lambda j: (0, 0))],
        out_shape=[
            jax.ShapeDtypeStruct((rows, width), jnp.float32),
            jax.ShapeDtypeStruct((rows, 128), jnp.float32),
        ],
        scratch_shapes=[
            pltpu.VMEM((rows, tile), jnp.float32),
            pltpu.VMEM((rows, tile), jnp.bfloat16),
            pltpu.VMEM((rows, 128), jnp.float32),
            pltpu.VMEM((rows, 128), jnp.float32),
        ],
        compiler_params=pltpu.CompilerParams(vmem_limit_bytes=VMEM_LIMIT),
        cost_estimate=pl.CostEstimate(
            flops=4 * rows * width * vocab,
            bytes_accessed=4 * width * vocab,
            transcendentals=rows * vocab,
        ),
    )(values, head_rows, head_rows, hits)


def fold_kernel(splits, count, *refs):
    fulls = refs[0:4]
    groups = refs[4:8]
    losses, master, first, second, bases = refs[8:13]
    loss_out, norm_out, first_out, second_out, master_out = refs[13:18]
    scratch = refs[18:]
    sends = scratch[0:splits]
    recvs = scratch[splits : 2 * splits]
    keeps = scratch[2 * splits : 3 * splits]
    (line_send, line_recv, turn_send, turn_recv, note_send, note_recv, tell_send, tell_recv) = scratch[
        3 * splits : 3 * splits + 8
    ]
    (half_out, half_in, line_out, line_in, turn_out, turn_in, note_out, note_in, tell_out, tell_in) = (
        scratch[3 * splits + 8 :]
    )
    shards = 2**splits
    me = lax.axis_index("dp")
    lane = lax.axis_index("mp")
    full_rows = fulls[0].shape[0] // shards
    group_rows = groups[0].shape[0] // shards
    own_rows = full_rows // count
    bits = [(me // 2**k) % 2 for k in range(splits)]
    mates = [me + 2**k * (1 - 2 * bits[k]) for k in range(splits)]
    peers = [lax.rem(lane + offset, count) for offset in range(count)]
    spot = lane * shards + me
    goal = (spot // count, lax.rem(spot, count))
    place = me * count + lane
    origin = (lax.rem(place, shards), place // shards)
    moved = spot != place

    barrier = pltpu.get_barrier_semaphore()
    for mate in mates:
        pl.semaphore_signal(barrier, inc=1, device_id={"dp": mate, "mp": lane}, device_id_type=MESH)
    for peer in peers[1:]:
        pl.semaphore_signal(barrier, inc=1, device_id={"dp": me, "mp": peer}, device_id_type=MESH)

    @pl.when(moved)
    def _():
        for device in (goal, origin):
            pl.semaphore_signal(
                barrier, inc=1, device_id={"dp": device[0], "mp": device[1]}, device_id_type=MESH
            )

    pl.semaphore_wait(barrier, splits + count - 1 + jnp.where(moved, 2, 0))

    def remote(src, dst, out_sem, in_sem, device):
        return pltpu.make_async_remote_copy(
            src_ref=src,
            dst_ref=dst,
            send_sem=out_sem,
            recv_sem=in_sem,
            device_id={"dp": device[0], "mp": device[1]},
            device_id_type=MESH,
        )

    def piece(index):
        whole = pl.ds(pl.multiple_of(index * full_rows, full_rows), full_rows)
        part = pl.ds(pl.multiple_of(index * group_rows, group_rows), group_rows)
        return jnp.concatenate(
            [ref[whole, :] for ref in fulls] + [ref[part, :] for ref in groups], 0
        )

    started = []
    current = piece
    for k in range(splits):
        half = shards >> (k + 1)
        for i in range(half):
            sends[k][i] = current(2 * i + 1 - bits[k]).astype(jnp.bfloat16)
        copy = remote(sends[k], recvs[k], half_out.at[k], half_in.at[k], (mates[k], lane))
        copy.start()
        started.append(copy)
        for i in range(half):
            keeps[k][i] = current(2 * i + bits[k])
        copy.wait_recv()
        current = functools.partial(
            lambda kept, came, i: kept[i] + came[i].astype(jnp.float32), keeps[k], recvs[k]
        )
    final = keeps[splits - 1]
    final[0] = current(0)

    def chosen(peer):
        return jnp.concatenate(
            [
                final[
                    0,
                    pl.ds(pl.multiple_of(a * full_rows + peer * own_rows, own_rows), own_rows),
                    :,
                ]
                for a in range(4)
            ],
            0,
        )

    turn_send[...] = final[0, 4 * full_rows :, :].astype(jnp.bfloat16)
    turn = remote(turn_send, turn_recv, turn_out, turn_in, goal)

    @pl.when(moved)
    def _():
        turn.start()

    for offset in range(1, count):
        line_send[offset] = chosen(peers[offset]).astype(jnp.bfloat16)
        copy = remote(
            line_send.at[offset],
            line_recv.at[offset],
            line_out.at[offset],
            line_in.at[offset],
            (me, peers[offset]),
        )
        copy.start()
        started.append(copy)
    total = chosen(lane)

    @pl.when(moved)
    def _():
        turn.wait()

    @pl.when(jnp.logical_not(moved))
    def _():
        turn_recv[...] = turn_send[...]

    for copy in started[splits:]:
        copy.wait_recv()
    for offset in range(1, count):
        total = total + line_recv[offset].astype(jnp.float32)
    part = turn_recv[...].astype(jnp.float32)

    column = lax.broadcasted_iota(jnp.int32, (8, 128), 1)
    row = lax.broadcasted_iota(jnp.int32, (8, 128), 0)
    squares = jnp.sum(total * total) + jnp.sum(part * part)
    spot_norm = (row == 0) & (column == 0)
    spot_loss = (row == 0) & (column == 1)
    note = jnp.where(spot_norm, squares, 0.0) + jnp.where(spot_loss, jnp.sum(losses[...]), 0.0)

    def rows_of(index):
        source, slot = (total, (0, 1, 2, 7).index(index)) if index in (0, 1, 2, 7) else (
            part,
            index - 3,
        )
        return source[slot * own_rows : (slot + 1) * own_rows, :]

    turned = [
        jnp.dot(
            rows_of(m), bases[m], precision=HIGH_PRECISION, preferred_element_type=jnp.float32
        )
        for m in range(8)
    ]
    for k in range(splits):
        note_send[k] = note
        copy = remote(
            note_send.at[k], note_recv.at[k], note_out.at[k], note_in.at[k], (mates[k], lane)
        )
        copy.start()
        started.append(copy)
        copy.wait_recv()
        note = note + note_recv[k]
    tell_send[...] = note
    tells = []
    for offset in range(1, count):
        copy = remote(
            tell_send,
            tell_recv.at[offset],
            tell_out.at[offset],
            tell_in.at[offset],
            (me, peers[offset]),
        )
        copy.start()
        tells.append(copy)
    for copy in tells:
        copy.wait_recv()
    everything = note
    for offset in range(1, count):
        everything = everything + tell_recv[offset]
    norm = jnp.sqrt(jnp.sum(jnp.where(spot_norm, everything, 0.0), keepdims=True))
    loss_out[...] = jnp.sum(jnp.where(spot_loss, note, 0.0), keepdims=True)
    norm_out[...] = norm
    factor = jnp.minimum(1.0, CLIP_LIMIT / norm)
    for m in range(8):
        rotated = turned[m] * factor
        new_first = BETA_FIRST * first[m] + (1.0 - BETA_FIRST) * rotated
        new_second = BETA_SECOND * second[m] + (1.0 - BETA_SECOND) * rotated * rotated
        first_out[m] = new_first
        second_out[m] = new_second
        normed = (
            new_first
            / (1.0 - BETA_FIRST**ADAM_STEP)
            / (jnp.sqrt(new_second / (1.0 - BETA_SECOND**ADAM_STEP)) + ADAM_EPS)
        )
        back = lax.dot_general(
            normed,
            bases[m],
            (((1,), (1,)), ((), ())),
            precision=HIGH_PRECISION,
            preferred_element_type=jnp.float32,
        )
        master_out[m] = master[m] - LEARN_RATE * (back + DECAY_RATE * master[m])
    for copy in started + tells:
        copy.wait_send()


def fold_call(fulls, groups, losses, master, first_moment, second_moment, bases):
    shards = lax.axis_size("dp")
    count = lax.axis_size("mp")
    splits = shards.bit_length() - 1
    width = fulls[0].shape[1]
    pile = 4 * (fulls[0].shape[0] + groups[0].shape[0]) // shards
    own = 4 * fulls[0].shape[0] // (shards * count)
    low = jnp.bfloat16
    halves = [shards >> (k + 1) for k in range(splits)]
    dma = pltpu.SemaphoreType.DMA
    scratch = (
        [pltpu.VMEM((half, pile, width), low) for half in halves] * 2
        + [pltpu.VMEM((half, pile, width), jnp.float32) for half in halves]
        + [pltpu.VMEM((count, own, width), low)] * 2
        + [pltpu.VMEM((4 * groups[0].shape[0] // shards, width), low)] * 2
        + [pltpu.VMEM((splits, 8, 128), jnp.float32)] * 2
        + [pltpu.VMEM((8, 128), jnp.float32), pltpu.VMEM((count, 8, 128), jnp.float32)]
        + [dma((splits,))] * 2
        + [dma((count,))] * 2
        + [dma(())] * 2
        + [dma((splits,))] * 2
        + [dma((count,))] * 2
    )
    scalar = jax.ShapeDtypeStruct((1, 1), jnp.float32)
    state = jax.ShapeDtypeStruct(master.shape, jnp.float32)
    return line_call(
        functools.partial(fold_kernel, splits, count),
        "fold",
        3,
        [scalar, scalar, state, state, state],
        scratch,
        [*fulls, *groups, losses, master, first_moment, second_moment, bases],
    )


def per_device(
    token_ids,
    prompt_len,
    example_len,
    embedding,
    w_qkv,
    w_out,
    w_in,
    b_in,
    w_down,
    unembed,
    ln_gain,
    ln_bias,
    master,
    first_moment,
    second_moment,
    eigen_bases,
):
    group_count = lax.axis_size("mp")
    group_index = lax.axis_index("mp")
    head_rows = lax.all_gather(unembed.T, "dp", axis=1, tiled=True)
    examples, length = token_ids.shape
    width = embedding.shape[0]
    vocab_local = head_rows.shape[0]
    rows = examples * length
    local_heads = HEADS // group_count
    group_width = local_heads * HD
    flat_ids = token_ids.reshape(rows)
    picked = pick_call(flat_ids - group_index * width, embedding, "pick_start")
    shape_low = jax.ShapeDtypeStruct((rows, D), jnp.bfloat16)
    shape_wide = jax.ShapeDtypeStruct((rows, D), jnp.float32)
    shards = lax.axis_size("dp")
    own_rows = master.shape[1]
    pool_shape = (shards, group_count, 8, own_rows, R)
    start_rows, normed_attn, base, ffn_part, pool = line_call(
        functools.partial(start_kernel, group_count),
        "start_rows",
        0,
        [
            shape_low,
            shape_low,
            jax.ShapeDtypeStruct((rows, w_qkv.shape[1]), jnp.float32),
            shape_low,
            jax.ShapeDtypeStruct(pool_shape, jnp.bfloat16),
        ],
        line_scratch(rows, D)
        + [
            pltpu.VMEM((rows, D), jnp.bfloat16),
            pltpu.VMEM(w_qkv.shape, jnp.bfloat16),
            pltpu.VMEM(w_qkv.shape, jnp.bfloat16),
            pltpu.VMEM(w_in.shape, jnp.bfloat16),
            pltpu.VMEM(w_down.shape, jnp.bfloat16),
            pltpu.SemaphoreType.DMA((3,)),
            pltpu.VMEM(pool_shape, jnp.bfloat16),
        ]
        + [pltpu.SemaphoreType.DMA((group_count,))] * 2
        + [pltpu.SemaphoreType.DMA((shards - 1,))] * 2,
        [picked, ln_gain, ln_bias, b_in.reshape(1, -1), master, w_qkv, w_in, w_down],
        spaces=(pl.ANY,) * 3,
    )
    adapters = pool.transpose(2, 0, 1, 3, 4).reshape(8, -1, R)
    target = jnp.roll(token_ids, -1, axis=1).reshape(rows)
    adapter_rows = [
        lax.dynamic_slice_in_dim(
            adapters[3 + selector_index], group_index * group_width, group_width, 0
        )
        for selector_index in range(3)
    ]
    out_rows = lax.dynamic_slice_in_dim(adapters[6], group_index * group_width, group_width, 0)
    cosine, sine = rope_tables(length)
    rest = jnp.zeros((length, HD - ROT), jnp.float32)
    wide_cosine = jnp.concatenate([cosine[:, 0], cosine[:, 0], rest + 1.0] * (128 // HD), 1)
    wide_sine = jnp.concatenate([-sine[:, 0], sine[:, 0], rest] * (128 // HD), 1)
    shape_group = jax.ShapeDtypeStruct((rows, group_width), jnp.bfloat16)
    (
        inner,
        queries,
        key_rows,
        value_rows,
        context,
        spread_lanes,
        inner_out,
        resid,
        final_rows,
    ) = line_call(
        functools.partial(resid_kernel, group_count),
        "resid_rows",
        1,
        [
            jax.ShapeDtypeStruct((rows, 3 * R), jnp.bfloat16),
            shape_group,
            shape_group,
            shape_group,
            shape_group,
            jax.ShapeDtypeStruct((rows, 128), jnp.float32),
            jax.ShapeDtypeStruct((rows, R), jnp.bfloat16),
            shape_wide,
            shape_low,
        ],
        line_scratch(rows, D) + [pltpu.VMEM((rows, D), jnp.bfloat16)],
        [
            normed_attn,
            base,
            ffn_part,
            start_rows,
            ln_gain,
            ln_bias,
            wide_cosine,
            wide_sine,
            jnp.concatenate([adapters[0], adapters[1], adapters[2]], 1),
            *adapter_rows,
            out_rows,
            adapters[7],
            w_out,
        ],
    )
    goal = target - group_index * vocab_local
    hits = pick_call(goal, head_rows, "pick_target")
    raw_grad, stats = loss_call(final_rows, head_rows, hits)
    late = [
        resid,
        queries,
        key_rows,
        value_rows,
        context,
        spread_lanes,
        inner,
        inner_out,
        normed_attn,
        w_out,
        adapters[7],
        wide_cosine,
        wide_sine,
    ]
    tall = jax.ShapeDtypeStruct((D, R), jnp.float32)
    short = jax.ShapeDtypeStruct((group_width, R), jnp.float32)
    losses, grad_q, grad_k, grad_v, grad_out_b, *local_grads = line_call(
        functools.partial(branch_kernel, group_count),
        "branch_rows",
        2,
        [jax.ShapeDtypeStruct((1, rows), jnp.float32)] + [tall] * 4 + [short] * 4,
        line_scratch(rows, D)
        + [
            pltpu.VMEM((rows, D), jnp.bfloat16),
            pltpu.VMEM((8, rows), jnp.float32),
            pltpu.VMEM((group_count, 8, rows), jnp.float32),
            pltpu.VMEM((rows, 128), jnp.float32),
            pltpu.SemaphoreType.DMA((group_count,)),
            pltpu.SemaphoreType.DMA((group_count,)),
        ]
        + [pltpu.VMEM(value.shape, value.dtype) for value in late]
        + [
            pltpu.SemaphoreType.DMA((len(late),)),
            pltpu.VMEM((rows, D), jnp.bfloat16),
            pltpu.VMEM((rows, group_width), jnp.bfloat16),
            pltpu.VMEM((group_width, rows), jnp.float32),
            pltpu.VMEM((group_width, rows), jnp.float32),
            pltpu.VMEM((R, D), jnp.float32),
            pltpu.VMEM((R, group_width), jnp.float32),
        ],
        [
            raw_grad,
            hits,
            stats,
            ln_gain,
            *adapter_rows,
            out_rows,
            prompt_len,
            example_len,
            *late,
        ],
        spaces=(pltpu.SMEM,) * 2 + (pl.ANY,) * len(late),
    )
    mean_loss, grad_norm, new_first, new_second, new_master = fold_call(
        [grad_q, grad_k, grad_v, grad_out_b],
        local_grads,
        losses,
        master,
        first_moment,
        second_moment,
        eigen_bases,
    )
    return (mean_loss.reshape(()), grad_norm.reshape(()), new_first, new_second, new_master)


def solution(mesh):
    placed = (
        P("dp", None),
        P(),
        P(),
        P("mp", None),
        P(None, "mp"),
        P("mp", None),
        P(None, "mp"),
        P("mp"),
        P("mp", None),
        P("dp", "mp"),
        P(),
        P(),
        P(None, ("dp", "mp"), None),
        P(None, ("dp", "mp"), None),
        P(None, ("dp", "mp"), None),
        P(),
    )
    return jax.shard_map(
        per_device,
        mesh=mesh,
        in_specs=placed,
        out_specs=(
            P(),
            P(),
            P(None, ("dp", "mp"), None),
            P(None, ("dp", "mp"), None),
            P(None, ("dp", "mp"), None),
        ),
        check_vma=False,
    )
```

```python
import functools

import jax
import jax.numpy as jnp
from jax import lax
from jax.experimental import pallas as pl
from jax.experimental.pallas import tpu as pltpu
from jax.sharding import PartitionSpec as P

MESH = pl.DeviceIdType.MESH
VMEM_LIMIT = 60 * 1024 * 1024

D = 1024
HEADS = 16
R = 128
ADAM_STEP = 10
HD = 64
ROT = 16


HIGH_PRECISION = lax.Precision.HIGHEST
NORM_EPS = 1e-05
ROPE_BASE = 10000.0
CLIP_LIMIT = 0.01
LEARN_RATE = 0.02
BETA_FIRST = 0.9
BETA_SECOND = 0.999
ADAM_EPS = 1e-08
DECAY_RATE = 0.01


def layer_norm(values, gain, shift):
    centre = values - jnp.mean(values, -1, keepdims=True)
    spread = jnp.mean(centre * centre, -1, keepdims=True)
    return centre * lax.rsqrt(spread + NORM_EPS) * gain + shift


def rope_tables(length):
    half = ROT // 2
    freqs = ROPE_BASE ** (-2.0 * jnp.arange(half, dtype=jnp.float32) / ROT)
    angles = jnp.arange(length, dtype=jnp.float32)[:, None] * freqs[None, :]
    return (jnp.cos(angles)[:, None, :], jnp.sin(angles)[:, None, :])


def line_chunk(index, size):
    return pl.ds(pl.multiple_of(index * size, size), size)


def greet_peers(me, count):
    barrier = pltpu.get_barrier_semaphore()
    for offset in range(1, count):
        pl.semaphore_signal(
            barrier, inc=1, device_id={"mp": lax.rem(me + offset, count)}, device_id_type=MESH
        )
    pl.semaphore_wait(barrier, count - 1)


def line_parts(count, chunk, own, wires, sems, emit, follow=None):
    me = lax.axis_index("mp")
    from_low, from_high, to_high, to_low = wires
    up_send, up_recv, down_send, down_recv = sems
    length = own.shape[0]
    chunks = length // chunk
    above = jnp.minimum(me + 1, count - 1)
    below = jnp.maximum(me - 1, 0)

    def up_copy(index):
        rows = line_chunk(index, chunk)
        return pltpu.make_async_remote_copy(
            src_ref=to_high.at[rows],
            dst_ref=from_low.at[rows],
            send_sem=up_send.at[index],
            recv_sem=up_recv.at[index],
            device_id={"mp": above},
            device_id_type=MESH,
        )

    def down_copy(index):
        rows = line_chunk(index, chunk)
        return pltpu.make_async_remote_copy(
            src_ref=to_low.at[rows],
            dst_ref=from_high.at[rows],
            send_sem=down_send.at[index],
            recv_sem=down_recv.at[index],
            device_id={"mp": below},
            device_id_type=MESH,
        )

    def clear():
        @pl.when(me == 0)
        def _():
            from_low[...] = jnp.zeros_like(from_low)

        @pl.when(me == count - 1)
        def _():
            from_high[...] = jnp.zeros_like(from_high)

    def step(at):
        up = at - LINE_LAG * me

        @pl.when((up >= 0) & (up < chunks))
        def _():
            rows = line_chunk(up, chunk)

            @pl.when(me > 0)
            def _():
                up_copy(up).wait_recv()

            @pl.when(me < count - 1)
            def _():
                to_high[rows, :] = (
                    from_low[rows, :].astype(jnp.float32) + own[rows, :].astype(jnp.float32)
                ).astype(jnp.bfloat16)
                up_copy(up).start()

        down = at - LINE_LAG * (count - 1 - me)

        @pl.when((down >= 0) & (down < chunks))
        def _():
            rows = line_chunk(down, chunk)

            @pl.when(me < count - 1)
            def _():
                down_copy(down).wait_recv()

            @pl.when(me > 0)
            def _():
                to_low[rows, :] = (
                    from_high[rows, :].astype(jnp.float32) + own[rows, :].astype(jnp.float32)
                ).astype(jnp.bfloat16)
                down_copy(down).start()

        ready = at - LINE_LAG * jnp.maximum(me, count - 1 - me)

        @pl.when((ready >= 0) & (ready < chunks))
        def _():
            rows = line_chunk(ready, chunk)
            total = (
                from_low[rows, :].astype(jnp.float32)
                + own[rows, :].astype(jnp.float32)
                + from_high[rows, :].astype(jnp.float32)
            )
            emit(rows, total)
            if follow is not None:
                follow(ready)

    def drain():
        def one(index, carry):
            @pl.when(me < count - 1)
            def _():
                up_copy(index).wait_send()

            @pl.when(me > 0)
            def _():
                down_copy(index).wait_send()

            return carry

        lax.fori_loop(0, chunks, one, 0)

    return clear, step, drain, chunks + LINE_LAG * (count - 1)


def line_sum(count, chunk, own, wires, sems, prepare, emit, follow=None):
    chunks = own.shape[0] // chunk
    clear, step, drain, steps = line_parts(count, chunk, own, wires, sems, emit, follow)
    clear()

    def turn(at, carry):
        @pl.when(at < chunks)
        def _():
            prepare(at)

        step(at)
        return carry

    lax.fori_loop(0, steps, turn, 0)
    drain()


PICK_GROUP = 32
PICK_ALIGN = 8


def pick_kernel(spots, places, table, out, held, sems):
    rows = out.shape[0]
    span = PICK_GROUP * PICK_ALIGN

    def start(group, carry):
        def one(token, carry):
            at = group * PICK_GROUP + token
            pltpu.make_async_copy(
                table.at[pl.ds(pl.multiple_of(spots[at], PICK_ALIGN), PICK_ALIGN)],
                held.at[pl.ds(pl.multiple_of(at * PICK_ALIGN, PICK_ALIGN), PICK_ALIGN)],
                sems.at[group],
            ).start()
            return carry

        return lax.fori_loop(0, PICK_GROUP, one, carry, unroll=8)

    lax.fori_loop(0, rows // PICK_GROUP, start, 0)

    def choose(group, carry):
        block = held.at[pl.ds(pl.multiple_of(group * span, span), span)]
        pltpu.make_async_copy(table.at[pl.ds(0, span)], block, sems.at[group]).wait()
        here = line_chunk(group, PICK_GROUP)
        wanted = places[here, :]
        column = lax.broadcasted_iota(jnp.int32, (PICK_GROUP, span), 1)
        chosen = jnp.where(column == wanted, 1.0, 0.0).astype(jnp.bfloat16)
        out[here, :] = jnp.dot(
            chosen, block[...], preferred_element_type=jnp.float32
        ).astype(jnp.bfloat16)
        return carry

    lax.fori_loop(0, rows // PICK_GROUP, choose, 0)


def pick_call(index, table, name):
    rows = index.shape[0]
    vocab, width = table.shape
    spread = (lax.iota(jnp.int32, rows) * PICK_ALIGN) % (vocab - PICK_ALIGN)
    safe = jnp.where((index >= 0) & (index < vocab), index, spread)
    spots = safe - safe % PICK_ALIGN
    column = index.reshape(rows, 1)
    token = lax.broadcasted_iota(jnp.int32, (rows, 1), 0) % PICK_GROUP
    places = jnp.where(
        (column >= 0) & (column < vocab), token * PICK_ALIGN + column % PICK_ALIGN, -1
    )
    return pl.pallas_call(
        pick_kernel,
        name=name,
        in_specs=[
            pl.BlockSpec(memory_space=pltpu.SMEM),
            pl.BlockSpec(memory_space=pltpu.VMEM),
            pl.BlockSpec(memory_space=pl.ANY),
        ],
        out_specs=pl.BlockSpec(memory_space=pltpu.VMEM),
        out_shape=jax.ShapeDtypeStruct((rows, width), jnp.bfloat16),
        scratch_shapes=[
            pltpu.VMEM((rows * PICK_ALIGN, width), jnp.bfloat16),
            pltpu.SemaphoreType.DMA((rows // PICK_GROUP,)),
        ],
        compiler_params=pltpu.CompilerParams(vmem_limit_bytes=VMEM_LIMIT),
        cost_estimate=pl.CostEstimate(
            flops=2 * rows * PICK_GROUP * PICK_ALIGN * width,
            bytes_accessed=2 * rows * PICK_ALIGN * width,
            transcendentals=0,
        ),
    )(spots, places, table)


LINE_CHUNK = 32
LINE_LAG = 3
WORK_ROWS = 256
FOLLOW_LAG = 28


def line_scratch(length, width):
    chunks = length // LINE_CHUNK
    return [pltpu.VMEM((length, width), jnp.bfloat16)] * 4 + [
        pltpu.SemaphoreType.DMA((chunks,))
    ] * 4


def line_call(kernel, name, collective_id, outs, scratch, operands, flops=0, spaces=()):
    size = sum(o.size * o.dtype.itemsize for o in operands) + sum(
        o.size * o.dtype.itemsize for o in outs
    )
    vmem = pl.BlockSpec(memory_space=pltpu.VMEM)
    return pl.pallas_call(
        kernel,
        name=name,
        out_shape=outs,
        in_specs=[vmem] * (len(operands) - len(spaces))
        + [pl.BlockSpec(memory_space=space) for space in spaces],
        out_specs=[vmem] * len(outs),
        scratch_shapes=scratch,
        compiler_params=pltpu.CompilerParams(
            collective_id=collective_id, has_side_effects=True, vmem_limit_bytes=VMEM_LIMIT
        ),
        cost_estimate=pl.CostEstimate(
            flops=flops, bytes_accessed=size + 100_000_000, transcendentals=0
        ),
    )(*operands)


def turn_pairs(field, cosine, sine, sign):
    lane = lax.broadcasted_iota(jnp.int32, field.shape, 1) % HD
    half = ROT // 2
    other = jnp.where(
        lane < half, pltpu.roll(field, field.shape[1] - half, 1), pltpu.roll(field, half, 1)
    )
    return field * cosine + sign * other * sine


CROSS = (((1,), (1,)), ((), ()))


def forward_kernel(
    count,
    part,
    gain,
    shift,
    bias,
    master,
    cosine,
    sine,
    w_qkv,
    w_in,
    w_down,
    w_wide,
    attn_out,
    inner_out,
    query_out,
    key_out,
    value_out,
    context_out,
    spread_out,
    low_out,
    resid_out,
    final_out,
    up_q,
    up_k,
    up_v,
    down_out,
    up_out,
    *scratch,
):
    (
        own,
        rows_out,
        base,
        ffn,
        normed,
        down_qkv,
        held_qkv,
        turned,
        held_in,
        held_down,
        w_out,
        sems,
        pool,
        near_out,
        near_in,
        far_out,
        far_in,
    ) = scratch[16:]
    shards = pool.shape[0]
    splits = shards.bit_length() - 1
    me = lax.axis_index("dp")
    lane = lax.axis_index("mp")
    mates = [me + 2**k * (1 - 2 * ((me // 2**k) % 2)) for k in range(splits)]
    peers = [lax.rem(lane + offset, count) for offset in range(count)]
    barrier = pltpu.get_barrier_semaphore()
    for mate in mates:
        pl.semaphore_signal(barrier, inc=1, device_id={"dp": mate, "mp": lane}, device_id_type=MESH)
    for peer in peers[1:]:
        pl.semaphore_signal(barrier, inc=1, device_id={"dp": me, "mp": peer}, device_id_type=MESH)
    pl.semaphore_wait(barrier, splits + count - 1)
    pool[me, lane] = master[...].astype(jnp.bfloat16)

    def near(offset):
        return pltpu.make_async_remote_copy(
            src_ref=pool.at[me, lane],
            dst_ref=pool.at[me, lane],
            send_sem=near_out.at[offset],
            recv_sem=near_in.at[offset],
            device_id={"dp": me, "mp": peers[offset]},
            device_id_type=MESH,
        )

    def far(stage):
        bit = splits - 1 - stage
        copies = []
        for place in range(2**stage):
            slot = lax.rem(me, 2 ** (bit + 1)) + place * 2 ** (bit + 1)
            copies.append(
                pltpu.make_async_remote_copy(
                    src_ref=pool.at[slot],
                    dst_ref=pool.at[slot],
                    send_sem=far_out.at[2**stage - 1 + place],
                    recv_sem=far_in.at[2**stage - 1 + place],
                    device_id={"dp": mates[bit], "mp": lane},
                    device_id_type=MESH,
                )
            )
        return copies

    for offset in range(1, count):
        near(offset).start()

    first, last = 4, FOLLOW_LAG - 6
    waits = (
        [first]
        + [
            first + (last - first) * (2 ** (stage + 1) - 1) // max(1, 2 ** (splits - 1) - 1)
            for stage in range(splits - 1)
        ]
        + [FOLLOW_LAG - 1]
    )

    own_rows = pool.shape[3]
    span = count * own_rows

    def strip(shard, matrix):
        return jnp.concatenate(
            [pool[shard, m, matrix].astype(jnp.float32) for m in range(count)], 0
        ).astype(jnp.bfloat16)

    def lay_out():
        def one(shard, carry):
            rows = line_chunk(shard, span)
            for kind in range(3):
                down_qkv[rows, kind * R : (kind + 1) * R] = strip(shard, kind)
            up_out[rows, :] = strip(shard, 7)
            return carry

        lax.fori_loop(0, shards, one, 0)
        each = shards // count
        for matrix, ref in ((3, up_q), (4, up_k), (5, up_v), (6, down_out)):
            for t in range(each):
                ref[t * span : (t + 1) * span, :] = strip(lane * each + t, matrix)

    def gather_adapters(at):
        for stage in range(splits + 1):

            @pl.when(at == waits[stage])
            def _(stage=stage):
                if stage == 0:
                    for offset in range(1, count):
                        near(offset).wait_recv()
                else:
                    for copy in far(stage - 1):
                        copy.wait_recv()
                if stage < splits:
                    for copy in far(stage):
                        copy.start()
                else:
                    lay_out()

    loads = [
        pltpu.make_async_copy(src, dst, sems.at[slot])
        for slot, (src, dst) in enumerate(
            ((w_qkv, held_qkv), (w_in, held_in), (w_down, held_down), (w_wide, w_out))
        )
    ]
    for load in loads:
        load.start()

    def emit_start(rows, total):
        rows_out[rows, :] = total.astype(jnp.bfloat16)
        centre = total - jnp.mean(total, -1, keepdims=True)
        spread = jnp.mean(centre * centre, -1, keepdims=True)
        flat = centre * lax.rsqrt(spread + NORM_EPS)
        attn_out[rows, :] = (flat * gain[0:1, :] + shift[0:1, :]).astype(jnp.bfloat16)
        normed[rows, :] = (flat * gain[1:2, :] + shift[1:2, :]).astype(jnp.bfloat16)

    per = WORK_ROWS // LINE_CHUNK

    def follow(ready):
        @pl.when(ready == per - 1)
        def _():
            for load in loads:
                load.wait()
            heads = held_qkv.shape[1] // (3 * HD)
            for kind in range(3):
                for head in range(heads):
                    into = (kind * heads + head) * HD
                    source = (head * 3 + kind) * HD
                    turned[:, into : into + HD] = held_qkv[:, source : source + HD]

        @pl.when(lax.rem(ready, per) == per - 1)
        def _():
            rows = line_chunk(ready // per, WORK_ROWS)
            base[rows, :] = jnp.dot(
                attn_out[rows, :], turned[...], preferred_element_type=jnp.float32
            )
            pre = (
                jnp.dot(normed[rows, :], held_in[...], preferred_element_type=jnp.float32)
                + bias[...]
            )
            hidden = (0.5 * pre * (1.0 + lax.erf(pre * 0.5**0.5))).astype(jnp.bfloat16)
            ffn[rows, :] = jnp.dot(
                hidden, held_down[...], preferred_element_type=jnp.float32
            ).astype(jnp.bfloat16)

    group = w_out.shape[0]
    total_rows = own.shape[0]
    key_out[...] = jnp.zeros_like(key_out)
    value_out[...] = jnp.zeros_like(value_out)

    def attend(block):
        rows = line_chunk(block, WORK_ROWS)
        low = jnp.dot(
            attn_out[rows, :], down_qkv[...], preferred_element_type=jnp.float32
        ).astype(jnp.bfloat16)
        inner_out[rows, :] = low
        for kind, (up, out) in enumerate(
            ((up_q, query_out), (up_k, key_out), (up_v, value_out))
        ):
            extra = lax.dot_general(
                low[:, kind * R : (kind + 1) * R],
                up[...],
                CROSS,
                preferred_element_type=jnp.float32,
            )
            for at in range(0, group, 128):
                field = base[rows, kind * group + at : kind * group + at + 128]
                field = field + extra[:, at : at + 128]
                if kind < 2:
                    field = turn_pairs(field, cosine[rows, :], sine[rows, :], 1.0)
                out[rows, at : at + 128] = field.astype(jnp.bfloat16)
        lane = lax.broadcasted_iota(jnp.int32, (WORK_ROWS, 128), 1)
        column = lax.broadcasted_iota(jnp.int32, (WORK_ROWS, total_rows), 1)
        place = lax.broadcasted_iota(jnp.int32, (WORK_ROWS, total_rows), 0)
        seen = column <= place + block * WORK_ROWS
        spreads = jnp.zeros((WORK_ROWS, 128), jnp.float32)
        for at in range(0, group, 128):
            pair = query_out[rows, at : at + 128]
            keys = key_out[:, at : at + 128]
            values = value_out[:, at : at + 128]
            results = []
            for side in range(128 // HD):
                mine = jnp.where(lane // HD == side, pair, jnp.zeros_like(pair))
                scores = (
                    lax.dot_general(mine, keys, CROSS, preferred_element_type=jnp.float32)
                    * HD**-0.5
                )
                scores = jnp.where(seen, scores, -1e30)
                top = jnp.max(scores, -1, keepdims=True)
                weights = jnp.exp(scores - top)
                total = jnp.sum(weights, -1, keepdims=True)
                probs = (weights * (1.0 / total)).astype(jnp.bfloat16)
                results.append(jnp.dot(probs, values, preferred_element_type=jnp.float32))
                head = at // HD + side
                spreads = jnp.where(lane == head, top + jnp.log(total), spreads)
            joined = results[0]
            for side in range(1, 128 // HD):
                joined = jnp.where(lane // HD == side, results[side], joined)
            context_out[rows, at : at + 128] = joined.astype(jnp.bfloat16)
        spread_out[rows, :] = spreads
        context = context_out[rows, :]
        low = jnp.dot(context, down_out[...], preferred_element_type=jnp.float32).astype(
            jnp.bfloat16
        )
        low_out[rows, :] = low
        own[rows, :] = (
            jnp.dot(context, w_out[...], preferred_element_type=jnp.float32)
            + lax.dot_general(low, up_out[...], CROSS, preferred_element_type=jnp.float32)
            + ffn[rows, :].astype(jnp.float32)
        ).astype(jnp.bfloat16)

    def emit_resid(rows, total):
        resid = rows_out[rows, :].astype(jnp.float32) + total
        resid_out[rows, :] = resid
        normed = layer_norm(resid, gain[2:3, :], shift[2:3, :])
        final_out[rows, :] = normed.astype(jnp.bfloat16)

    chunks = total_rows // LINE_CHUNK
    clear, step, drain, steps = line_parts(
        count, LINE_CHUNK, part, scratch[0:4], scratch[4:8], emit_start, follow
    )
    clear_next, step_next, drain_next, steps_next = line_parts(
        count, LINE_CHUNK, own, scratch[8:12], scratch[12:16], emit_resid
    )
    clear()
    clear_next()

    def turn(at, carry):
        gather_adapters(at)
        step(at)
        later = at - FOLLOW_LAG

        @pl.when((later >= 0) & (later < chunks) & (lax.rem(later, per) == 0))
        def _():
            attend(later // per)

        step_next(later)
        return carry

    lax.fori_loop(0, FOLLOW_LAG + steps_next, turn, 0)
    drain()
    drain_next()
    for offset in range(1, count):
        near(offset).wait_send()
    for stage in range(splits):
        for copy in far(stage):
            copy.wait_send()


DOWN = (((0,), (0,)), ((), ()))


def branch_kernel(count, raw, hits, stats, gain, up_q, up_k, up_v, down_out, *refs):
    prompts, totals = refs[0:2]
    sources = refs[2:15]
    loss_out = refs[15]
    grad_down = refs[16:19]
    grad_out_b = refs[19]
    grad_up = refs[20:23]
    grad_out_a = refs[23]
    scratch = refs[24:]
    own, note_send, note_recv, scales, note_out, note_in = scratch[8:14]
    held = scratch[14:27]
    sems, out, query_grad, key_turned, value_turned, out_b_turned, out_a_turned = scratch[27:]
    (
        resid,
        queries,
        keys,
        values,
        context,
        spreads,
        inner,
        low,
        attn,
        w_out,
        up_out,
        cosine,
        sine,
    ) = held
    me = lax.axis_index("mp")
    rows_all = raw.shape[0]
    group = w_out.shape[0]
    loads = [
        pltpu.make_async_copy(src, dst, sems.at[slot])
        for slot, (src, dst) in enumerate(zip(sources, held))
    ]
    for load in loads:
        load.start()
    greet_peers(me, count)
    note_send[...] = stats[...].T[0:8, :]
    copies = []
    for offset in range(1, count):
        copy = pltpu.make_async_remote_copy(
            src_ref=note_send,
            dst_ref=note_recv.at[offset],
            send_sem=note_out.at[offset],
            recv_sem=note_in.at[offset],
            device_id={"mp": lax.rem(me + offset, count)},
            device_id_type=MESH,
        )
        copy.start()
        copies.append(copy)
    for ref in (key_turned, value_turned, out_b_turned, out_a_turned):
        ref[...] = jnp.zeros_like(ref)
    mine = note_send[...]
    for copy in copies:
        copy.wait_recv()
    others = [mine] + [note_recv[offset] for offset in range(1, count)]
    top = functools.reduce(jnp.maximum, [part[0:1, :] for part in others])
    total = sum(part[1:2, :] * jnp.exp(part[0:1, :] - top) for part in others)
    found = sum(part[2:3, :] for part in others)
    spread_row = top + jnp.log(total)
    amount = sum(totals[e] - prompts[e] for e in range(prompts.shape[0]))
    example = lax.axis_index("dp")
    position = lax.broadcasted_iota(jnp.int32, (1, rows_all), 1)
    keep = (position >= prompts[example] - 1) & (position < totals[example] - 1)
    share = jnp.where(keep, 1.0 / jnp.broadcast_to(amount, (1, rows_all)).astype(jnp.float32), 0.0)
    loss_out[...] = (spread_row - found) * share
    factor = jnp.exp(mine[0:1, :] - spread_row) * share
    pair = jnp.concatenate([factor, share, jnp.zeros((126, rows_all), jnp.float32)], 0)
    scales[...] = pair.T
    for load in loads:
        load.wait()

    def prepare(at):
        rows = line_chunk(at, LINE_CHUNK)
        scale = scales[rows, :]
        own[rows, :] = (
            raw[rows, :] * scale[:, 0:1] - hits[rows, :].astype(jnp.float32) * scale[:, 1:2]
        ).astype(jnp.bfloat16)

    def emit(rows, total):
        values_here = resid[rows, :]
        centre = values_here - jnp.mean(values_here, -1, keepdims=True)
        spread = jnp.mean(centre * centre, -1, keepdims=True)
        inverse = lax.rsqrt(spread + NORM_EPS)
        normed = centre * inverse
        up = total * gain[2:3, :]
        out[rows, :] = (
            inverse
            * (
                up
                - jnp.mean(up, -1, keepdims=True)
                - normed * jnp.mean(up * normed, -1, keepdims=True)
            )
        ).astype(jnp.bfloat16)

    def attend_back(block):
        rows = line_chunk(block, WORK_ROWS)
        upstream = out[rows, :]
        low_grad = jnp.dot(upstream, up_out[...], preferred_element_type=jnp.float32).astype(
            jnp.bfloat16
        )
        grads = (
            lax.dot_general(upstream, w_out[...], CROSS, preferred_element_type=jnp.float32)
            + lax.dot_general(low_grad, down_out[...], CROSS, preferred_element_type=jnp.float32)
        ).astype(jnp.bfloat16)
        out_b_turned[...] += lax.dot_general(
            low[rows, :], upstream, DOWN, preferred_element_type=jnp.float32
        )
        out_a_turned[...] += lax.dot_general(
            low_grad, context[rows, :], DOWN, preferred_element_type=jnp.float32
        )
        lane = lax.broadcasted_iota(jnp.int32, (WORK_ROWS, 128), 1)
        column = lax.broadcasted_iota(jnp.int32, (WORK_ROWS, rows_all), 1)
        place = lax.broadcasted_iota(jnp.int32, (WORK_ROWS, rows_all), 0)
        seen = column <= place + block * WORK_ROWS
        for at in range(0, group, 128):
            pick = slice(at, at + 128)
            joined = jnp.zeros((WORK_ROWS, 128), jnp.float32)
            key_part = jnp.zeros((128, rows_all), jnp.float32)
            value_part = jnp.zeros((128, rows_all), jnp.float32)
            for side in range(128 // HD):
                head = at // HD + side
                here = lane // HD == side
                query = jnp.where(here, queries[rows, pick], jnp.zeros((), jnp.bfloat16))
                grad = jnp.where(here, grads[:, pick], jnp.zeros((), jnp.bfloat16))
                scores = (
                    lax.dot_general(
                        query, keys[:, pick], CROSS, preferred_element_type=jnp.float32
                    )
                    * HD**-0.5
                )
                scores = jnp.where(seen, scores, -1e30)
                probs = jnp.exp(scores - spreads[rows, head : head + 1])
                prob_grad = lax.dot_general(
                    grad, values[:, pick], CROSS, preferred_element_type=jnp.float32
                )
                mean = jnp.sum(probs * prob_grad, -1, keepdims=True)
                score_grad = (probs * (prob_grad - mean)).astype(jnp.bfloat16)
                result = jnp.dot(score_grad, keys[:, pick], preferred_element_type=jnp.float32)
                joined = jnp.where(here, result, joined)
                key_part += lax.dot_general(
                    query, score_grad, DOWN, preferred_element_type=jnp.float32
                )
                value_part += lax.dot_general(
                    grad, probs.astype(jnp.bfloat16), DOWN, preferred_element_type=jnp.float32
                )
            key_turned[pick, :] += key_part
            value_turned[pick, :] += value_part
            query_grad[rows, pick] = turn_pairs(
                joined * HD**-0.5, cosine[rows, :], sine[rows, :], -1.0
            ).astype(jnp.bfloat16)

    per = WORK_ROWS // LINE_CHUNK

    def follow(ready):
        @pl.when(lax.rem(ready, per) == per - 1)
        def _():
            attend_back(ready // per)

    line_sum(
        count,
        LINE_CHUNK,
        own,
        scratch[:4],
        scratch[4:8],
        prepare,
        emit,
        follow=follow,
    )
    key_grad = jnp.concatenate(
        [
            turn_pairs(
                key_turned[at : at + 128, :].T * HD**-0.5, cosine[...], sine[...], -1.0
            ).astype(jnp.bfloat16)
            for at in range(0, group, 128)
        ],
        1,
    )
    value_grad = value_turned[...].T.astype(jnp.bfloat16)
    for kind, (grad, up) in enumerate(
        ((query_grad[...], up_q), (key_grad, up_k), (value_grad, up_v))
    ):
        wide = jnp.dot(grad, up[...], preferred_element_type=jnp.float32)
        high = wide.astype(jnp.bfloat16)
        rest = (wide - high.astype(jnp.float32)).astype(jnp.bfloat16)
        turned = lax.dot_general(high, attn[...], DOWN, preferred_element_type=jnp.float32)
        turned += lax.dot_general(rest, attn[...], DOWN, preferred_element_type=jnp.float32)
        grad_down[kind][...] = turned.T
        grad_up[kind][...] = lax.dot_general(
            inner[:, kind * R : (kind + 1) * R], grad, DOWN, preferred_element_type=jnp.float32
        ).T
    grad_out_b[...] = out_b_turned[...].T
    grad_out_a[...] = out_a_turned[...].T
    for copy in copies:
        copy.wait_send()


def loss_kernel(vocab, tile, values, ahead, behind, hits, acc, stats, logits, probs, tops, sums):
    at = pl.program_id(0)
    tiles = pl.num_programs(0) - 1
    rows_all = values.shape[0]

    @pl.when(at == 0)
    def _():
        acc[...] = jnp.zeros_like(acc)
        tops[...] = jnp.full_like(tops, -1e29)
        sums[...] = jnp.zeros_like(sums)
        logits[...] = jnp.full_like(logits, -1e30)

    tail = vocab % tile
    if tail:

        @pl.when(at >= tiles - 1)
        def _():
            ahead[tail:, :] = jnp.zeros((tile - tail, ahead.shape[1]), ahead.dtype)

        @pl.when(at >= tiles)
        def _():
            behind[tail:, :] = jnp.zeros((tile - tail, behind.shape[1]), behind.dtype)

    ids = (at - 1) * tile + lax.broadcasted_iota(jnp.int32, (1, tile), 1)
    scores = logits[...] + jnp.where(ids < vocab, 0.0, -1e30)
    old = tops[:, 0:1]
    new = jnp.maximum(old, jnp.max(scores, -1, keepdims=True))
    weights = jnp.exp(scores - new)
    shrink = jnp.exp(old - new)
    sums[...] = sums[...] * shrink + jnp.sum(weights, -1, keepdims=True)
    tops[...] = jnp.broadcast_to(new, tops.shape)
    acc[...] = acc[...] * shrink
    probs[...] = weights.astype(jnp.bfloat16)
    logits[...] = lax.dot_general(
        values[...], ahead[...], (((1,), (1,)), ((), ())), preferred_element_type=jnp.float32
    )
    acc[...] += jnp.dot(probs[...], behind[...], preferred_element_type=jnp.float32)

    @pl.when(at == tiles)
    def _():
        found = jnp.sum(
            values[...].astype(jnp.float32) * hits[...].astype(jnp.float32), -1, keepdims=True
        )
        column = lax.broadcasted_iota(jnp.int32, (rows_all, 128), 1)
        stats[...] = jnp.where(
            column == 0, tops[...], jnp.where(column == 1, sums[...], found)
        )


LOSS_TILE = 512


def loss_call(values, head_rows, hits):
    rows, width = values.shape
    vocab = head_rows.shape[0]
    tile = LOSS_TILE
    tiles = pl.cdiv(vocab, tile)
    whole = pl.BlockSpec((rows, width), lambda j: (0, 0))
    return pl.pallas_call(
        functools.partial(loss_kernel, vocab, tile),
        name="loss",
        grid=(tiles + 1,),
        in_specs=[
            whole,
            pl.BlockSpec((tile, width), lambda j: (jnp.minimum(j, tiles - 1), 0)),
            pl.BlockSpec((tile, width), lambda j: (jnp.maximum(j - 1, 0), 0)),
            whole,
        ],
        out_specs=[whole, pl.BlockSpec((rows, 128), lambda j: (0, 0))],
        out_shape=[
            jax.ShapeDtypeStruct((rows, width), jnp.float32),
            jax.ShapeDtypeStruct((rows, 128), jnp.float32),
        ],
        scratch_shapes=[
            pltpu.VMEM((rows, tile), jnp.float32),
            pltpu.VMEM((rows, tile), jnp.bfloat16),
            pltpu.VMEM((rows, 128), jnp.float32),
            pltpu.VMEM((rows, 128), jnp.float32),
        ],
        compiler_params=pltpu.CompilerParams(vmem_limit_bytes=VMEM_LIMIT),
        cost_estimate=pl.CostEstimate(
            flops=4 * rows * width * vocab,
            bytes_accessed=4 * width * vocab,
            transcendentals=rows * vocab,
        ),
    )(values, head_rows, head_rows, hits)


def fold_kernel(splits, count, *refs):
    fulls = refs[0:4]
    groups = refs[4:8]
    losses, master, first, second, bases = refs[8:13]
    loss_out, norm_out, first_out, second_out, master_out = refs[13:18]
    scratch = refs[18:]
    sends = scratch[0:splits]
    recvs = scratch[splits : 2 * splits]
    keeps = scratch[2 * splits : 3 * splits]
    (line_send, line_recv, turn_send, turn_recv, note_send, note_recv, tell_send, tell_recv) = scratch[
        3 * splits : 3 * splits + 8
    ]
    (half_out, half_in, line_out, line_in, turn_out, turn_in, note_out, note_in, tell_out, tell_in) = (
        scratch[3 * splits + 8 :]
    )
    shards = 2**splits
    me = lax.axis_index("dp")
    lane = lax.axis_index("mp")
    full_rows = fulls[0].shape[0] // shards
    group_rows = groups[0].shape[0] // shards
    own_rows = full_rows // count
    bits = [(me // 2**k) % 2 for k in range(splits)]
    mates = [me + 2**k * (1 - 2 * bits[k]) for k in range(splits)]
    peers = [lax.rem(lane + offset, count) for offset in range(count)]
    spot = lane * shards + me
    goal = (spot // count, lax.rem(spot, count))
    place = me * count + lane
    origin = (lax.rem(place, shards), place // shards)
    moved = spot != place

    barrier = pltpu.get_barrier_semaphore()
    for mate in mates:
        pl.semaphore_signal(barrier, inc=1, device_id={"dp": mate, "mp": lane}, device_id_type=MESH)
    for peer in peers[1:]:
        pl.semaphore_signal(barrier, inc=1, device_id={"dp": me, "mp": peer}, device_id_type=MESH)

    @pl.when(moved)
    def _():
        for device in (goal, origin):
            pl.semaphore_signal(
                barrier, inc=1, device_id={"dp": device[0], "mp": device[1]}, device_id_type=MESH
            )

    pl.semaphore_wait(barrier, splits + count - 1 + jnp.where(moved, 2, 0))

    def remote(src, dst, out_sem, in_sem, device):
        return pltpu.make_async_remote_copy(
            src_ref=src,
            dst_ref=dst,
            send_sem=out_sem,
            recv_sem=in_sem,
            device_id={"dp": device[0], "mp": device[1]},
            device_id_type=MESH,
        )

    def piece(index):
        whole = pl.ds(pl.multiple_of(index * full_rows, full_rows), full_rows)
        part = pl.ds(pl.multiple_of(index * group_rows, group_rows), group_rows)
        return jnp.concatenate(
            [ref[whole, :] for ref in fulls] + [ref[part, :] for ref in groups], 0
        )

    started = []
    current = piece
    for k in range(splits):
        half = shards >> (k + 1)
        for i in range(half):
            sends[k][i] = current(2 * i + 1 - bits[k]).astype(jnp.bfloat16)
        copy = remote(sends[k], recvs[k], half_out.at[k], half_in.at[k], (mates[k], lane))
        copy.start()
        started.append(copy)
        for i in range(half):
            keeps[k][i] = current(2 * i + bits[k])
        copy.wait_recv()
        current = functools.partial(
            lambda kept, came, i: kept[i] + came[i].astype(jnp.float32), keeps[k], recvs[k]
        )
    final = keeps[splits - 1]
    final[0] = current(0)

    def chosen(peer):
        return jnp.concatenate(
            [
                final[
                    0,
                    pl.ds(pl.multiple_of(a * full_rows + peer * own_rows, own_rows), own_rows),
                    :,
                ]
                for a in range(4)
            ],
            0,
        )

    turn_send[...] = final[0, 4 * full_rows :, :].astype(jnp.bfloat16)
    turn = remote(turn_send, turn_recv, turn_out, turn_in, goal)

    @pl.when(moved)
    def _():
        turn.start()

    for offset in range(1, count):
        line_send[offset] = chosen(peers[offset]).astype(jnp.bfloat16)
        copy = remote(
            line_send.at[offset],
            line_recv.at[offset],
            line_out.at[offset],
            line_in.at[offset],
            (me, peers[offset]),
        )
        copy.start()
        started.append(copy)
    total = chosen(lane)

    @pl.when(moved)
    def _():
        turn.wait()

    @pl.when(jnp.logical_not(moved))
    def _():
        turn_recv[...] = turn_send[...]

    for copy in started[splits:]:
        copy.wait_recv()
    for offset in range(1, count):
        total = total + line_recv[offset].astype(jnp.float32)
    part = turn_recv[...].astype(jnp.float32)

    column = lax.broadcasted_iota(jnp.int32, (8, 128), 1)
    row = lax.broadcasted_iota(jnp.int32, (8, 128), 0)
    squares = jnp.sum(total * total) + jnp.sum(part * part)
    spot_norm = (row == 0) & (column == 0)
    spot_loss = (row == 0) & (column == 1)
    note = jnp.where(spot_norm, squares, 0.0) + jnp.where(spot_loss, jnp.sum(losses[...]), 0.0)

    def rows_of(index):
        source, slot = (total, (0, 1, 2, 7).index(index)) if index in (0, 1, 2, 7) else (
            part,
            index - 3,
        )
        return source[slot * own_rows : (slot + 1) * own_rows, :]

    turned = [
        jnp.dot(
            rows_of(m), bases[m], precision=HIGH_PRECISION, preferred_element_type=jnp.float32
        )
        for m in range(8)
    ]
    for k in range(splits):
        note_send[k] = note
        copy = remote(
            note_send.at[k], note_recv.at[k], note_out.at[k], note_in.at[k], (mates[k], lane)
        )
        copy.start()
        started.append(copy)
        copy.wait_recv()
        note = note + note_recv[k]
    tell_send[...] = note
    tells = []
    for offset in range(1, count):
        copy = remote(
            tell_send,
            tell_recv.at[offset],
            tell_out.at[offset],
            tell_in.at[offset],
            (me, peers[offset]),
        )
        copy.start()
        tells.append(copy)
    for copy in tells:
        copy.wait_recv()
    everything = note
    for offset in range(1, count):
        everything = everything + tell_recv[offset]
    norm = jnp.sqrt(jnp.sum(jnp.where(spot_norm, everything, 0.0), keepdims=True))
    loss_out[...] = jnp.sum(jnp.where(spot_loss, note, 0.0), keepdims=True)
    norm_out[...] = norm
    factor = jnp.minimum(1.0, CLIP_LIMIT / norm)
    for m in range(8):
        rotated = turned[m] * factor
        new_first = BETA_FIRST * first[m] + (1.0 - BETA_FIRST) * rotated
        new_second = BETA_SECOND * second[m] + (1.0 - BETA_SECOND) * rotated * rotated
        first_out[m] = new_first
        second_out[m] = new_second
        normed = (
            new_first
            / (1.0 - BETA_FIRST**ADAM_STEP)
            / (jnp.sqrt(new_second / (1.0 - BETA_SECOND**ADAM_STEP)) + ADAM_EPS)
        )
        back = lax.dot_general(
            normed,
            bases[m],
            (((1,), (1,)), ((), ())),
            precision=HIGH_PRECISION,
            preferred_element_type=jnp.float32,
        )
        master_out[m] = master[m] - LEARN_RATE * (back + DECAY_RATE * master[m])
    for copy in started + tells:
        copy.wait_send()


def fold_call(fulls, groups, losses, master, first_moment, second_moment, bases):
    shards = lax.axis_size("dp")
    count = lax.axis_size("mp")
    splits = shards.bit_length() - 1
    width = fulls[0].shape[1]
    pile = 4 * (fulls[0].shape[0] + groups[0].shape[0]) // shards
    own = 4 * fulls[0].shape[0] // (shards * count)
    low = jnp.bfloat16
    halves = [shards >> (k + 1) for k in range(splits)]
    dma = pltpu.SemaphoreType.DMA
    scratch = (
        [pltpu.VMEM((half, pile, width), low) for half in halves] * 2
        + [pltpu.VMEM((half, pile, width), jnp.float32) for half in halves]
        + [pltpu.VMEM((count, own, width), low)] * 2
        + [pltpu.VMEM((4 * groups[0].shape[0] // shards, width), low)] * 2
        + [pltpu.VMEM((splits, 8, 128), jnp.float32)] * 2
        + [pltpu.VMEM((8, 128), jnp.float32), pltpu.VMEM((count, 8, 128), jnp.float32)]
        + [dma((splits,))] * 2
        + [dma((count,))] * 2
        + [dma(())] * 2
        + [dma((splits,))] * 2
        + [dma((count,))] * 2
    )
    scalar = jax.ShapeDtypeStruct((1, 1), jnp.float32)
    state = jax.ShapeDtypeStruct(master.shape, jnp.float32)
    return line_call(
        functools.partial(fold_kernel, splits, count),
        "fold",
        3,
        [scalar, scalar, state, state, state],
        scratch,
        [*fulls, *groups, losses, master, first_moment, second_moment, bases],
    )


def per_device(
    token_ids,
    prompt_len,
    example_len,
    embedding,
    w_qkv,
    w_out,
    w_in,
    b_in,
    w_down,
    unembed,
    ln_gain,
    ln_bias,
    master,
    first_moment,
    second_moment,
    eigen_bases,
):
    group_count = lax.axis_size("mp")
    group_index = lax.axis_index("mp")
    head_rows = lax.all_gather(unembed.T, "dp", axis=1, tiled=True)
    examples, length = token_ids.shape
    width = embedding.shape[0]
    vocab_local = head_rows.shape[0]
    rows = examples * length
    local_heads = HEADS // group_count
    group_width = local_heads * HD
    flat_ids = token_ids.reshape(rows)
    picked = pick_call(flat_ids - group_index * width, embedding, "pick_start")
    shape_low = jax.ShapeDtypeStruct((rows, D), jnp.bfloat16)
    shape_wide = jax.ShapeDtypeStruct((rows, D), jnp.float32)
    shards = lax.axis_size("dp")
    own_rows = master.shape[1]
    pool_shape = (shards, group_count, 8, own_rows, R)
    target = jnp.roll(token_ids, -1, axis=1).reshape(rows)
    cosine, sine = rope_tables(length)
    rest = jnp.zeros((length, HD - ROT), jnp.float32)
    wide_cosine = jnp.concatenate([cosine[:, 0], cosine[:, 0], rest + 1.0] * (128 // HD), 1)
    wide_sine = jnp.concatenate([-sine[:, 0], sine[:, 0], rest] * (128 // HD), 1)
    shape_group = jax.ShapeDtypeStruct((rows, group_width), jnp.bfloat16)
    low = jnp.bfloat16
    shape_up = jax.ShapeDtypeStruct((group_width, R), low)
    (
        normed_attn,
        inner,
        queries,
        key_rows,
        value_rows,
        context,
        spread_lanes,
        inner_out,
        resid,
        final_rows,
        up_q,
        up_k,
        up_v,
        down_out,
        up_out,
    ) = line_call(
        functools.partial(forward_kernel, group_count),
        "forward",
        0,
        [
            shape_low,
            jax.ShapeDtypeStruct((rows, 3 * R), low),
            shape_group,
            shape_group,
            shape_group,
            shape_group,
            jax.ShapeDtypeStruct((rows, 128), jnp.float32),
            jax.ShapeDtypeStruct((rows, R), low),
            shape_wide,
            shape_low,
            shape_up,
            shape_up,
            shape_up,
            shape_up,
            jax.ShapeDtypeStruct((D, R), low),
        ],
        line_scratch(rows, D) * 2
        + [
            pltpu.VMEM((rows, D), low),
            pltpu.VMEM((rows, D), low),
            pltpu.VMEM((rows, w_qkv.shape[1]), jnp.float32),
            pltpu.VMEM((rows, D), low),
            pltpu.VMEM((rows, D), low),
            pltpu.VMEM((D, 3 * R), low),
            pltpu.VMEM(w_qkv.shape, low),
            pltpu.VMEM(w_qkv.shape, low),
            pltpu.VMEM(w_in.shape, low),
            pltpu.VMEM(w_down.shape, low),
            pltpu.VMEM(w_out.shape, low),
            pltpu.SemaphoreType.DMA((4,)),
            pltpu.VMEM(pool_shape, low),
        ]
        + [pltpu.SemaphoreType.DMA((group_count,))] * 2
        + [pltpu.SemaphoreType.DMA((shards - 1,))] * 2,
        [
            picked,
            ln_gain,
            ln_bias,
            b_in.reshape(1, -1),
            master,
            wide_cosine,
            wide_sine,
            w_qkv,
            w_in,
            w_down,
            w_out,
        ],
        spaces=(pl.ANY,) * 4,
    )
    goal = target - group_index * vocab_local
    hits = pick_call(goal, head_rows, "pick_target")
    raw_grad, stats = loss_call(final_rows, head_rows, hits)
    late = [
        resid,
        queries,
        key_rows,
        value_rows,
        context,
        spread_lanes,
        inner,
        inner_out,
        normed_attn,
        w_out,
        up_out,
        wide_cosine,
        wide_sine,
    ]
    tall = jax.ShapeDtypeStruct((D, R), jnp.float32)
    short = jax.ShapeDtypeStruct((group_width, R), jnp.float32)
    losses, grad_q, grad_k, grad_v, grad_out_b, *local_grads = line_call(
        functools.partial(branch_kernel, group_count),
        "branch_rows",
        2,
        [jax.ShapeDtypeStruct((1, rows), jnp.float32)] + [tall] * 4 + [short] * 4,
        line_scratch(rows, D)
        + [
            pltpu.VMEM((rows, D), jnp.bfloat16),
            pltpu.VMEM((8, rows), jnp.float32),
            pltpu.VMEM((group_count, 8, rows), jnp.float32),
            pltpu.VMEM((rows, 128), jnp.float32),
            pltpu.SemaphoreType.DMA((group_count,)),
            pltpu.SemaphoreType.DMA((group_count,)),
        ]
        + [pltpu.VMEM(value.shape, value.dtype) for value in late]
        + [
            pltpu.SemaphoreType.DMA((len(late),)),
            pltpu.VMEM((rows, D), jnp.bfloat16),
            pltpu.VMEM((rows, group_width), jnp.bfloat16),
            pltpu.VMEM((group_width, rows), jnp.float32),
            pltpu.VMEM((group_width, rows), jnp.float32),
            pltpu.VMEM((R, D), jnp.float32),
            pltpu.VMEM((R, group_width), jnp.float32),
        ],
        [
            raw_grad,
            hits,
            stats,
            ln_gain,
            up_q,
            up_k,
            up_v,
            down_out,
            prompt_len,
            example_len,
            *late,
        ],
        spaces=(pltpu.SMEM,) * 2 + (pl.ANY,) * len(late),
    )
    mean_loss, grad_norm, new_first, new_second, new_master = fold_call(
        [grad_q, grad_k, grad_v, grad_out_b],
        local_grads,
        losses,
        master,
        first_moment,
        second_moment,
        eigen_bases,
    )
    return (mean_loss.reshape(()), grad_norm.reshape(()), new_first, new_second, new_master)


def solution(mesh):
    placed = (
        P("dp", None),
        P(),
        P(),
        P("mp", None),
        P(None, "mp"),
        P("mp", None),
        P(None, "mp"),
        P("mp"),
        P("mp", None),
        P("dp", "mp"),
        P(),
        P(),
        P(None, ("dp", "mp"), None),
        P(None, ("dp", "mp"), None),
        P(None, ("dp", "mp"), None),
        P(),
    )
    return jax.shard_map(
        per_device,
        mesh=mesh,
        in_specs=placed,
        out_specs=(
            P(),
            P(),
            P(None, ("dp", "mp"), None),
            P(None, ("dp", "mp"), None),
            P(None, ("dp", "mp"), None),
        ),
        check_vma=False,
    )
```

```python
import functools

import jax
import jax.numpy as jnp
from jax import lax
from jax.experimental import pallas as pl
from jax.experimental.pallas import tpu as pltpu
from jax.sharding import PartitionSpec as P

MESH = pl.DeviceIdType.MESH
VMEM_LIMIT = 60 * 1024 * 1024

D = 1024
HEADS = 16
R = 128
ADAM_STEP = 10
HD = 64
ROT = 16


HIGH_PRECISION = lax.Precision.HIGHEST
NORM_EPS = 1e-05
ROPE_BASE = 10000.0
CLIP_LIMIT = 0.01
LEARN_RATE = 0.02
BETA_FIRST = 0.9
BETA_SECOND = 0.999
ADAM_EPS = 1e-08
DECAY_RATE = 0.01


def layer_norm(values, gain, shift):
    centre = values - jnp.mean(values, -1, keepdims=True)
    spread = jnp.mean(centre * centre, -1, keepdims=True)
    return centre * lax.rsqrt(spread + NORM_EPS) * gain + shift


def rope_tables(length):
    half = ROT // 2
    freqs = ROPE_BASE ** (-2.0 * jnp.arange(half, dtype=jnp.float32) / ROT)
    angles = jnp.arange(length, dtype=jnp.float32)[:, None] * freqs[None, :]
    return (jnp.cos(angles)[:, None, :], jnp.sin(angles)[:, None, :])


def line_chunk(index, size):
    return pl.ds(pl.multiple_of(index * size, size), size)


def greet_peers(me, count):
    barrier = pltpu.get_barrier_semaphore()
    for offset in range(1, count):
        pl.semaphore_signal(
            barrier, inc=1, device_id={"mp": lax.rem(me + offset, count)}, device_id_type=MESH
        )
    pl.semaphore_wait(barrier, count - 1)


def line_parts(count, chunk, own, wires, sems, emit, follow=None):
    me = lax.axis_index("mp")
    from_low, from_high, to_high, to_low = wires
    up_send, up_recv, down_send, down_recv = sems
    length = own.shape[0]
    chunks = length // chunk
    above = jnp.minimum(me + 1, count - 1)
    below = jnp.maximum(me - 1, 0)

    def up_copy(index):
        rows = line_chunk(index, chunk)
        return pltpu.make_async_remote_copy(
            src_ref=to_high.at[rows],
            dst_ref=from_low.at[rows],
            send_sem=up_send.at[index],
            recv_sem=up_recv.at[index],
            device_id={"mp": above},
            device_id_type=MESH,
        )

    def down_copy(index):
        rows = line_chunk(index, chunk)
        return pltpu.make_async_remote_copy(
            src_ref=to_low.at[rows],
            dst_ref=from_high.at[rows],
            send_sem=down_send.at[index],
            recv_sem=down_recv.at[index],
            device_id={"mp": below},
            device_id_type=MESH,
        )

    def clear():
        @pl.when(me == 0)
        def _():
            from_low[...] = jnp.zeros_like(from_low)

        @pl.when(me == count - 1)
        def _():
            from_high[...] = jnp.zeros_like(from_high)

    def step(at):
        up = at - LINE_LAG * me

        @pl.when((up >= 0) & (up < chunks))
        def _():
            rows = line_chunk(up, chunk)

            @pl.when(me > 0)
            def _():
                up_copy(up).wait_recv()

            @pl.when(me < count - 1)
            def _():
                to_high[rows, :] = (
                    from_low[rows, :].astype(jnp.float32) + own[rows, :].astype(jnp.float32)
                ).astype(jnp.bfloat16)
                up_copy(up).start()

        down = at - LINE_LAG * (count - 1 - me)

        @pl.when((down >= 0) & (down < chunks))
        def _():
            rows = line_chunk(down, chunk)

            @pl.when(me < count - 1)
            def _():
                down_copy(down).wait_recv()

            @pl.when(me > 0)
            def _():
                to_low[rows, :] = (
                    from_high[rows, :].astype(jnp.float32) + own[rows, :].astype(jnp.float32)
                ).astype(jnp.bfloat16)
                down_copy(down).start()

        ready = at - LINE_LAG * jnp.maximum(me, count - 1 - me)

        @pl.when((ready >= 0) & (ready < chunks))
        def _():
            rows = line_chunk(ready, chunk)
            total = (
                from_low[rows, :].astype(jnp.float32)
                + own[rows, :].astype(jnp.float32)
                + from_high[rows, :].astype(jnp.float32)
            )
            emit(rows, total)
            if follow is not None:
                follow(ready)

    def drain():
        def one(index, carry):
            @pl.when(me < count - 1)
            def _():
                up_copy(index).wait_send()

            @pl.when(me > 0)
            def _():
                down_copy(index).wait_send()

            return carry

        lax.fori_loop(0, chunks, one, 0)

    return clear, step, drain, chunks + LINE_LAG * (count - 1)


def line_sum(count, chunk, own, wires, sems, prepare, emit, follow=None):
    chunks = own.shape[0] // chunk
    clear, step, drain, steps = line_parts(count, chunk, own, wires, sems, emit, follow)
    clear()

    def turn(at, carry):
        @pl.when(at < chunks)
        def _():
            prepare(at)

        step(at)
        return carry

    lax.fori_loop(0, steps, turn, 0)
    drain()


PICK_GROUP = 32
PICK_ALIGN = 8


def pick_kernel(spots, places, table, out, held, sems):
    rows = out.shape[0]
    span = PICK_GROUP * PICK_ALIGN

    def start(group, carry):
        def one(token, carry):
            at = group * PICK_GROUP + token
            pltpu.make_async_copy(
                table.at[pl.ds(pl.multiple_of(spots[at], PICK_ALIGN), PICK_ALIGN)],
                held.at[pl.ds(pl.multiple_of(at * PICK_ALIGN, PICK_ALIGN), PICK_ALIGN)],
                sems.at[group],
            ).start()
            return carry

        return lax.fori_loop(0, PICK_GROUP, one, carry, unroll=8)

    lax.fori_loop(0, rows // PICK_GROUP, start, 0)

    def choose(group, carry):
        block = held.at[pl.ds(pl.multiple_of(group * span, span), span)]
        pltpu.make_async_copy(table.at[pl.ds(0, span)], block, sems.at[group]).wait()
        here = line_chunk(group, PICK_GROUP)
        wanted = places[here, :]
        column = lax.broadcasted_iota(jnp.int32, (PICK_GROUP, span), 1)
        chosen = jnp.where(column == wanted, 1.0, 0.0).astype(jnp.bfloat16)
        out[here, :] = jnp.dot(
            chosen, block[...], preferred_element_type=jnp.float32
        ).astype(jnp.bfloat16)
        return carry

    lax.fori_loop(0, rows // PICK_GROUP, choose, 0)


def pick_call(index, table, name):
    rows = index.shape[0]
    vocab, width = table.shape
    spread = (lax.iota(jnp.int32, rows) * PICK_ALIGN) % (vocab - PICK_ALIGN)
    safe = jnp.where((index >= 0) & (index < vocab), index, spread)
    spots = safe - safe % PICK_ALIGN
    column = index.reshape(rows, 1)
    token = lax.broadcasted_iota(jnp.int32, (rows, 1), 0) % PICK_GROUP
    places = jnp.where(
        (column >= 0) & (column < vocab), token * PICK_ALIGN + column % PICK_ALIGN, -1
    )
    return pl.pallas_call(
        pick_kernel,
        name=name,
        in_specs=[
            pl.BlockSpec(memory_space=pltpu.SMEM),
            pl.BlockSpec(memory_space=pltpu.VMEM),
            pl.BlockSpec(memory_space=pl.ANY),
        ],
        out_specs=pl.BlockSpec(memory_space=pltpu.VMEM),
        out_shape=jax.ShapeDtypeStruct((rows, width), jnp.bfloat16),
        scratch_shapes=[
            pltpu.VMEM((rows * PICK_ALIGN, width), jnp.bfloat16),
            pltpu.SemaphoreType.DMA((rows // PICK_GROUP,)),
        ],
        compiler_params=pltpu.CompilerParams(vmem_limit_bytes=VMEM_LIMIT),
        cost_estimate=pl.CostEstimate(
            flops=2 * rows * PICK_GROUP * PICK_ALIGN * width,
            bytes_accessed=2 * rows * PICK_ALIGN * width,
            transcendentals=0,
        ),
    )(spots, places, table)


LINE_CHUNK = 32
LINE_LAG = 3
WORK_ROWS = 256
FOLLOW_LAG = 28
HEAD_STEPS = (33, 48, 64)


def line_scratch(length, width):
    chunks = length // LINE_CHUNK
    return [pltpu.VMEM((length, width), jnp.bfloat16)] * 4 + [
        pltpu.SemaphoreType.DMA((chunks,))
    ] * 4


def line_call(kernel, name, collective_id, outs, scratch, operands, flops=0, spaces=(), far_outs=0):
    size = sum(o.size * o.dtype.itemsize for o in operands) + sum(
        o.size * o.dtype.itemsize for o in outs
    )
    vmem = pl.BlockSpec(memory_space=pltpu.VMEM)
    return pl.pallas_call(
        kernel,
        name=name,
        out_shape=outs,
        in_specs=[vmem] * (len(operands) - len(spaces))
        + [pl.BlockSpec(memory_space=space) for space in spaces],
        out_specs=[vmem] * (len(outs) - far_outs)
        + [pl.BlockSpec(memory_space=pl.ANY)] * far_outs,
        scratch_shapes=scratch,
        compiler_params=pltpu.CompilerParams(
            collective_id=collective_id, has_side_effects=True, vmem_limit_bytes=VMEM_LIMIT
        ),
        cost_estimate=pl.CostEstimate(
            flops=flops, bytes_accessed=size + 100_000_000, transcendentals=0
        ),
    )(*operands)


def turn_pairs(field, cosine, sine, sign):
    lane = lax.broadcasted_iota(jnp.int32, field.shape, 1) % HD
    half = ROT // 2
    other = jnp.where(
        lane < half, pltpu.roll(field, field.shape[1] - half, 1), pltpu.roll(field, half, 1)
    )
    return field * cosine + sign * other * sine


CROSS = (((1,), (1,)), ((), ()))


def forward_kernel(
    moving,
    count,
    part,
    gain,
    shift,
    bias,
    master,
    table,
    w_qkv,
    w_in,
    w_down,
    w_wide,
    *refs,
):
    head_src = refs[0] if moving else None
    refs = refs[1:] if moving else refs
    head_all = refs[17] if moving else None
    (
        attn_out,
        inner_out,
        query_out,
        key_out,
        value_out,
        context_out,
        spread_out,
        low_out,
        resid_out,
        final_out,
        up_q,
        up_k,
        up_v,
        down_out,
        up_out,
        cosine_out,
        sine_out,
    ) = refs[:17]
    scratch = refs[18:] if moving else refs[17:]
    (
        own,
        rows_out,
        base,
        ffn,
        normed,
        down_qkv,
        held_qkv,
        turned,
        held_in,
        held_down,
        w_out,
        sems,
        pool,
        near_out,
        near_in,
        far_out,
        far_in,
        *extra_sems,
    ) = scratch[16:]
    shards = pool.shape[0]
    splits = shards.bit_length() - 1
    me = lax.axis_index("dp")
    lane = lax.axis_index("mp")
    mates = [me + 2**k * (1 - 2 * ((me // 2**k) % 2)) for k in range(splits)]
    peers = [lax.rem(lane + offset, count) for offset in range(count)]
    barrier = pltpu.get_barrier_semaphore()
    for mate in mates:
        pl.semaphore_signal(barrier, inc=1, device_id={"dp": mate, "mp": lane}, device_id_type=MESH)
    for peer in peers[1:]:
        pl.semaphore_signal(barrier, inc=1, device_id={"dp": me, "mp": peer}, device_id_type=MESH)
    pl.semaphore_wait(barrier, splits + count - 1)
    pool[me, lane] = master[...].astype(jnp.bfloat16)

    def near(offset):
        return pltpu.make_async_remote_copy(
            src_ref=pool.at[me, lane],
            dst_ref=pool.at[me, lane],
            send_sem=near_out.at[offset],
            recv_sem=near_in.at[offset],
            device_id={"dp": me, "mp": peers[offset]},
            device_id_type=MESH,
        )

    def far(stage):
        bit = splits - 1 - stage
        copies = []
        for place in range(2**stage):
            slot = lax.rem(me, 2 ** (bit + 1)) + place * 2 ** (bit + 1)
            copies.append(
                pltpu.make_async_remote_copy(
                    src_ref=pool.at[slot],
                    dst_ref=pool.at[slot],
                    send_sem=far_out.at[2**stage - 1 + place],
                    recv_sem=far_in.at[2**stage - 1 + place],
                    device_id={"dp": mates[bit], "mp": lane},
                    device_id_type=MESH,
                )
            )
        return copies

    for offset in range(1, count):
        near(offset).start()

    def flip(slot, bit):
        return slot + 2**bit * (1 - 2 * ((slot // 2**bit) % 2))

    def head_copy(half, stage, place):
        order = ((2, 1, 0), (1, 2, 0))[half]
        slots = [me]
        for bit in order[:stage]:
            slots = slots + [flip(slot, bit) for slot in slots]
        slot = slots[place]
        long = head_all.shape[0] // 2
        rows = pl.ds(half * long, long)
        wide = head_src.shape[1]
        there = head_all.at[rows, pl.ds(pl.multiple_of(slot * wide, wide), wide)]
        index = half * 7 + 2**stage - 1 + place
        return pltpu.make_async_remote_copy(
            src_ref=head_src.at[rows] if place == 0 else there,
            dst_ref=there,
            send_sem=extra_sems[0].at[index],
            recv_sem=extra_sems[1].at[index],
            device_id={"dp": flip(me, order[stage]), "mp": lane},
            device_id_type=MESH,
        )

    def head_mine():
        wide = head_src.shape[1]
        return pltpu.make_async_copy(
            head_src,
            head_all.at[:, pl.ds(pl.multiple_of(me * wide, wide), wide)],
            extra_sems[2],
        )

    def head_moves(at):
        @pl.when(at == HEAD_STEPS[0])
        def _():
            for half in range(2):
                head_copy(half, 0, 0).wait_recv()
            for half in range(2):
                head_copy(half, 1, 1).start()
                head_copy(half, 2, 1).start()

        @pl.when(at == HEAD_STEPS[1])
        def _():
            for half in range(2):
                head_copy(half, 1, 0).wait_recv()
                head_copy(half, 2, 2).start()

        @pl.when(at == HEAD_STEPS[2])
        def _():
            for half in range(2):
                head_copy(half, 1, 1).wait_recv()
                head_copy(half, 2, 3).start()

    first, last = 3, 13
    waits = (
        [first]
        + [
            first + (last - first) * (2 ** (stage + 1) - 1) // max(1, 2 ** (splits - 1) - 1)
            for stage in range(splits - 1)
        ]
        + [FOLLOW_LAG - 1]
    )

    own_rows = pool.shape[3]
    span = count * own_rows

    def strip(shard, matrix):
        return jnp.concatenate(
            [pool[shard, m, matrix].astype(jnp.float32) for m in range(count)], 0
        ).astype(jnp.bfloat16)

    def lay_out():
        def one(shard, carry):
            rows = line_chunk(shard, span)
            for kind in range(3):
                down_qkv[rows, kind * R : (kind + 1) * R] = strip(shard, kind)
            up_out[rows, :] = strip(shard, 7)
            return carry

        lax.fori_loop(0, shards, one, 0)
        each = shards // count
        for matrix, ref in ((3, up_q), (4, up_k), (5, up_v), (6, down_out)):
            for t in range(each):
                ref[t * span : (t + 1) * span, :] = strip(lane * each + t, matrix)

    def gather_adapters(at):
        for stage in range(splits + 1):

            @pl.when(at == waits[stage])
            def _(stage=stage):
                if stage == 0:
                    for offset in range(1, count):
                        near(offset).wait_recv()
                else:
                    for copy in far(stage - 1):
                        copy.wait_recv()
                if stage < splits:
                    for copy in far(stage):
                        copy.start()
                    if moving and stage == 0:
                        head_copy(0, 0, 0).start()
                        head_copy(1, 1, 0).start()
                        head_mine().start()
                    if moving and stage == 1:
                        head_copy(1, 0, 0).start()
                        head_copy(0, 1, 0).start()
                    if moving and stage == 2:
                        head_copy(0, 2, 0).start()
                        head_copy(1, 2, 0).start()
                else:
                    lay_out()

    loads = [
        pltpu.make_async_copy(src, dst, sems.at[slot])
        for slot, (src, dst) in enumerate(
            ((w_qkv, held_qkv), (w_in, held_in), (w_down, held_down), (w_wide, w_out))
        )
    ]
    for load in loads:
        load.start()

    def emit_start(rows, total):
        rows_out[rows, :] = total.astype(jnp.bfloat16)
        centre = total - jnp.mean(total, -1, keepdims=True)
        spread = jnp.mean(centre * centre, -1, keepdims=True)
        flat = centre * lax.rsqrt(spread + NORM_EPS)
        attn_out[rows, :] = (flat * gain[0:1, :] + shift[0:1, :]).astype(jnp.bfloat16)
        normed[rows, :] = (flat * gain[1:2, :] + shift[1:2, :]).astype(jnp.bfloat16)

    per = WORK_ROWS // LINE_CHUNK

    def follow(ready):
        @pl.when(ready == per - 1)
        def _():
            for load in loads:
                load.wait()
            heads = held_qkv.shape[1] // (3 * HD)
            for kind in range(3):
                for head in range(heads):
                    into = (kind * heads + head) * HD
                    source = (head * 3 + kind) * HD
                    turned[:, into : into + HD] = held_qkv[:, source : source + HD]

        @pl.when(lax.rem(ready, per) == per - 1)
        def _():
            rows = line_chunk(ready // per, WORK_ROWS)
            base[rows, :] = jnp.dot(
                attn_out[rows, :], turned[...], preferred_element_type=jnp.float32
            )
            pre = (
                jnp.dot(normed[rows, :], held_in[...], preferred_element_type=jnp.float32)
                + bias[...]
            )
            hidden = (0.5 * pre * (1.0 + lax.erf(pre * 0.5**0.5))).astype(jnp.bfloat16)
            ffn[rows, :] = jnp.dot(
                hidden, held_down[...], preferred_element_type=jnp.float32
            ).astype(jnp.bfloat16)

    group = w_out.shape[0]
    total_rows = own.shape[0]
    key_out[...] = jnp.zeros_like(key_out)
    value_out[...] = jnp.zeros_like(value_out)

    def attend(block):
        rows = line_chunk(block, WORK_ROWS)
        low = jnp.dot(
            attn_out[rows, :], down_qkv[...], preferred_element_type=jnp.float32
        ).astype(jnp.bfloat16)
        inner_out[rows, :] = low
        half = ROT // 2
        source = lax.broadcasted_iota(jnp.int32, (ROT, 128), 0)
        into = lax.broadcasted_iota(jnp.int32, (ROT, 128), 1) % HD
        turning = into < ROT
        angles = table[rows, :]
        cosine = jnp.dot(
            angles,
            jnp.where(turning & (into % half == source), 1.0, 0.0),
            precision=HIGH_PRECISION,
            preferred_element_type=jnp.float32,
        )
        lanes = lax.broadcasted_iota(jnp.int32, (WORK_ROWS, 128), 1) % HD
        cosine = jnp.where(lanes < ROT, cosine, 1.0)
        sine = jnp.dot(
            angles,
            jnp.where(
                turning & (into % half + half == source),
                jnp.where(into < half, -1.0, 1.0),
                0.0,
            ),
            precision=HIGH_PRECISION,
            preferred_element_type=jnp.float32,
        )
        cosine_out[rows, :] = cosine
        sine_out[rows, :] = sine
        for kind, (up, out) in enumerate(
            ((up_q, query_out), (up_k, key_out), (up_v, value_out))
        ):
            extra = lax.dot_general(
                low[:, kind * R : (kind + 1) * R],
                up[...],
                CROSS,
                preferred_element_type=jnp.float32,
            )
            for at in range(0, group, 128):
                field = base[rows, kind * group + at : kind * group + at + 128]
                field = field + extra[:, at : at + 128]
                if kind < 2:
                    field = turn_pairs(field, cosine, sine, 1.0)
                out[rows, at : at + 128] = field.astype(jnp.bfloat16)
        lane = lax.broadcasted_iota(jnp.int32, (WORK_ROWS, 128), 1)
        column = lax.broadcasted_iota(jnp.int32, (WORK_ROWS, total_rows), 1)
        place = lax.broadcasted_iota(jnp.int32, (WORK_ROWS, total_rows), 0)
        seen = column <= place + block * WORK_ROWS
        spreads = jnp.zeros((WORK_ROWS, 128), jnp.float32)
        for at in range(0, group, 128):
            pair = query_out[rows, at : at + 128]
            keys = key_out[:, at : at + 128]
            values = value_out[:, at : at + 128]
            results = []
            for side in range(128 // HD):
                mine = jnp.where(lane // HD == side, pair, jnp.zeros_like(pair))
                scores = (
                    lax.dot_general(mine, keys, CROSS, preferred_element_type=jnp.float32)
                    * HD**-0.5
                )
                scores = jnp.where(seen, scores, -1e30)
                top = jnp.max(scores, -1, keepdims=True)
                weights = jnp.exp(scores - top)
                total = jnp.sum(weights, -1, keepdims=True)
                probs = (weights * (1.0 / total)).astype(jnp.bfloat16)
                results.append(jnp.dot(probs, values, preferred_element_type=jnp.float32))
                head = at // HD + side
                spreads = jnp.where(lane == head, top + jnp.log(total), spreads)
            joined = results[0]
            for side in range(1, 128 // HD):
                joined = jnp.where(lane // HD == side, results[side], joined)
            context_out[rows, at : at + 128] = joined.astype(jnp.bfloat16)
        spread_out[rows, :] = spreads
        context = context_out[rows, :]
        low = jnp.dot(context, down_out[...], preferred_element_type=jnp.float32).astype(
            jnp.bfloat16
        )
        low_out[rows, :] = low
        own[rows, :] = (
            jnp.dot(context, w_out[...], preferred_element_type=jnp.float32)
            + lax.dot_general(low, up_out[...], CROSS, preferred_element_type=jnp.float32)
            + ffn[rows, :].astype(jnp.float32)
        ).astype(jnp.bfloat16)

    def emit_resid(rows, total):
        resid = rows_out[rows, :].astype(jnp.float32) + total
        resid_out[rows, :] = resid
        normed = layer_norm(resid, gain[2:3, :], shift[2:3, :])
        final_out[rows, :] = normed.astype(jnp.bfloat16)

    chunks = total_rows // LINE_CHUNK
    clear, step, drain, steps = line_parts(
        count, LINE_CHUNK, part, scratch[0:4], scratch[4:8], emit_start, follow
    )
    clear_next, step_next, drain_next, steps_next = line_parts(
        count, LINE_CHUNK, own, scratch[8:12], scratch[12:16], emit_resid
    )
    clear()
    clear_next()

    def turn(at, carry):
        gather_adapters(at)
        if moving:
            head_moves(at)
        step(at)
        later = at - FOLLOW_LAG

        @pl.when((later >= 0) & (later < chunks) & (lax.rem(later, per) == 0))
        def _():
            attend(later // per)

        step_next(later)
        return carry

    lax.fori_loop(0, FOLLOW_LAG + steps_next, turn, 0)
    drain()
    drain_next()
    for offset in range(1, count):
        near(offset).wait_send()
    for stage in range(splits):
        for copy in far(stage):
            copy.wait_send()
    if moving:
        for half in range(2):
            for place in range(4):
                head_copy(half, 2, place).wait_recv()
        head_mine().wait()
        for half in range(2):
            for stage in range(splits):
                for place in range(2**stage):
                    head_copy(half, stage, place).wait_send()


DOWN = (((0,), (0,)), ((), ()))


def branch_kernel(count, raw, hits, stats, gain, up_q, up_k, up_v, down_out, *refs):
    prompts, totals = refs[0:2]
    sources = refs[2:15]
    loss_out = refs[15]
    grad_down = refs[16:19]
    grad_out_b = refs[19]
    grad_up = refs[20:23]
    grad_out_a = refs[23]
    scratch = refs[24:]
    own, note_send, note_recv, scales, note_out, note_in = scratch[8:14]
    held = scratch[14:27]
    sems, out, query_grad, key_turned, value_turned, out_b_turned, out_a_turned = scratch[27:]
    (
        resid,
        queries,
        keys,
        values,
        context,
        spreads,
        inner,
        low,
        attn,
        w_out,
        up_out,
        cosine,
        sine,
    ) = held
    me = lax.axis_index("mp")
    rows_all = raw.shape[0]
    group = w_out.shape[0]
    loads = [
        pltpu.make_async_copy(src, dst, sems.at[slot])
        for slot, (src, dst) in enumerate(zip(sources, held))
    ]
    for load in loads:
        load.start()
    greet_peers(me, count)
    note_send[...] = stats[...].T[0:8, :]
    copies = []
    for offset in range(1, count):
        copy = pltpu.make_async_remote_copy(
            src_ref=note_send,
            dst_ref=note_recv.at[offset],
            send_sem=note_out.at[offset],
            recv_sem=note_in.at[offset],
            device_id={"mp": lax.rem(me + offset, count)},
            device_id_type=MESH,
        )
        copy.start()
        copies.append(copy)
    for ref in (key_turned, value_turned, out_b_turned, out_a_turned):
        ref[...] = jnp.zeros_like(ref)
    mine = note_send[...]
    for copy in copies:
        copy.wait_recv()
    others = [mine] + [note_recv[offset] for offset in range(1, count)]
    top = functools.reduce(jnp.maximum, [part[0:1, :] for part in others])
    total = sum(part[1:2, :] * jnp.exp(part[0:1, :] - top) for part in others)
    found = sum(part[2:3, :] for part in others)
    spread_row = top + jnp.log(total)
    amount = sum(totals[e] - prompts[e] for e in range(prompts.shape[0]))
    example = lax.axis_index("dp")
    position = lax.broadcasted_iota(jnp.int32, (1, rows_all), 1)
    keep = (position >= prompts[example] - 1) & (position < totals[example] - 1)
    share = jnp.where(keep, 1.0 / jnp.broadcast_to(amount, (1, rows_all)).astype(jnp.float32), 0.0)
    loss_out[...] = (spread_row - found) * share
    factor = jnp.exp(mine[0:1, :] - spread_row) * share
    pair = jnp.concatenate([factor, share, jnp.zeros((126, rows_all), jnp.float32)], 0)
    scales[...] = pair.T
    for load in loads:
        load.wait()

    def prepare(at):
        rows = line_chunk(at, LINE_CHUNK)
        scale = scales[rows, :]
        own[rows, :] = (
            raw[rows, :] * scale[:, 0:1] - hits[rows, :].astype(jnp.float32) * scale[:, 1:2]
        ).astype(jnp.bfloat16)

    def emit(rows, total):
        values_here = resid[rows, :]
        centre = values_here - jnp.mean(values_here, -1, keepdims=True)
        spread = jnp.mean(centre * centre, -1, keepdims=True)
        inverse = lax.rsqrt(spread + NORM_EPS)
        normed = centre * inverse
        up = total * gain[2:3, :]
        out[rows, :] = (
            inverse
            * (
                up
                - jnp.mean(up, -1, keepdims=True)
                - normed * jnp.mean(up * normed, -1, keepdims=True)
            )
        ).astype(jnp.bfloat16)

    def attend_back(block):
        rows = line_chunk(block, WORK_ROWS)
        upstream = out[rows, :]
        low_grad = jnp.dot(upstream, up_out[...], preferred_element_type=jnp.float32).astype(
            jnp.bfloat16
        )
        grads = (
            lax.dot_general(upstream, w_out[...], CROSS, preferred_element_type=jnp.float32)
            + lax.dot_general(low_grad, down_out[...], CROSS, preferred_element_type=jnp.float32)
        ).astype(jnp.bfloat16)
        out_b_turned[...] += lax.dot_general(
            low[rows, :], upstream, DOWN, preferred_element_type=jnp.float32
        )
        out_a_turned[...] += lax.dot_general(
            low_grad, context[rows, :], DOWN, preferred_element_type=jnp.float32
        )
        lane = lax.broadcasted_iota(jnp.int32, (WORK_ROWS, 128), 1)
        column = lax.broadcasted_iota(jnp.int32, (WORK_ROWS, rows_all), 1)
        place = lax.broadcasted_iota(jnp.int32, (WORK_ROWS, rows_all), 0)
        seen = column <= place + block * WORK_ROWS
        for at in range(0, group, 128):
            pick = slice(at, at + 128)
            joined = jnp.zeros((WORK_ROWS, 128), jnp.float32)
            key_part = jnp.zeros((128, rows_all), jnp.float32)
            value_part = jnp.zeros((128, rows_all), jnp.float32)
            for side in range(128 // HD):
                head = at // HD + side
                here = lane // HD == side
                query = jnp.where(here, queries[rows, pick], jnp.zeros((), jnp.bfloat16))
                grad = jnp.where(here, grads[:, pick], jnp.zeros((), jnp.bfloat16))
                scores = (
                    lax.dot_general(
                        query, keys[:, pick], CROSS, preferred_element_type=jnp.float32
                    )
                    * HD**-0.5
                )
                scores = jnp.where(seen, scores, -1e30)
                probs = jnp.exp(scores - spreads[rows, head : head + 1])
                prob_grad = lax.dot_general(
                    grad, values[:, pick], CROSS, preferred_element_type=jnp.float32
                )
                mean = jnp.sum(probs * prob_grad, -1, keepdims=True)
                score_grad = (probs * (prob_grad - mean)).astype(jnp.bfloat16)
                result = jnp.dot(score_grad, keys[:, pick], preferred_element_type=jnp.float32)
                joined = jnp.where(here, result, joined)
                key_part += lax.dot_general(
                    query, score_grad, DOWN, preferred_element_type=jnp.float32
                )
                value_part += lax.dot_general(
                    grad, probs.astype(jnp.bfloat16), DOWN, preferred_element_type=jnp.float32
                )
            key_turned[pick, :] += key_part
            value_turned[pick, :] += value_part
            query_grad[rows, pick] = turn_pairs(
                joined * HD**-0.5, cosine[rows, :], sine[rows, :], -1.0
            ).astype(jnp.bfloat16)

    per = WORK_ROWS // LINE_CHUNK

    def follow(ready):
        @pl.when(lax.rem(ready, per) == per - 1)
        def _():
            attend_back(ready // per)

    line_sum(
        count,
        LINE_CHUNK,
        own,
        scratch[:4],
        scratch[4:8],
        prepare,
        emit,
        follow=follow,
    )
    key_grad = jnp.concatenate(
        [
            turn_pairs(
                key_turned[at : at + 128, :].T * HD**-0.5, cosine[...], sine[...], -1.0
            ).astype(jnp.bfloat16)
            for at in range(0, group, 128)
        ],
        1,
    )
    value_grad = value_turned[...].T.astype(jnp.bfloat16)
    for kind, (grad, up) in enumerate(
        ((query_grad[...], up_q), (key_grad, up_k), (value_grad, up_v))
    ):
        wide = jnp.dot(grad, up[...], preferred_element_type=jnp.float32)
        high = wide.astype(jnp.bfloat16)
        rest = (wide - high.astype(jnp.float32)).astype(jnp.bfloat16)
        turned = lax.dot_general(high, attn[...], DOWN, preferred_element_type=jnp.float32)
        turned += lax.dot_general(rest, attn[...], DOWN, preferred_element_type=jnp.float32)
        grad_down[kind][...] = turned.T
        grad_up[kind][...] = lax.dot_general(
            inner[:, kind * R : (kind + 1) * R], grad, DOWN, preferred_element_type=jnp.float32
        ).T
    grad_out_b[...] = out_b_turned[...].T
    grad_out_a[...] = out_a_turned[...].T
    for copy in copies:
        copy.wait_send()


def loss_kernel(vocab, tile, values, ahead, behind, hits, acc, stats, logits, probs, tops, sums):
    at = pl.program_id(0)
    tiles = pl.num_programs(0) - 1
    rows_all = values.shape[0]

    @pl.when(at == 0)
    def _():
        acc[...] = jnp.zeros_like(acc)
        tops[...] = jnp.full_like(tops, -1e29)
        sums[...] = jnp.zeros_like(sums)
        logits[...] = jnp.full_like(logits, -1e30)

    tail = vocab % tile
    if tail:

        @pl.when(at >= tiles - 1)
        def _():
            ahead[tail:, :] = jnp.zeros((tile - tail, ahead.shape[1]), ahead.dtype)

        @pl.when(at >= tiles)
        def _():
            behind[tail:, :] = jnp.zeros((tile - tail, behind.shape[1]), behind.dtype)

    ids = (at - 1) * tile + lax.broadcasted_iota(jnp.int32, (1, tile), 1)
    scores = logits[...] + jnp.where(ids < vocab, 0.0, -1e30)
    old = tops[:, 0:1]
    new = jnp.maximum(old, jnp.max(scores, -1, keepdims=True))
    weights = jnp.exp(scores - new)
    shrink = jnp.exp(old - new)
    sums[...] = sums[...] * shrink + jnp.sum(weights, -1, keepdims=True)
    tops[...] = jnp.broadcast_to(new, tops.shape)
    acc[...] = acc[...] * shrink
    probs[...] = weights.astype(jnp.bfloat16)
    logits[...] = lax.dot_general(
        values[...], ahead[...], (((1,), (1,)), ((), ())), preferred_element_type=jnp.float32
    )
    acc[...] += jnp.dot(probs[...], behind[...], preferred_element_type=jnp.float32)

    @pl.when(at == tiles)
    def _():
        found = jnp.sum(
            values[...].astype(jnp.float32) * hits[...].astype(jnp.float32), -1, keepdims=True
        )
        column = lax.broadcasted_iota(jnp.int32, (rows_all, 128), 1)
        stats[...] = jnp.where(
            column == 0, tops[...], jnp.where(column == 1, sums[...], found)
        )


LOSS_TILE = 512


def loss_call(values, head_rows, hits):
    rows, width = values.shape
    vocab = head_rows.shape[0]
    tile = LOSS_TILE
    tiles = pl.cdiv(vocab, tile)
    whole = pl.BlockSpec((rows, width), lambda j: (0, 0))
    return pl.pallas_call(
        functools.partial(loss_kernel, vocab, tile),
        name="loss",
        grid=(tiles + 1,),
        in_specs=[
            whole,
            pl.BlockSpec((tile, width), lambda j: (jnp.minimum(j, tiles - 1), 0)),
            pl.BlockSpec((tile, width), lambda j: (jnp.maximum(j - 1, 0), 0)),
            whole,
        ],
        out_specs=[whole, pl.BlockSpec((rows, 128), lambda j: (0, 0))],
        out_shape=[
            jax.ShapeDtypeStruct((rows, width), jnp.float32),
            jax.ShapeDtypeStruct((rows, 128), jnp.float32),
        ],
        scratch_shapes=[
            pltpu.VMEM((rows, tile), jnp.float32),
            pltpu.VMEM((rows, tile), jnp.bfloat16),
            pltpu.VMEM((rows, 128), jnp.float32),
            pltpu.VMEM((rows, 128), jnp.float32),
        ],
        compiler_params=pltpu.CompilerParams(vmem_limit_bytes=VMEM_LIMIT),
        cost_estimate=pl.CostEstimate(
            flops=4 * rows * width * vocab,
            bytes_accessed=4 * width * vocab,
            transcendentals=rows * vocab,
        ),
    )(values, head_rows, head_rows, hits)


def fold_kernel(splits, count, *refs):
    fulls = refs[0:4]
    groups = refs[4:8]
    losses, master, first, second, bases = refs[8:13]
    loss_out, norm_out, first_out, second_out, master_out = refs[13:18]
    scratch = refs[18:]
    sends = scratch[0:splits]
    recvs = scratch[splits : 2 * splits]
    keeps = scratch[2 * splits : 3 * splits]
    (line_send, line_recv, turn_send, turn_recv, note_send, note_recv, tell_send, tell_recv) = scratch[
        3 * splits : 3 * splits + 8
    ]
    (half_out, half_in, line_out, line_in, turn_out, turn_in, note_out, note_in, tell_out, tell_in) = (
        scratch[3 * splits + 8 :]
    )
    shards = 2**splits
    me = lax.axis_index("dp")
    lane = lax.axis_index("mp")
    full_rows = fulls[0].shape[0] // shards
    group_rows = groups[0].shape[0] // shards
    own_rows = full_rows // count
    bits = [(me // 2**k) % 2 for k in range(splits)]
    mates = [me + 2**k * (1 - 2 * bits[k]) for k in range(splits)]
    peers = [lax.rem(lane + offset, count) for offset in range(count)]
    spot = lane * shards + me
    goal = (spot // count, lax.rem(spot, count))
    place = me * count + lane
    origin = (lax.rem(place, shards), place // shards)
    moved = spot != place

    barrier = pltpu.get_barrier_semaphore()
    for mate in mates:
        pl.semaphore_signal(barrier, inc=1, device_id={"dp": mate, "mp": lane}, device_id_type=MESH)
    for peer in peers[1:]:
        pl.semaphore_signal(barrier, inc=1, device_id={"dp": me, "mp": peer}, device_id_type=MESH)

    @pl.when(moved)
    def _():
        for device in (goal, origin):
            pl.semaphore_signal(
                barrier, inc=1, device_id={"dp": device[0], "mp": device[1]}, device_id_type=MESH
            )

    pl.semaphore_wait(barrier, splits + count - 1 + jnp.where(moved, 2, 0))

    def remote(src, dst, out_sem, in_sem, device):
        return pltpu.make_async_remote_copy(
            src_ref=src,
            dst_ref=dst,
            send_sem=out_sem,
            recv_sem=in_sem,
            device_id={"dp": device[0], "mp": device[1]},
            device_id_type=MESH,
        )

    def piece(index):
        whole = pl.ds(pl.multiple_of(index * full_rows, full_rows), full_rows)
        part = pl.ds(pl.multiple_of(index * group_rows, group_rows), group_rows)
        return jnp.concatenate(
            [ref[whole, :] for ref in fulls] + [ref[part, :] for ref in groups], 0
        )

    started = []
    current = piece
    for k in range(splits):
        half = shards >> (k + 1)
        for i in range(half):
            sends[k][i] = current(2 * i + 1 - bits[k]).astype(jnp.bfloat16)
        copy = remote(sends[k], recvs[k], half_out.at[k], half_in.at[k], (mates[k], lane))
        copy.start()
        started.append(copy)
        for i in range(half):
            keeps[k][i] = current(2 * i + bits[k])
        copy.wait_recv()
        current = functools.partial(
            lambda kept, came, i: kept[i] + came[i].astype(jnp.float32), keeps[k], recvs[k]
        )
    final = keeps[splits - 1]
    final[0] = current(0)

    def chosen(peer):
        return jnp.concatenate(
            [
                final[
                    0,
                    pl.ds(pl.multiple_of(a * full_rows + peer * own_rows, own_rows), own_rows),
                    :,
                ]
                for a in range(4)
            ],
            0,
        )

    turn_send[...] = final[0, 4 * full_rows :, :].astype(jnp.bfloat16)
    turn = remote(turn_send, turn_recv, turn_out, turn_in, goal)

    @pl.when(moved)
    def _():
        turn.start()

    for offset in range(1, count):
        line_send[offset] = chosen(peers[offset]).astype(jnp.bfloat16)
        copy = remote(
            line_send.at[offset],
            line_recv.at[offset],
            line_out.at[offset],
            line_in.at[offset],
            (me, peers[offset]),
        )
        copy.start()
        started.append(copy)
    total = chosen(lane)

    @pl.when(moved)
    def _():
        turn.wait()

    @pl.when(jnp.logical_not(moved))
    def _():
        turn_recv[...] = turn_send[...]

    for copy in started[splits:]:
        copy.wait_recv()
    for offset in range(1, count):
        total = total + line_recv[offset].astype(jnp.float32)
    part = turn_recv[...].astype(jnp.float32)

    column = lax.broadcasted_iota(jnp.int32, (8, 128), 1)
    row = lax.broadcasted_iota(jnp.int32, (8, 128), 0)
    squares = jnp.sum(total * total) + jnp.sum(part * part)
    spot_norm = (row == 0) & (column == 0)
    spot_loss = (row == 0) & (column == 1)
    note = jnp.where(spot_norm, squares, 0.0) + jnp.where(spot_loss, jnp.sum(losses[...]), 0.0)

    def rows_of(index):
        source, slot = (total, (0, 1, 2, 7).index(index)) if index in (0, 1, 2, 7) else (
            part,
            index - 3,
        )
        return source[slot * own_rows : (slot + 1) * own_rows, :]

    turned = [
        jnp.dot(
            rows_of(m), bases[m], precision=HIGH_PRECISION, preferred_element_type=jnp.float32
        )
        for m in range(8)
    ]
    for k in range(splits):
        note_send[k] = note
        copy = remote(
            note_send.at[k], note_recv.at[k], note_out.at[k], note_in.at[k], (mates[k], lane)
        )
        copy.start()
        started.append(copy)
        copy.wait_recv()
        note = note + note_recv[k]
    tell_send[...] = note
    tells = []
    for offset in range(1, count):
        copy = remote(
            tell_send,
            tell_recv.at[offset],
            tell_out.at[offset],
            tell_in.at[offset],
            (me, peers[offset]),
        )
        copy.start()
        tells.append(copy)
    for copy in tells:
        copy.wait_recv()
    everything = note
    for offset in range(1, count):
        everything = everything + tell_recv[offset]
    norm = jnp.sqrt(jnp.sum(jnp.where(spot_norm, everything, 0.0), keepdims=True))
    loss_out[...] = jnp.sum(jnp.where(spot_loss, note, 0.0), keepdims=True)
    norm_out[...] = norm
    factor = jnp.minimum(1.0, CLIP_LIMIT / norm)
    for m in range(8):
        rotated = turned[m] * factor
        new_first = BETA_FIRST * first[m] + (1.0 - BETA_FIRST) * rotated
        new_second = BETA_SECOND * second[m] + (1.0 - BETA_SECOND) * rotated * rotated
        first_out[m] = new_first
        second_out[m] = new_second
        normed = (
            new_first
            / (1.0 - BETA_FIRST**ADAM_STEP)
            / (jnp.sqrt(new_second / (1.0 - BETA_SECOND**ADAM_STEP)) + ADAM_EPS)
        )
        back = lax.dot_general(
            normed,
            bases[m],
            (((1,), (1,)), ((), ())),
            precision=HIGH_PRECISION,
            preferred_element_type=jnp.float32,
        )
        master_out[m] = master[m] - LEARN_RATE * (back + DECAY_RATE * master[m])
    for copy in started + tells:
        copy.wait_send()


def fold_call(fulls, groups, losses, master, first_moment, second_moment, bases):
    shards = lax.axis_size("dp")
    count = lax.axis_size("mp")
    splits = shards.bit_length() - 1
    width = fulls[0].shape[1]
    pile = 4 * (fulls[0].shape[0] + groups[0].shape[0]) // shards
    own = 4 * fulls[0].shape[0] // (shards * count)
    low = jnp.bfloat16
    halves = [shards >> (k + 1) for k in range(splits)]
    dma = pltpu.SemaphoreType.DMA
    scratch = (
        [pltpu.VMEM((half, pile, width), low) for half in halves] * 2
        + [pltpu.VMEM((half, pile, width), jnp.float32) for half in halves]
        + [pltpu.VMEM((count, own, width), low)] * 2
        + [pltpu.VMEM((4 * groups[0].shape[0] // shards, width), low)] * 2
        + [pltpu.VMEM((splits, 8, 128), jnp.float32)] * 2
        + [pltpu.VMEM((8, 128), jnp.float32), pltpu.VMEM((count, 8, 128), jnp.float32)]
        + [dma((splits,))] * 2
        + [dma((count,))] * 2
        + [dma(())] * 2
        + [dma((splits,))] * 2
        + [dma((count,))] * 2
    )
    scalar = jax.ShapeDtypeStruct((1, 1), jnp.float32)
    state = jax.ShapeDtypeStruct(master.shape, jnp.float32)
    return line_call(
        functools.partial(fold_kernel, splits, count),
        "fold",
        3,
        [scalar, scalar, state, state, state],
        scratch,
        [*fulls, *groups, losses, master, first_moment, second_moment, bases],
    )


def per_device(
    token_ids,
    prompt_len,
    example_len,
    embedding,
    w_qkv,
    w_out,
    w_in,
    b_in,
    w_down,
    unembed,
    ln_gain,
    ln_bias,
    master,
    first_moment,
    second_moment,
    eigen_bases,
):
    group_count = lax.axis_size("mp")
    group_index = lax.axis_index("mp")
    shards = lax.axis_size("dp")
    moving = shards == 8 and unembed.shape[0] % 128 == 0 and unembed.shape[1] % 32 == 0
    if not moving:
        head_rows = lax.all_gather(unembed.T, "dp", axis=1, tiled=True)
    examples, length = token_ids.shape
    width = embedding.shape[0]
    vocab_local = unembed.shape[1]
    rows = examples * length
    local_heads = HEADS // group_count
    group_width = local_heads * HD
    flat_ids = token_ids.reshape(rows)
    picked = pick_call(flat_ids - group_index * width, embedding, "pick_start")
    shape_low = jax.ShapeDtypeStruct((rows, D), jnp.bfloat16)
    shape_wide = jax.ShapeDtypeStruct((rows, D), jnp.float32)
    shards = lax.axis_size("dp")
    own_rows = master.shape[1]
    pool_shape = (shards, group_count, 8, own_rows, R)
    target = jnp.roll(token_ids, -1, axis=1).reshape(rows)
    cosine, sine = rope_tables(length)
    table = jnp.concatenate([cosine[:, 0], sine[:, 0]], 1)
    shape_group = jax.ShapeDtypeStruct((rows, group_width), jnp.bfloat16)
    low = jnp.bfloat16
    shape_up = jax.ShapeDtypeStruct((group_width, R), low)
    (
        normed_attn,
        inner,
        queries,
        key_rows,
        value_rows,
        context,
        spread_lanes,
        inner_out,
        resid,
        final_rows,
        up_q,
        up_k,
        up_v,
        down_out,
        up_out,
        wide_cosine,
        wide_sine,
        *gathered,
    ) = line_call(
        functools.partial(forward_kernel, moving, group_count),
        "forward",
        0,
        [
            shape_low,
            jax.ShapeDtypeStruct((rows, 3 * R), low),
            shape_group,
            shape_group,
            shape_group,
            shape_group,
            jax.ShapeDtypeStruct((rows, 128), jnp.float32),
            jax.ShapeDtypeStruct((rows, R), low),
            shape_wide,
            shape_low,
            shape_up,
            shape_up,
            shape_up,
            shape_up,
            jax.ShapeDtypeStruct((D, R), low),
            jax.ShapeDtypeStruct((rows, 128), jnp.float32),
            jax.ShapeDtypeStruct((rows, 128), jnp.float32),
        ]
        + ([jax.ShapeDtypeStruct((vocab_local, D), low)] if moving else []),
        line_scratch(rows, D) * 2
        + [
            pltpu.VMEM((rows, D), low),
            pltpu.VMEM((rows, D), low),
            pltpu.VMEM((rows, w_qkv.shape[1]), jnp.float32),
            pltpu.VMEM((rows, D), low),
            pltpu.VMEM((rows, D), low),
            pltpu.VMEM((D, 3 * R), low),
            pltpu.VMEM(w_qkv.shape, low),
            pltpu.VMEM(w_qkv.shape, low),
            pltpu.VMEM(w_in.shape, low),
            pltpu.VMEM(w_down.shape, low),
            pltpu.VMEM(w_out.shape, low),
            pltpu.SemaphoreType.DMA((4,)),
            pltpu.VMEM(pool_shape, low),
        ]
        + [pltpu.SemaphoreType.DMA((group_count,))] * 2
        + [pltpu.SemaphoreType.DMA((shards - 1,))] * 2
        + ([pltpu.SemaphoreType.DMA((14,))] * 2 + [pltpu.SemaphoreType.DMA] if moving else []),
        [
            picked,
            ln_gain,
            ln_bias,
            b_in.reshape(1, -1),
            master,
            table,
            w_qkv,
            w_in,
            w_down,
            w_out,
        ]
        + ([unembed.T] if moving else []),
        spaces=(pl.ANY,) * (5 if moving else 4),
        far_outs=1 if moving else 0,
    )
    if moving:
        (head_rows,) = gathered
    goal = target - group_index * vocab_local
    hits = pick_call(goal, head_rows, "pick_target")
    raw_grad, stats = loss_call(final_rows, head_rows, hits)
    late = [
        resid,
        queries,
        key_rows,
        value_rows,
        context,
        spread_lanes,
        inner,
        inner_out,
        normed_attn,
        w_out,
        up_out,
        wide_cosine,
        wide_sine,
    ]
    tall = jax.ShapeDtypeStruct((D, R), jnp.float32)
    short = jax.ShapeDtypeStruct((group_width, R), jnp.float32)
    losses, grad_q, grad_k, grad_v, grad_out_b, *local_grads = line_call(
        functools.partial(branch_kernel, group_count),
        "branch_rows",
        2,
        [jax.ShapeDtypeStruct((1, rows), jnp.float32)] + [tall] * 4 + [short] * 4,
        line_scratch(rows, D)
        + [
            pltpu.VMEM((rows, D), jnp.bfloat16),
            pltpu.VMEM((8, rows), jnp.float32),
            pltpu.VMEM((group_count, 8, rows), jnp.float32),
            pltpu.VMEM((rows, 128), jnp.float32),
            pltpu.SemaphoreType.DMA((group_count,)),
            pltpu.SemaphoreType.DMA((group_count,)),
        ]
        + [pltpu.VMEM(value.shape, value.dtype) for value in late]
        + [
            pltpu.SemaphoreType.DMA((len(late),)),
            pltpu.VMEM((rows, D), jnp.bfloat16),
            pltpu.VMEM((rows, group_width), jnp.bfloat16),
            pltpu.VMEM((group_width, rows), jnp.float32),
            pltpu.VMEM((group_width, rows), jnp.float32),
            pltpu.VMEM((R, D), jnp.float32),
            pltpu.VMEM((R, group_width), jnp.float32),
        ],
        [
            raw_grad,
            hits,
            stats,
            ln_gain,
            up_q,
            up_k,
            up_v,
            down_out,
            prompt_len,
            example_len,
            *late,
        ],
        spaces=(pltpu.SMEM,) * 2 + (pl.ANY,) * len(late),
    )
    mean_loss, grad_norm, new_first, new_second, new_master = fold_call(
        [grad_q, grad_k, grad_v, grad_out_b],
        local_grads,
        losses,
        master,
        first_moment,
        second_moment,
        eigen_bases,
    )
    return (mean_loss.reshape(()), grad_norm.reshape(()), new_first, new_second, new_master)


def solution(mesh):
    placed = (
        P("dp", None),
        P(),
        P(),
        P("mp", None),
        P(None, "mp"),
        P("mp", None),
        P(None, "mp"),
        P("mp"),
        P("mp", None),
        P("dp", "mp"),
        P(),
        P(),
        P(None, ("dp", "mp"), None),
        P(None, ("dp", "mp"), None),
        P(None, ("dp", "mp"), None),
        P(),
    )
    return jax.shard_map(
        per_device,
        mesh=mesh,
        in_specs=placed,
        out_specs=(
            P(),
            P(),
            P(None, ("dp", "mp"), None),
            P(None, ("dp", "mp"), None),
            P(None, ("dp", "mp"), None),
        ),
        check_vma=False,
    )
```
